32 devices in a mesh: dp: 8 (over y, x, core), tensor: 4 (over z).
Axes of the slice: x: 2, y: 2, z: 4, core: 2. Of those that a mesh axis runs over, the one named last changes fastest.
Arguments:
- tokens: bfloat16 [8192, 1024], P(('dp', 'tensor')), may hold values from -6 to 6
- gain_attn: bfloat16 [1024], replicated, may hold values from 0.5 to 1.5
- w_query: bfloat16 [1024, 1024], P(None, 'tensor'), may hold values from -0.1875 to 0.1875
- w_key: bfloat16 [1024, 1024], P(None, 'tensor'), may hold values from -0.1875 to 0.1875
- w_value: bfloat16 [1024, 1024], P(None, 'tensor'), may hold values from -0.1875 to 0.1875
- w_out: bfloat16 [1024, 1024], P('tensor'), may hold values from -1 to 1
- gain_mlp: bfloat16 [1024], replicated, may hold values from 0.5 to 1.5
- w_gate: bfloat16 [1024, 2752], P(None, 'tensor'), may hold values from -0.1875 to 0.1875
- w_up: bfloat16 [1024, 2752], P(None, 'tensor'), may hold values from -0.1875 to 0.1875
- w_down: bfloat16 [2752, 1024], P('tensor'), may hold values from -0.21875 to 0.21875
- out_grad: bfloat16 [8192, 1024], P(('dp', 'tensor')), may hold values from -6 to 6
Outputs:
- output: bfloat16 [8192, 1024], P(('dp', 'tensor'))
- input_grad: float32 [8192, 1024], P(('dp', 'tensor'))
- grad_gain_attn: float32 [1024], replicated
- grad_query: float32 [1024, 1024], P(None, 'tensor')
- grad_key: float32 [1024, 1024], P(None, 'tensor')
- grad_value: float32 [1024, 1024], P(None, 'tensor')
- grad_out: float32 [1024, 1024], P('tensor')
- grad_gain_mlp: float32 [1024], replicated
- grad_gate: float32 [1024, 2752], P(None, 'tensor')
- grad_up: float32 [1024, 2752], P(None, 'tensor')
- grad_down: float32 [2752, 1024], P('tensor')
The draws below stay inside these ranges and needn't reach their ends.
All inputs are finite; a program needn't handle non-finite values.
Results may differ from the reference program's by a relative error of at most 0.017.
Values may be sent and summed in bfloat16 or wider, within the bound.
No kernel may reach another device: no remote copies, remote signals or barrier semaphores. Data moves between devices by JAX's collectives and lax.ppermute only.
A program may use at most 128 MiB of HBM per device.

```python
import jax
import jax.numpy as jnp
from jax import lax

D = 1024
HEADS = 16
HEAD_DIM = 64
FF = 2752
WINDOW = 64
SEQ_LEN = 1024
SEQS = 8
TOKENS = 8192


def block_scale(stream_key, dims, cuts, smallest, largest):
    level, own = 1.0, jax.random.fold_in(stream_key, 6)
    for dim, parts in cuts:
        draws = jnp.exp(jax.random.uniform(jax.random.fold_in(own, dim), (parts,), jnp.float32, smallest / len(cuts), largest / len(cuts)))
        level = level * jnp.repeat(draws, dims[dim] // parts).reshape([-1 if axis == dim else 1 for axis in range(len(dims))])
    return level


def noise(rng, extent, spread, bound, split=(), held_as=jnp.bfloat16):
    level = block_scale(rng, extent, split, -0.22, 0.18) if split else 1.0
    values = jax.random.normal(rng, extent, jnp.float32) * spread * level
    return jnp.minimum(jnp.maximum(values, -bound), bound).astype(held_as)


def setup_inputs(seed: int = 0) -> dict:
    keys = jax.random.split(jax.random.key(seed), 12)
    return {
        "tokens": noise(keys[0], (TOKENS, D), 1.0, 6.0, ((0, 32),)),
        "gain_attn": jnp.clip(1.0 + 0.1 * jax.random.normal(keys[1], (D,), jnp.float32), 0.5, 1.5).astype(jnp.bfloat16),
        "w_query": noise(keys[2], (D, D), D ** -0.5, 0.1875, ((1, 4),)),
        "w_key": noise(keys[3], (D, D), D ** -0.5, 0.1875, ((1, 4),)),
        "w_value": noise(keys[4], (D, D), D ** -0.5, 0.1875, ((1, 4),)),
        "w_out": noise(keys[5], (D, D), (D // 32) ** -0.5, 1.0, ((0, 4),)),
        "gain_mlp": jnp.clip(1.0 + 0.1 * jax.random.normal(keys[6], (D,), jnp.float32), 0.5, 1.5).astype(jnp.bfloat16),
        "w_gate": noise(keys[7], (D, FF), D ** -0.5, 0.1875, ((1, 4),)),
        "w_up": noise(keys[8], (D, FF), D ** -0.5, 0.1875, ((1, 4),)),
        "w_down": noise(keys[9], (FF, D), (FF // 4) ** -0.5, 0.21875, ((0, 4),)),
        "out_grad": noise(keys[10], (TOKENS, D), 1.0, 6.0, ((0, 32),)),
    }


norm_eps = 1e-05
very_low = -1e+30
highest = lax.Precision.HIGHEST

@jax.custom_vjp
def low(v):
    return lax.optimization_barrier(v.astype(jnp.bfloat16)).astype(jnp.float32)

@jax.custom_vjp
def low_back(v):
    return v

def low_keep(v):
    return (low(v), None)

def low_pass(kept, grad):
    return (grad,)

def back_keep(v):
    return (v, None)

def back_low(kept, grad):
    return (low(grad),)
low.defvjp(low_keep, low_pass)
low_back.defvjp(back_keep, back_low)

def rms_norm(values, gain):
    return values * lax.rsqrt(lax.optimization_barrier(jnp.mean(values * values, axis=-1, keepdims=True)) + norm_eps) * gain

def band_mask(blocks, width):
    query_pos = jnp.arange(width)[:, None]
    key_pos = jnp.arange(2 * width)[None, :]
    banded = (key_pos >= query_pos + 1) & (key_pos <= query_pos + width)
    first_ok = jnp.arange(blocks)[:, None, None] > 0
    return banded[None] & ((key_pos >= width)[None] | first_ok)

def with_previous(blocked):
    earlier = jnp.concatenate([jnp.zeros_like(blocked[:1]), blocked[:-1]], axis=0)
    return jnp.concatenate([earlier, blocked], axis=1)

def seq_attend(triple):
    queries, keys_in, values_in = triple
    blocks = SEQ_LEN // WINDOW
    q_blocks = queries.reshape(blocks, WINDOW, HEADS, HEAD_DIM)
    k_wide = with_previous(keys_in.reshape(blocks, WINDOW, HEADS, HEAD_DIM))
    v_wide = with_previous(values_in.reshape(blocks, WINDOW, HEADS, HEAD_DIM))
    scores = jnp.einsum('nqhd,nkhd->nhqk', q_blocks, k_wide, precision=highest) * HEAD_DIM ** (-0.5)
    scores = low_back(scores)
    scores = jnp.where(band_mask(blocks, WINDOW)[:, None], scores, very_low)
    top_score = lax.optimization_barrier(jnp.max(scores, axis=-1, keepdims=True))
    expo = jnp.exp(scores - top_score)
    probs = expo / lax.optimization_barrier(jnp.sum(expo, axis=-1, keepdims=True))
    mixed = jnp.einsum('nhqk,nkhd->nqhd', low(probs), v_wide, precision=highest)
    return mixed.reshape(SEQ_LEN, HEADS * HEAD_DIM)

def per_sequence(flat):
    return flat.reshape(SEQS, SEQ_LEN, HEADS, HEAD_DIM)

def forward(tokens, gain_attn, w_query, w_key, w_value, w_out, gain_mlp, w_gate, w_up, w_down):
    normed = low(rms_norm(tokens, gain_attn))
    queries = low(low_back(jnp.dot(normed, w_query, precision=highest)))
    keys_all = low(low_back(jnp.dot(normed, w_key, precision=highest)))
    values_all = low(low_back(jnp.dot(normed, w_value, precision=highest)))
    attended = lax.map(jax.checkpoint(seq_attend), (per_sequence(queries), per_sequence(keys_all), per_sequence(values_all)))
    attended = low(low_back(attended.reshape(SEQS * SEQ_LEN, D)))
    branch = low_back(jnp.dot(attended, w_out, precision=highest))
    middle = tokens + branch
    normed_mid = low(rms_norm(middle, gain_mlp))
    gate_pre = low_back(jnp.dot(normed_mid, w_gate, precision=highest))
    up_pre = low_back(jnp.dot(normed_mid, w_up, precision=highest))
    hidden = low(gate_pre / (1.0 + jnp.exp(-gate_pre)) * up_pre)
    return middle + low_back(jnp.dot(hidden, w_down, precision=highest))

def reference(tokens, gain_attn, w_query, w_key, w_value, w_out, gain_mlp, w_gate, w_up, w_down, out_grad):
    inputs = (tokens, gain_attn, w_query, w_key, w_value, w_out, gain_mlp, w_gate, w_up, w_down)
    inputs = tuple((member.astype(jnp.float32) for member in inputs))
    result, pullback = jax.vjp(forward, *inputs)
    grads = pullback(out_grad.astype(jnp.float32))
    return (result.astype(jnp.bfloat16), grads[0], grads[1], grads[2], grads[3], grads[4], grads[5], grads[6], grads[7], grads[8], grads[9])
```

```python
import functools

import jax
import jax.numpy as jnp
from jax import lax
from jax.experimental import pallas as pl
from jax.experimental.pallas import tpu as pltpu
from jax.sharding import PartitionSpec as P

HEAD_DIM = 64
WINDOW = 64
SEQ_LEN = 1024

norm_eps = 1e-05
very_low = -1e30
AXES = ("dp", "tensor")
low = jnp.bfloat16
full = jnp.float32


def mat(left, right):
    return jnp.dot(left, right, preferred_element_type=full)


def mat_left(left, right):
    return lax.dot_general(left, right, (((0,), (0,)), ((), ())), preferred_element_type=full)


def mat_right(left, right):
    return lax.dot_general(left, right, (((1,), (1,)), ((), ())), preferred_element_type=full)


def head_pair(rows):
    lane = lax.broadcasted_iota(jnp.int32, rows.shape, 1)
    zero = jnp.zeros_like(rows)
    return jnp.concatenate(
        [jnp.where(lane < HEAD_DIM, rows, zero), jnp.where(lane < HEAD_DIM, zero, rows)], axis=0
    )


def unstack(stacked):
    half = stacked.shape[0] // 2
    lane = lax.broadcasted_iota(jnp.int32, (half, stacked.shape[1]), 1)
    return jnp.where(lane < HEAD_DIM, stacked[:half], stacked[half:])


def unit_probs(q_stack, keys, first, has_halo):
    scores = mat_right(q_stack, keys) * HEAD_DIM ** (-0.5)
    row = lax.broadcasted_iota(jnp.int32, scores.shape, 0) % WINDOW
    col = lax.broadcasted_iota(jnp.int32, scores.shape, 1)
    mask = (col > row) & (col <= row + WINDOW)
    if first:
        mask = mask & ((col >= WINDOW) | (has_halo > 0))
    scores = jnp.where(mask, scores, very_low)
    expo = jnp.exp(scores - jnp.max(scores, axis=-1, keepdims=True))
    return expo / jnp.sum(expo, axis=-1, keepdims=True)


def attend_kernel(halo_ref, qkv_ref, out_ref):
    seqs, rows, width3 = qkv_ref.shape
    width = width3 // 3
    has_halo = halo_ref[0]
    for seq in range(seqs):
        for lane in range(0, width, 128):
            for top in range(0, rows - WINDOW, WINDOW):
                q = qkv_ref[seq, top + WINDOW : top + 2 * WINDOW, lane : lane + 128]
                k = qkv_ref[seq, top : top + 2 * WINDOW, width + lane : width + lane + 128]
                v = qkv_ref[seq, top : top + 2 * WINDOW, 2 * width + lane : 2 * width + lane + 128]
                probs = unit_probs(head_pair(q), k, top == 0, has_halo).astype(low)
                out_ref[seq, top : top + WINDOW, lane : lane + 128] = unstack(mat(probs, v)).astype(low)


def attend_back_kernel(halo_ref, qkv_ref, grad_ref, out_ref):
    seqs, rows, width3 = qkv_ref.shape
    width = width3 // 3
    has_halo = halo_ref[0]
    factor = HEAD_DIM ** (-0.5)
    for seq in range(seqs):
        for lane in range(0, width, 128):
            out_ref[seq, 0:WINDOW, lane : lane + 128] = jnp.zeros((WINDOW, 128), low)
            k_tail = v_tail = jnp.zeros((WINDOW, 128), full)
            for top in range(0, rows - WINDOW, WINDOW):
                q = head_pair(qkv_ref[seq, top + WINDOW : top + 2 * WINDOW, lane : lane + 128])
                k = qkv_ref[seq, top : top + 2 * WINDOW, width + lane : width + lane + 128]
                v = qkv_ref[seq, top : top + 2 * WINDOW, 2 * width + lane : 2 * width + lane + 128]
                g = head_pair(grad_ref[seq, top : top + WINDOW, lane : lane + 128])
                probs = unit_probs(q, k, top == 0, has_halo)
                prob_grad = mat_right(g, v)
                inner = jnp.sum(probs * prob_grad, axis=-1, keepdims=True)
                score_grad = (probs * (prob_grad - inner)).astype(low)
                q_grad = unstack(mat(score_grad, k)) * factor
                k_grad = mat_left(score_grad, q) * factor
                v_grad = mat_left(probs.astype(low), g)
                out_ref[seq, top + WINDOW : top + 2 * WINDOW, lane : lane + 128] = q_grad.astype(low)
                at = width + lane
                out_ref[seq, top : top + WINDOW, at : at + 128] = (k_tail + k_grad[:WINDOW]).astype(low)
                at = 2 * width + lane
                out_ref[seq, top : top + WINDOW, at : at + 128] = (v_tail + v_grad[:WINDOW]).astype(low)
                k_tail, v_tail = k_grad[WINDOW:], v_grad[WINDOW:]
            at = width + lane
            out_ref[seq, rows - WINDOW : rows, at : at + 128] = k_tail.astype(low)
            at = 2 * width + lane
            out_ref[seq, rows - WINDOW : rows, at : at + 128] = v_tail.astype(low)


def attend(has_halo, qkv):
    seqs, rows, width3 = qkv.shape
    work = seqs * rows * width3
    return pl.pallas_call(
        attend_kernel,
        out_shape=jax.ShapeDtypeStruct((seqs, rows - WINDOW, width3 // 3), low),
        in_specs=[pl.BlockSpec(memory_space=pltpu.SMEM), pl.BlockSpec(memory_space=pltpu.VMEM)],
        out_specs=pl.BlockSpec(memory_space=pltpu.VMEM),
        compiler_params=pltpu.CompilerParams(vmem_limit_bytes=16 << 20),
        cost_estimate=pl.CostEstimate(flops=work * 512, bytes_accessed=work * 3, transcendentals=work),
    )(has_halo, qkv)


def attend_back(has_halo, qkv, grad):
    work = qkv.size
    return pl.pallas_call(
        attend_back_kernel,
        out_shape=jax.ShapeDtypeStruct(qkv.shape, low),
        in_specs=[pl.BlockSpec(memory_space=pltpu.SMEM)] + [pl.BlockSpec(memory_space=pltpu.VMEM)] * 2,
        out_specs=pl.BlockSpec(memory_space=pltpu.VMEM),
        compiler_params=pltpu.CompilerParams(vmem_limit_bytes=16 << 20),
        cost_estimate=pl.CostEstimate(flops=work * 1024, bytes_accessed=work * 5, transcendentals=work),
    )(has_halo, qkv, grad)


def rms_scale(values):
    return lax.rsqrt(jnp.mean(values * values, axis=-1, keepdims=True) + norm_eps)


def rms_norm(values, gain):
    return values * rms_scale(values) * gain


def rms_pull(values, gain, grad):
    scale = rms_scale(values)
    unit = values * scale
    scaled = grad * gain
    inner = jnp.mean(scaled * unit, axis=-1, keepdims=True)
    return scale * (scaled - unit * inner), jnp.sum(grad * unit, axis=0)


def build(n_dp, n_t):
    bits = [1 << k for k in range(1, n_dp.bit_length() - 1)]
    rounds = len(bits)
    quarters = 1 << rounds

    def perm(target):
        pairs = []
        for d in range(n_dp):
            for t in range(n_t):
                to = target(d, t)
                if to is not None:
                    pairs.append((d * n_t + t, to[0] * n_t + to[1]))
        return pairs

    def order(which):
        return bits if which == 0 else bits[::-1]

    send_core = functools.partial(lax.ppermute, axis_name=AXES, perm=perm(lambda d, t: (d ^ 1, t)))
    send_pair = functools.partial(lax.ppermute, axis_name=AXES, perm=perm(lambda d, t: (d, t ^ 1)))
    send_far = functools.partial(lax.ppermute, axis_name=AXES, perm=perm(lambda d, t: (d, t ^ 2)))

    def local(
        tokens, gain_attn, w_query, w_key, w_value, w_out, gain_mlp, w_gate, w_up, w_down, out_grad
    ):
        own_rows, depth = tokens.shape
        hidden_cols = w_gate.shape[1]
        head_cols = w_query.shape[1]
        d, t = lax.axis_index("dp"), lax.axis_index("tensor")
        core, part, side = d & 1, t & 1, t >> 1
        resident = core == side

        def bit_of(bit):
            return (d // bit) & 1

        def ordered(index, mine, other, axis=0):
            first = jnp.where(index == 0, mine, other)
            second = jnp.where(index == 0, other, mine)
            return jnp.concatenate([first, second], axis=axis)

        def pick(array, index):
            return lax.dynamic_index_in_dim(array, index, 0, keepdims=False)

        def double(piece, sequence_of, index_of):
            for i in range(rounds):
                way = perm(lambda d_, t_: (d_ ^ sequence_of(d_ & 1, t_ >> 1)[i], t_))
                piece = ordered(index_of(i), piece[None], lax.ppermute(piece, AXES, way)[None])
                piece = piece.reshape((-1,) + piece.shape[2:]) if i else piece
            return piece

        def select_bit(i, lists):
            return jnp.where(core == 0, bit_of(lists[0][i]), bit_of(lists[1][i]))

        def untranspose(stack):
            rest = stack.shape[1:]
            dims = tuple(range(rounds - 1, -1, -1)) + tuple(range(rounds, rounds + len(rest)))
            return stack.reshape((2,) * rounds + rest).transpose(dims).reshape(stack.shape)

        def fetch(pieces):
            index = 0
            for bit in bits[::-1]:
                index = index * 2 + bit_of(bit)
            piece = pick(pieces, index * 2 + core)
            piece = lax.ppermute(piece, AXES, perm(lambda d_, t_: (d_, t_ ^ 2)))
            lists = (bits, bits[::-1])
            stack = double(
                piece, lambda c_, h_: lists[c_], lambda i: select_bit(i, lists)
            )
            other = lax.ppermute(
                stack, AXES, perm(lambda d_, t_: (d_ ^ 1, t_) if (d_ & 1) == (t_ >> 1) else None)
            )
            zero = jnp.where(core == 0, stack, other)
            one = untranspose(jnp.where(core == 0, other, stack))
            both = jnp.stack([zero, one], axis=1)
            return both.reshape(pieces.shape)

        def rows_in(array):
            return array.reshape((2 * quarters, array.shape[0] // (2 * quarters)) + array.shape[1:])

        def columns_in(array):
            return array.reshape(array.shape[0], 2 * quarters, -1).transpose(1, 0, 2)

        def columns_out(pieces):
            return pieces.transpose(1, 0, 2).reshape(pieces.shape[1], -1)

        def gather_group(rows):
            pair = ordered(part, rows, send_pair(rows))
            return ordered(core, pair, send_core(pair))

        def scatter_group(make):
            theirs = make(1 - core).astype(low)
            arrived = send_core(theirs)
            mine = make(core) + arrived.astype(full)
            halves = mine.reshape(2, -1, mine.shape[-1])
            arrived = send_pair(pick(halves, 1 - part).astype(low))
            return pick(halves, part) + arrived.astype(full)

        def reduce_slice(pieces):
            lists = (bits, bits[::-1])
            stack = pieces
            for i in range(rounds):
                bit = select_bit(i, lists)
                halves = stack.reshape((2, stack.shape[0] // 2) + stack.shape[1:])
                way = perm(lambda d_, t_: (d_ ^ lists[d_ & 1][i], t_))
                arrived = lax.ppermute(pick(halves, 1 - bit).astype(low), AXES, way)
                stack = pick(halves, bit).astype(full) + arrived.astype(full)
            piece = stack[0]
            arrived = lax.ppermute(
                piece.astype(low),
                AXES,
                perm(lambda d_, t_: (d_, t_ ^ 2) if (d_ & 1) != (t_ >> 1) else None),
            )
            total = (piece + arrived.astype(full)).astype(low)
            halves = total.reshape((2, total.shape[0] // 2) + total.shape[1:])
            arrived = lax.ppermute(
                pick(halves, 1 - core),
                AXES,
                perm(lambda d_, t_: (d_ ^ 1, t_) if (d_ & 1) == (t_ >> 1) else None),
            )
            half = jnp.where(resident, pick(halves, core), arrived)
            def back(c_, h_):
                return lists[h_][::-1] if c_ == 0 else lists[h_]

            def back_bit(i):
                up = jnp.where(side == 0, bit_of(lists[0][i]), bit_of(lists[1][i]))
                down = jnp.where(
                    side == 0, bit_of(lists[0][rounds - 1 - i]), bit_of(lists[1][rounds - 1 - i])
                )
                return jnp.where(core == 0, down, up)

            stack = double(half, back, back_bit)
            other = send_core(stack)
            zero = jnp.where(core == 0, stack, other)
            one = untranspose(jnp.where(core == 0, other, stack))
            both = jnp.stack([zero, one], axis=1)
            return both

        tail = tokens[own_rows - WINDOW :]
        halo = lax.ppermute(
            tail, AXES, perm(lambda d_, t_: (d_, 2) if t_ == 1 else None)
        ) + lax.ppermute(tail, AXES, perm(lambda d_, t_: (d_, 3) if t_ == 1 else None))
        mine = jnp.concatenate([halo, ordered(part, tokens, send_pair(tokens))], axis=0)
        seqs = ordered(core, mine[None], send_core(mine)[None])

        own_qkv = jnp.concatenate([w_query, w_key, w_value], axis=1)
        far_qkv = fetch(rows_in(own_qkv)).reshape(own_qkv.shape)
        qkv_weight = jnp.where(resident, own_qkv, far_qkv)

        own_deep = columns_in(jnp.concatenate([w_out, w_down], axis=0))
        deep = columns_out(jnp.where(resident, own_deep, fetch(own_deep)))
        out_weight, down_weight = deep[:head_cols], deep[head_cols:]

        own_wide = jnp.stack([rows_in(w_gate), rows_in(w_up)], axis=1)
        wide = jnp.where(resident, own_wide, fetch(own_wide))
        gate_weight = wide[:, 0].reshape(depth, hidden_cols)
        up_weight = wide[:, 1].reshape(depth, hidden_cols)

        attn_gain = gain_attn.astype(full)
        mlp_gain = gain_mlp.astype(full)
        has_halo = jnp.reshape(side, (1,)).astype(jnp.int32)

        normed = rms_norm(seqs.astype(full), attn_gain).astype(low)
        ext = normed.shape[1]
        normed_flat = normed.reshape(2 * ext, depth)
        qkv = mat(normed_flat, qkv_weight).astype(low).reshape(2, ext, 3 * head_cols)
        attended = attend(has_halo, qkv)
        branch = scatter_group(lambda which: mat(pick(attended, which), out_weight))
        token_float = tokens.astype(full)
        middle = token_float + branch

        normed_mid = rms_norm(middle, mlp_gain).astype(low)
        mid_all = gather_group(normed_mid)
        grad_all = gather_group(out_grad)
        gate_pre = mat(mid_all, gate_weight)
        up_pre = mat(mid_all, up_weight)
        gate_sig = jax.nn.sigmoid(gate_pre)
        silu_val = gate_pre * gate_sig
        hidden = (silu_val * up_pre).astype(low)
        hidden_grad = mat_right(grad_all, down_weight)
        up_grad = (hidden_grad * silu_val).astype(low)
        gate_grad = (hidden_grad * up_pre * gate_sig * (1.0 + gate_pre * (1.0 - gate_sig))).astype(low)

        def core_rows(array, which):
            return pick(array.reshape((2, -1) + array.shape[1:]), which)

        mid_grad = scatter_group(
            lambda which: mat_right(core_rows(gate_grad, which), gate_weight)
            + mat_right(core_rows(up_grad, which), up_weight)
        )
        mid_pull, mlp_gain_part = rms_pull(middle, mlp_gain, mid_grad)
        middle_grad = out_grad.astype(full) + mid_pull

        mlp_out = scatter_group(lambda which: mat(core_rows(hidden, which), down_weight))
        output = (middle + mlp_out).astype(low)

        down_part = mat_left(hidden, grad_all).astype(low)
        down_part = down_part.reshape(hidden_cols, quarters, 2, -1).transpose(1, 2, 0, 3)
        grad_down = reduce_slice(down_part)
        grad_down = grad_down.reshape((2 * quarters,) + grad_down.shape[3:])
        grad_down = columns_out(grad_down).astype(full)

        wide_part = jnp.stack(
            [
                mat_left(mid_all, gate_grad).astype(low).reshape(quarters, 2, -1, hidden_cols),
                mat_left(mid_all, up_grad).astype(low).reshape(quarters, 2, -1, hidden_cols),
            ],
            axis=2,
        )
        wide_sum = reduce_slice(wide_part)
        wide_sum = wide_sum.reshape((2 * quarters, 2) + wide_sum.shape[4:])
        grad_gate = wide_sum[:, 0].reshape(depth, hidden_cols).astype(full)
        grad_up = wide_sum[:, 1].reshape(depth, hidden_cols).astype(full)

        branch_all = gather_group(middle_grad.astype(low))
        attended_grad = mat_right(branch_all, out_weight).astype(low).reshape(attended.shape)
        qkv_grad = attend_back(has_halo, qkv, attended_grad)
        qkv_grad_flat = qkv_grad.reshape(2 * ext, 3 * head_cols)
        attn_part = jnp.concatenate(
            [
                mat_left(normed_flat, qkv_grad_flat),
                mat_left(branch_all, attended.reshape(-1, head_cols)),
            ],
            axis=1,
        ).astype(low)
        attn_sum = reduce_slice(attn_part.reshape(quarters, 2, -1, 4 * head_cols))
        attn_sum = attn_sum.reshape(depth, 4 * head_cols).astype(full)
        grad_query = attn_sum[:, :head_cols]
        grad_key = attn_sum[:, head_cols : 2 * head_cols]
        grad_value = attn_sum[:, 2 * head_cols : 3 * head_cols]
        grad_out = attn_sum[:, 3 * head_cols :].T

        arrived = send_core(mat_right(pick(qkv_grad, 1 - core), qkv_weight).astype(low))
        mine = mat_right(pick(qkv_grad, core), qkv_weight) + arrived.astype(full)
        halo_part = mine[:WINDOW]
        halves = mine[WINDOW:].reshape(2, own_rows, depth)
        arrived = send_pair(
            jnp.concatenate([halo_part, pick(halves, 1 - part)], axis=0).astype(low)
        ).astype(full)
        halo_grad = lax.ppermute(
            (halo_part + arrived[:WINDOW]).astype(low),
            AXES,
            perm(lambda d_, t_: (d_, 1) if t_ == 2 else None),
        ).astype(full)
        normed_grad = pick(halves, part) + arrived[WINDOW:]
        normed_grad = jnp.concatenate(
            [normed_grad[: own_rows - WINDOW], normed_grad[own_rows - WINDOW :] + halo_grad], axis=0
        )
        token_pull, attn_gain_part = rms_pull(token_float, attn_gain, normed_grad)
        input_grad = middle_grad + token_pull
        gain_totals = lax.psum(jnp.stack([attn_gain_part, mlp_gain_part]), AXES)
        return (
            output,
            input_grad,
            gain_totals[0],
            grad_query,
            grad_key,
            grad_value,
            grad_out,
            gain_totals[1],
            grad_gate,
            grad_up,
            grad_down,
        )

    return local


def solution(mesh):
    both = P(("dp", "tensor"), None)
    columns, rows = P(None, "tensor"), P("tensor", None)
    return jax.shard_map(
        build(mesh.shape["dp"], mesh.shape["tensor"]),
        mesh=mesh,
        in_specs=(both, P(), columns, columns, columns, rows, P(), columns, columns, rows, both),
        out_specs=(both, both, P(), columns, columns, columns, rows, P(), columns, columns, rows),
        check_vma=False,
    )
```

```python
import functools

import jax
import jax.numpy as jnp
from jax import lax
from jax.experimental import pallas as pl
from jax.experimental.pallas import tpu as pltpu
from jax.sharding import PartitionSpec as P

HEAD_DIM = 64
WINDOW = 64
LANES = 128

norm_eps = 1e-05
very_low = -1e30
AXES = ("dp", "tensor")
low = jnp.bfloat16
full = jnp.float32


def mat(left, right):
    return jnp.dot(left, right, preferred_element_type=full)


def mat_left(left, right):
    return lax.dot_general(left, right, (((0,), (0,)), ((), ())), preferred_element_type=full)


def mat_right(left, right):
    return lax.dot_general(left, right, (((1,), (1,)), ((), ())), preferred_element_type=full)


def rms_scale(values):
    return lax.rsqrt(jnp.mean(values * values, axis=-1, keepdims=True) + norm_eps)


def rms_norm(values, gain):
    return values * rms_scale(values) * gain


def rms_pull(values, gain, grad):
    scale = rms_scale(values)
    unit = values * scale
    scaled = grad * gain
    inner = jnp.mean(scaled * unit, axis=-1, keepdims=True)
    return scale * (scaled - unit * inner), jnp.sum(grad * unit, axis=0, keepdims=True)


def aligned(index, size):
    return pl.ds(pl.multiple_of(index * size, size), size)


def call(kernel, outs, args, scratch=(), smem=0, anywhere=0, limit=24, flops=0, size=0):
    specs = (
        [pl.BlockSpec(memory_space=pltpu.SMEM)] * smem
        + [pl.BlockSpec(memory_space=pl.ANY)] * anywhere
        + [pl.BlockSpec(memory_space=pltpu.VMEM)] * (len(args) - smem - anywhere)
    )
    shapes = [jax.ShapeDtypeStruct(o[0], o[1]) for o in outs]
    places = [
        pl.BlockSpec(memory_space=pl.ANY if len(o) > 2 else pltpu.VMEM) for o in outs
    ]
    results = pl.pallas_call(
        kernel,
        out_shape=shapes,
        in_specs=specs,
        out_specs=places,
        scratch_shapes=list(scratch),
        compiler_params=pltpu.CompilerParams(vmem_limit_bytes=limit << 20),
        cost_estimate=pl.CostEstimate(flops=flops, bytes_accessed=size, transcendentals=0),
    )(*args)
    return list(results)


def pack_attention(at_ref, q_ref, k_ref, v_ref, o_ref, out_ref, sems):
    block = aligned(at_ref[0], LANES)
    moves = []
    for i, ref in enumerate((q_ref, k_ref, v_ref)):
        for j in range(2):
            moves.append((ref.at[block, pl.ds(j * LANES, LANES)], (2 * i + j) * LANES, LANES))
    moves.append((o_ref.at[:, block], 6 * LANES, o_ref.shape[0]))
    copies = [
        pltpu.make_async_copy(src, out_ref.at[pl.ds(top, size)], sems.at[n])
        for n, (src, top, size) in enumerate(moves)
    ]
    for copy in copies:
        copy.start()
    for copy in copies:
        copy.wait()


def pack_mlp(at_ref, g_ref, u_ref, d_ref, out_ref, sems):
    block = aligned(at_ref[0], LANES)
    rows = g_ref.shape[0]
    copies = [
        pltpu.make_async_copy(ref.at[:, block], out_ref.at[pl.ds(n * rows, rows)], sems.at[n])
        for n, ref in enumerate((g_ref, u_ref, d_ref))
    ]
    for copy in copies:
        copy.start()
    for copy in copies:
        copy.wait()


def unpack_attention(at_ref, q_ref, k_ref, v_ref, o_ref, *rest):
    pieces, (qkv_ref, out_ref) = rest[:8], rest[8:]
    width = q_ref.shape[1]

    @pl.when(at_ref[8] == 1)
    def _():
        for i, ref in enumerate((q_ref, k_ref, v_ref)):
            qkv_ref[:, i * width : (i + 1) * width] = ref[...]
        out_ref[...] = o_ref[...]

    @pl.when(at_ref[8] == 0)
    def _():
        for n, piece in enumerate(pieces):
            block = aligned(at_ref[n], LANES)
            for j in range(3 * width // LANES):
                qkv_ref[block, j * LANES : (j + 1) * LANES] = piece[j * LANES : (j + 1) * LANES]
            out_ref[:, block] = piece[3 * width :]


def unpack_mlp(at_ref, g_ref, u_ref, d_ref, *rest):
    pieces, outs = rest[:8], rest[8:]
    rows = g_ref.shape[0]
    for out in outs:
        out[rows:] = jnp.zeros((out.shape[0] - rows, out.shape[1]), low)

    @pl.when(at_ref[8] == 1)
    def _():
        for ref, out in zip((g_ref, u_ref, d_ref), outs):
            out[:rows] = ref[...]

    @pl.when(at_ref[8] == 0)
    def _():
        for n, piece in enumerate(pieces):
            block = aligned(at_ref[n], LANES)
            for i, out in enumerate(outs):
                out[:rows, block] = piece[i * rows : (i + 1) * rows]


def head_pair(rows):
    lane = lax.broadcasted_iota(jnp.int32, rows.shape, 1)
    zero = jnp.zeros_like(rows)
    return jnp.concatenate(
        [jnp.where(lane < HEAD_DIM, rows, zero), jnp.where(lane < HEAD_DIM, zero, rows)], axis=0
    )


def unstack(stacked):
    half = stacked.shape[0] // 2
    lane = lax.broadcasted_iota(jnp.int32, (half, stacked.shape[1]), 1)
    return jnp.where(lane < HEAD_DIM, stacked[:half], stacked[half:])


def band(first, has_halo):
    shape = (2 * WINDOW, 2 * WINDOW)
    row = lax.broadcasted_iota(jnp.int32, shape, 0) % WINDOW
    col = lax.broadcasted_iota(jnp.int32, shape, 1)
    mask = (col > row) & (col <= row + WINDOW)
    if first:
        mask = mask & ((col >= WINDOW) | (has_halo > 0))
    return mask


def softmax(scores, mask):
    scores = jnp.where(mask, scores * HEAD_DIM ** (-0.5), very_low)
    expo = jnp.exp(scores - jnp.max(scores, axis=-1, keepdims=True))
    return expo * (1.0 / jnp.sum(expo, axis=-1, keepdims=True))


def place(ref, seq, part, halo, own, pair, change):
    rows = own.shape[0]
    ref[seq, 0:WINDOW] = change(halo[...])
    ref[seq, pl.ds(pl.multiple_of(WINDOW + rows * part, WINDOW), rows)] = change(own[...])
    ref[seq, pl.ds(pl.multiple_of(WINDOW + rows * (1 - part), WINDOW), rows)] = change(pair[...])


def forward_kernel(
    at_ref, gain_ref, qkv_w, out_w, halo0, own0, pair0, halo1, own1, pair1,
    normed_ref, qkv_ref, mixed_ref, mine_ref, theirs_ref,
):
    part, has_halo = at_ref[9], at_ref[10]
    gain = gain_ref[...].astype(full)

    def norm(rows):
        return rms_norm(rows.astype(full), gain).astype(low)

    place(normed_ref, 0, part, halo0, own0, pair0, norm)
    place(normed_ref, 1, part, halo1, own1, pair1, norm)
    seqs, rows, width3 = qkv_ref.shape
    width = width3 // 3
    for seq in (1, 0):
        qkv_ref[seq] = mat(normed_ref[seq], qkv_w[...]).astype(low)
    plain, first = band(False, 0), band(True, has_halo)
    units = [(lane, top) for top in range(0, rows - WINDOW, WINDOW) for lane in range(0, width, LANES)]
    for seq in (1, 0):
        for start in range(0, len(units), 4):
            group = units[start : start + 4]
            scores = []
            for lane, top in group:
                q = qkv_ref[seq, top + WINDOW : top + 2 * WINDOW, lane : lane + LANES]
                k = qkv_ref[seq, top : top + 2 * WINDOW, width + lane : width + lane + LANES]
                scores.append(mat_right(head_pair(q), k))
            probs = [
                softmax(s, plain if top else first).astype(low)
                for s, (lane, top) in zip(scores, group)
            ]
            for p, (lane, top) in zip(probs, group):
                at = 2 * width + lane
                v = qkv_ref[seq, top : top + 2 * WINDOW, at : at + LANES]
                mixed_ref[seq, top : top + WINDOW, lane : lane + LANES] = unstack(mat(p, v)).astype(low)
        target = theirs_ref if seq else mine_ref
        target[...] = mat(mixed_ref[seq], out_w[...]).astype(target.dtype)


def backward_kernel(
    at_ref, bg00, bg01, bg10, bg11, out_w, mixed_ref, qkv_ref, normed_ref,
    out_ref, first_ref, mixed_grad,
):
    has_halo = at_ref[10]
    seqs, rows, width3 = qkv_ref.shape
    width = width3 // 3
    factor = HEAD_DIM ** (-0.5)
    half = bg00.shape[0]
    for seq, pair in enumerate(((bg00, bg01), (bg10, bg11))):
        for i, ref in enumerate(pair):
            mixed_grad[seq, i * half : (i + 1) * half] = mat_right(ref[...], out_w[...]).astype(low)
    plain, first = band(False, 0), band(True, has_halo)
    for seq in range(seqs):
        out_ref[seq, 0:WINDOW, 0:width] = jnp.zeros((WINDOW, width), low)
        tails = {}
        for lane in range(0, width, LANES):
            tails[lane] = (jnp.zeros((WINDOW, LANES), full), jnp.zeros((WINDOW, LANES), full))
        for top0 in range(0, rows - WINDOW, 2 * WINDOW):
            group = [(lane, top0 + w) for w in (0, WINDOW) for lane in range(0, width, LANES)]
            loaded, scores, prob_grads = [], [], []
            for lane, top in group:
                q = head_pair(qkv_ref[seq, top + WINDOW : top + 2 * WINDOW, lane : lane + LANES])
                k = qkv_ref[seq, top : top + 2 * WINDOW, width + lane : width + lane + LANES]
                v = qkv_ref[seq, top : top + 2 * WINDOW, 2 * width + lane : 2 * width + lane + LANES]
                g = head_pair(mixed_grad[seq, top : top + WINDOW, lane : lane + LANES])
                loaded.append((q, k, g))
                scores.append(mat_right(q, k))
                prob_grads.append(mat_right(g, v))
            probs = [softmax(s, plain if top else first) for s, (lane, top) in zip(scores, group)]
            score_grads = [
                (p * (pg - jnp.sum(p * pg, axis=-1, keepdims=True))).astype(low)
                for p, pg in zip(probs, prob_grads)
            ]
            for p, sg, (q, k, g), (lane, top) in zip(probs, score_grads, loaded, group):
                q_grad = unstack(mat(sg, k)) * factor
                k_grad = mat_left(sg, q) * factor
                v_grad = mat_left(p.astype(low), g)
                k_tail, v_tail = tails[lane]
                out_ref[seq, top + WINDOW : top + 2 * WINDOW, lane : lane + LANES] = q_grad.astype(low)
                at = width + lane
                out_ref[seq, top : top + WINDOW, at : at + LANES] = (k_tail + k_grad[:WINDOW]).astype(low)
                at = 2 * width + lane
                out_ref[seq, top : top + WINDOW, at : at + LANES] = (v_tail + v_grad[:WINDOW]).astype(low)
                tails[lane] = (k_grad[WINDOW:], v_grad[WINDOW:])
        for lane, (k_tail, v_tail) in tails.items():
            at = width + lane
            out_ref[seq, rows - WINDOW : rows, at : at + LANES] = k_tail.astype(low)
            at = 2 * width + lane
            out_ref[seq, rows - WINDOW : rows, at : at + LANES] = v_tail.astype(low)
    attention_role(at_ref[11], first_ref, (bg00, bg01, bg10, bg11), mixed_ref, out_ref, normed_ref)


def attention_role(quarter, target, grads, mixed_ref, qkv_grad_ref, normed_ref):
    seqs, rows, width3 = qkv_grad_ref.shape
    block = aligned(quarter, target.shape[0])
    total = mat_left(normed_ref[0, :, block], qkv_grad_ref[0])
    total += mat_left(normed_ref[1, :, block], qkv_grad_ref[1])
    target[:, :width3] = total.astype(low)
    half = grads[0].shape[0]
    total = None
    for n, ref in enumerate(grads):
        seq, i = divmod(n, 2)
        term = mat_left(ref[:, block], mixed_ref[seq, i * half : (i + 1) * half])
        total = term if total is None else total + term
    target[:, width3:] = total.astype(low)


def attention_grads_kernel(
    at_ref, bg00, bg01, bg10, bg11, mixed_ref, qkv_grad_ref, normed_ref, one_ref, two_ref, own_ref
):
    for n, ref in enumerate((one_ref, two_ref, own_ref)):
        attention_role(
            at_ref[12 + n], ref, (bg00, bg01, bg10, bg11), mixed_ref, qkv_grad_ref, normed_ref
        )


def mlp_kernel(
    mid0, mid1, dy0, dy1, gate_w, up_w, down_w, mine_ref, theirs_ref, hidden_ref, gg_ref, ug_ref
):
    rows = mid0.shape[0]
    for n, (mid, dy, target) in enumerate(((mid1, dy1, theirs_ref), (mid0, dy0, mine_ref))):
        at = pl.ds((1 - n) * rows, rows)
        gate = mat_right(mid[...], gate_w[...])
        up = mat_right(mid[...], up_w[...])
        back = mat_right(dy[...], down_w[...])
        sig = 1.0 / (1.0 + jnp.exp(-gate))
        silu = gate * sig
        hidden_ref[at] = (silu * up).astype(low)
        ug = (back * silu).astype(low)
        gg = (back * up * sig * (1.0 + gate * (1.0 - sig))).astype(low)
        ug_ref[at] = ug
        gg_ref[at] = gg
        target[...] = (mat(gg, gate_w[...]) + mat(ug, up_w[...])).astype(target.dtype)


def mlp_role(quarter, target, rows, tables, mids, dys):
    block = aligned(quarter, target.shape[1])
    (h0, g0, u0), (h1, g1, u1) = tables

    def total(left0, left1, right):
        return (
            mat_left(left0[...], jnp.concatenate([r[:, block] for r in right[:2]], axis=0))
            + mat_left(left1[...], jnp.concatenate([r[:, block] for r in right[2:]], axis=0))
        )[:rows].astype(low)

    target[0:rows] = total(g0, g1, mids)
    target[rows : 2 * rows] = total(u0, u1, mids)
    target[2 * rows : 3 * rows] = total(h0, h1, dys)


def mlp_grads_kernel(roles, at_ref, h0, g0, u0, h1, g1, u1, *rest):
    mids, dys, targets = rest[:4], rest[4:8], rest[8:]
    rows = targets[0].shape[0] // 3
    for role, target in zip(roles, targets):
        mlp_role(at_ref[11 + role], target, rows, ((h0, g0, u0), (h1, g1, u1)), mids, dys)


def finish_attention(at_ref, *rest):
    pieces, (gq, gk, gv, go, gq_s, gk_s, gv_s, go_s, sems) = rest[:8], rest[8:]
    width = gq.shape[1]
    for n, piece in enumerate(pieces):
        block = aligned(at_ref[n], LANES)
        for i, ref in enumerate((gq_s, gk_s, gv_s)):
            ref[block] = piece[:, i * width : (i + 1) * width].astype(full)
        go_s[:, block] = piece[:, 3 * width :].astype(full).T
    copies = [
        pltpu.make_async_copy(src, dst, sems.at[n])
        for n, (src, dst) in enumerate(((gq_s, gq), (gk_s, gk), (gv_s, gv), (go_s, go)))
    ]
    for copy in copies:
        copy.start()
    for copy in copies:
        copy.wait()


def finish_mlp(at_ref, *rest):
    pieces, (gg, gu, gd, gg_s, gu_s, gd_s, sems) = rest[:8], rest[8:]
    rows = gg.shape[0]
    copies = []
    for i, (ref, out) in enumerate(((gg_s, gg), (gu_s, gu), (gd_s, gd))):
        for n, piece in enumerate(pieces):
            ref[:, aligned(at_ref[n], LANES)] = piece[i * rows : (i + 1) * rows].astype(full)
        copies.append(pltpu.make_async_copy(ref, out, sems.at[i]))
        copies[-1].start()
    for copy in copies:
        copy.wait()


def build(n_dp, n_t):
    extra = [1 << k for k in range(3, n_dp.bit_length() - 1)]

    def perm(target):
        pairs = []
        for d in range(n_dp):
            for t in range(n_t):
                to = target(d, t)
                if to is not None:
                    pairs.append((d * n_t + t, to[0] * n_t + to[1]))
        return pairs

    def sender(target):
        return functools.partial(lax.ppermute, axis_name=AXES, perm=perm(target))

    send_core = sender(lambda d, t: (d ^ 1, t))
    send_pair = sender(lambda d, t: (d, t ^ 1))
    send_far = sender(lambda d, t: (d, t ^ 2))
    send_owner = sender(lambda d, t: (d, t ^ 2) if (d & 1) != (t >> 1) else None)
    send_help = sender(lambda d, t: (d ^ 1, t) if (d & 1) == (t >> 1) else None)
    send_one = sender(lambda d, t: (d ^ (4 if d & 1 else 2), t))
    send_two = sender(lambda d, t: (d ^ (2 if d & 1 else 4), t))
    send_extra = [sender(lambda d, t, bit=bit: (d ^ bit, t)) for bit in extra]

    def local(
        tokens, gain_attn, w_query, w_key, w_value, w_out, gain_mlp, w_gate, w_up, w_down, out_grad
    ):
        own_rows, depth = tokens.shape
        hidden_cols = w_gate.shape[1]
        head_cols = w_query.shape[1]
        padded = -(-hidden_cols // 256) * 256
        d, t = lax.axis_index("dp"), lax.axis_index("tensor")
        core, part, side = d & 1, t & 1, t >> 1
        x, y = (d >> 1) & 1, (d >> 2) & 1
        resident = core == side

        def quarter_of(flip_one, flip_two, which=core):
            flip_x = jnp.where(which == 0, flip_one, flip_two)
            flip_y = jnp.where(which == 0, flip_two, flip_one)
            return 2 * (y ^ flip_y) + (x ^ flip_x)

        flips = ((0, 0), (1, 0), (0, 1), (1, 1))
        blocks = [2 * quarter_of(*f) + core for f in flips]
        blocks += [2 * quarter_of(*f, which=1 - core) + 1 - core for f in flips]
        roles = [quarter_of(*f) for f in ((1, 1), (1, 0), (0, 1), (0, 0))]
        table = jnp.stack(
            blocks + [jnp.where(resident, 1, 0), part, side] + roles
        ).astype(jnp.int32)

        def spread(piece, to_core):
            one = send_one(piece)
            two = send_two(piece)
            both = send_two(one)
            mine = [piece, one, two, both]
            return mine + [to_core(p) for p in mine]

        def reduce_slice(diag, one, two, own, axis):
            far = send_one(diag)
            near = send_one(one)
            two = (two.astype(full) + far.astype(full)).astype(low)
            last = send_two(two)
            total = own.astype(full) + near.astype(full) + last.astype(full)
            for send in send_extra:
                total = total + send(total.astype(low)).astype(full)
            arrived = send_owner(total.astype(low))
            total = (total + arrived.astype(full)).astype(low)
            size = total.shape[axis] // 2
            keep = lax.dynamic_slice_in_dim(total, core * size, size, axis)
            give = lax.dynamic_slice_in_dim(total, (1 - core) * size, size, axis)
            piece = jnp.where(resident, keep, send_help(give))
            return spread(piece, send_core)

        def halves(array):
            return array[:own_rows], array[own_rows:]

        gate_t, up_t = w_gate.T, w_up.T
        piece = call(
            pack_attention,
            [((3 * head_cols + w_out.shape[0], LANES), low)],
            (table, w_query, w_key, w_value, w_out),
            scratch=[pltpu.SemaphoreType.DMA((7,))],
            smem=1,
            anywhere=4,
        )[0]
        pieces = spread(send_far(piece), send_help)
        qkv_w, out_w = call(
            unpack_attention,
            [((depth, 3 * head_cols), low), (w_out.shape, low)],
            (table, w_query, w_key, w_value, w_out, *pieces),
            smem=1,
            size=1 << 21,
        )

        token_pair = send_pair(tokens)
        tail = tokens[own_rows - WINDOW :]
        halo = sender(lambda d_, t_: (d_, 2) if t_ == 1 else None)(tail) + sender(
            lambda d_, t_: (d_, 3) if t_ == 1 else None
        )(tail)
        ours = (halo, tokens, token_pair)
        theirs = tuple(send_core(a) for a in ours)

        piece = call(
            pack_mlp,
            [((3 * hidden_cols, LANES), low)],
            (table, gate_t, up_t, w_down),
            scratch=[pltpu.SemaphoreType.DMA((3,))],
            smem=1,
            anywhere=3,
        )[0]
        pieces = spread(send_far(piece), send_help)
        gate_w, up_w, down_w = call(
            unpack_mlp,
            [((padded, depth), low)] * 3,
            (table, gate_t, up_t, w_down, *pieces),
            smem=1,
            size=1 << 22,
        )
        grad_pair = send_pair(out_grad)
        dys = [jnp.where(part == k, out_grad, grad_pair) for k in range(2)]
        dys_sib = [send_core(a) for a in dys]
        token_rows = [jnp.where(part == k, tokens, token_pair) for k in range(2)]

        attn_gain = gain_attn.reshape(1, depth)
        mlp_gain = gain_mlp.astype(full)

        ext = WINDOW + 2 * own_rows
        normed, qkv, mixed, mine, sib = call(
            forward_kernel,
            [
                ((2, ext, depth), low),
                ((2, ext, 3 * head_cols), low),
                ((2, 2 * own_rows, head_cols), low),
                ((2 * own_rows, depth), full),
                ((2 * own_rows, depth), low),
            ],
            (table, attn_gain, qkv_w, out_w, *ours, *theirs),
            smem=1,
            flops=5 << 30,
            size=8 << 20,
        )

        def total_over_group(mine, sib):
            chunk = (mine.astype(full) + send_core(sib).astype(full)).astype(low)
            return chunk.astype(full) + send_pair(chunk).astype(full)

        middles, mids = [], []
        for k, (a, b) in enumerate(zip(halves(mine), halves(sib))):
            middle = token_rows[k].astype(full) + total_over_group(a, b)
            middles.append(middle)
            mids.append(rms_norm(middle, mlp_gain).astype(low))
        mids_sib = [send_core(a) for a in mids]

        branch_grads, middle_grads, hiddens, tables, gain_part = [], [], [], [], 0.0
        for k in range(2):
            mine, sib, hidden, gg, ug = call(
                mlp_kernel,
                [((own_rows, depth), full), ((own_rows, depth), low)]
                + [((2 * own_rows, padded), low)] * 3,
                (mids[k], mids_sib[k], dys[k], dys_sib[k], gate_w, up_w, down_w),
                flops=5 << 30,
                size=8 << 20,
            )
            tables += [hidden, gg, ug]
            hiddens.append(hidden)
            pull, gain = rms_pull(middles[k], mlp_gain, total_over_group(mine, sib))
            gain_part = gain_part + gain
            middle_grads.append(dys[k].astype(full) + pull)
            branch_grads.append(middle_grads[k].astype(low))
        branch_grads_sib = [send_core(a) for a in branch_grads]

        grad_args = (table, *tables, mids[0], mids_sib[0], mids[1], mids_sib[1],
                     dys[0], dys_sib[0], dys[1], dys_sib[1])
        quarter = ((3 * hidden_cols, depth // 4), low)
        parts = call(
            functools.partial(mlp_grads_kernel, (0,)), [quarter], grad_args, smem=1, flops=1 << 30, size=8 << 20
        )
        parts += call(
            functools.partial(mlp_grads_kernel, (1, 2, 3)), [quarter] * 3, grad_args, smem=1, flops=3 << 30, size=8 << 20
        )
        pieces = reduce_slice(*parts, axis=1)
        shape = (hidden_cols, depth)
        grad_gate, grad_up, grad_down = call(
            finish_mlp,
            [(shape, full, 0)] * 3,
            (table, *pieces),
            scratch=[pltpu.VMEM(shape, full)] * 3 + [pltpu.SemaphoreType.DMA((3,))],
            smem=1,
            size=12 << 20,
        )

        bgs = (branch_grads[0], branch_grads[1], branch_grads_sib[0], branch_grads_sib[1])
        quarter = ((depth // 4, 4 * head_cols), low)
        qkv_grad, diag = call(
            backward_kernel,
            [((2, ext, 3 * head_cols), low), quarter],
            (table, *bgs, out_w, mixed, qkv, normed),
            scratch=[pltpu.VMEM((2, 2 * own_rows, head_cols), low)],
            smem=1,
            flops=5 << 30,
            size=8 << 20,
        )
        parts = [diag] + call(
            attention_grads_kernel,
            [quarter] * 3,
            (table, *bgs, mixed, qkv_grad, normed),
            smem=1,
            flops=2 << 30,
            size=8 << 20,
        )
        pieces = reduce_slice(*parts, axis=0)
        grad_query, grad_key, grad_value, grad_out = call(
            finish_attention,
            [(w_query.shape, full, 0)] * 3 + [(w_out.shape, full, 0)],
            (table, *pieces),
            scratch=[pltpu.VMEM(w_query.shape, full)] * 3
            + [pltpu.VMEM(w_out.shape, full), pltpu.SemaphoreType.DMA((4,))],
            smem=1,
            size=4 << 20,
        )

        outs = []
        for k in range(2):
            outs.append(mat(hiddens[k], down_w))
        arrived = [send_core(o[own_rows:].astype(low)) for o in outs]
        sums = [o[:own_rows] + a.astype(full) for o, a in zip(outs, arrived)]
        arrived = send_pair(jnp.where(part == 0, sums[1], sums[0]).astype(low))
        own_middle = jnp.where(part == 0, middles[0], middles[1])
        output = own_middle + jnp.where(part == 0, sums[0], sums[1]) + arrived.astype(full)
        output = output.astype(low)

        arrived = send_core(mat_right(qkv_grad[1], qkv_w).astype(low))
        mine = mat_right(qkv_grad[0], qkv_w) + arrived.astype(full)
        halo_part = mine[:WINDOW]
        first, second = halves(mine[WINDOW:])
        away = jnp.where(part == 0, second, first)
        arrived = send_pair(jnp.concatenate([halo_part, away], axis=0).astype(low)).astype(full)
        halo_grad = sender(lambda d_, t_: (d_, 1) if t_ == 2 else None)(
            (halo_part + arrived[:WINDOW]).astype(low)
        )
        normed_grad = jnp.where(part == 0, first, second) + arrived[WINDOW:]
        normed_grad = normed_grad + jnp.pad(halo_grad.astype(full), ((own_rows - WINDOW, 0), (0, 0)))
        pull, attn_gain_part = rms_pull(tokens.astype(full), gain_attn.astype(full), normed_grad)
        input_grad = jnp.where(part == 0, middle_grads[0], middle_grads[1]) + pull

        gains = jnp.concatenate([attn_gain_part, 0.5 * gain_part], axis=0)
        for send in [send_core, send_one, send_two, send_pair, send_far] + send_extra:
            gains = gains + send(gains)
        return (
            output,
            input_grad,
            gains[0],
            grad_query,
            grad_key,
            grad_value,
            grad_out,
            gains[1],
            grad_gate.T,
            grad_up.T,
            grad_down,
        )

    return local


def solution(mesh):
    both = P(("dp", "tensor"), None)
    columns, rows = P(None, "tensor"), P("tensor", None)
    return jax.shard_map(
        build(mesh.shape["dp"], mesh.shape["tensor"]),
        mesh=mesh,
        in_specs=(both, P(), columns, columns, columns, rows, P(), columns, columns, rows, both),
        out_specs=(both, both, P(), columns, columns, columns, rows, P(), columns, columns, rows),
        check_vma=False,
    )
```

```python
import functools

import jax
import jax.numpy as jnp
from jax import lax
from jax.experimental import pallas as pl
from jax.experimental.pallas import tpu as pltpu
from jax.sharding import PartitionSpec as P

HEAD_DIM = 64
WINDOW = 64
LANES = 128

norm_eps = 1e-05
very_low = -1e30
AXES = ("dp", "tensor")
low = jnp.bfloat16
full = jnp.float32


def mat(left, right):
    return jnp.dot(left, right, preferred_element_type=full)


def mat_left(left, right):
    return lax.dot_general(left, right, (((0,), (0,)), ((), ())), preferred_element_type=full)


def mat_right(left, right):
    return lax.dot_general(left, right, (((1,), (1,)), ((), ())), preferred_element_type=full)


def rms_scale(values):
    return lax.rsqrt(jnp.mean(values * values, axis=-1, keepdims=True) + norm_eps)


def rms_norm(values, gain):
    return values * rms_scale(values) * gain


def rms_pull(values, gain, grad):
    scale = rms_scale(values)
    unit = values * scale
    scaled = grad * gain
    inner = jnp.mean(scaled * unit, axis=-1, keepdims=True)
    return scale * (scaled - unit * inner), jnp.sum(grad * unit, axis=0, keepdims=True)


def after(value, event):
    return lax.optimization_barrier((value, event))[0]


def aligned(index, size):
    return pl.ds(pl.multiple_of(index * size, size), size)


class Place:
    def __init__(self):
        d, t = lax.axis_index("dp"), lax.axis_index("tensor")
        self.core, self.part, self.side = d & 1, t & 1, (t >> 1) & 1
        self.x, self.y = (d >> 1) & 1, (d >> 2) & 1
        self.resident = 1 - (self.core ^ self.side)

    def quarter(self, one, two, other=0):
        core = self.core ^ other
        flip_x = (1 - core) * one + core * two
        flip_y = (1 - core) * two + core * one
        return 2 * (self.y ^ flip_y) + (self.x ^ flip_x)

    def block(self, n):
        other = n // 4
        return 2 * self.quarter(n % 2, n % 4 // 2, other) + (self.core ^ other)

    def role(self, n):
        return self.quarter((1, 1, 0, 0)[n], (1, 0, 1, 0)[n])


def call(kernel, outs, args, scratch=(), anywhere=0, limit=24):
    specs = [pl.BlockSpec(memory_space=pl.ANY)] * anywhere + [
        pl.BlockSpec(memory_space=pltpu.VMEM)
    ] * (len(args) - anywhere)
    shapes = [jax.ShapeDtypeStruct(o[0], o[1]) for o in outs]
    places = [
        pl.BlockSpec(memory_space=pl.ANY if len(o) > 2 else pltpu.VMEM) for o in outs
    ]
    results = pl.pallas_call(
        kernel,
        out_shape=shapes,
        in_specs=specs,
        out_specs=places,
        scratch_shapes=list(scratch),
        compiler_params=pltpu.CompilerParams(vmem_limit_bytes=limit << 20),
        cost_estimate=pl.CostEstimate(flops=0, bytes_accessed=0, transcendentals=0),
    )(*args)
    return list(results)


def pack_attention(q_ref, k_ref, v_ref, o_ref, out_ref, sems):
    block = aligned(Place().block(0), LANES)
    moves = []
    for i, ref in enumerate((q_ref, k_ref, v_ref)):
        for j in range(2):
            moves.append((ref.at[block, pl.ds(j * LANES, LANES)], (2 * i + j) * LANES, LANES))
    moves.append((o_ref.at[:, block], 6 * LANES, o_ref.shape[0]))
    copies = [
        pltpu.make_async_copy(src, out_ref.at[pl.ds(top, size)], sems.at[n])
        for n, (src, top, size) in enumerate(moves)
    ]
    for copy in copies:
        copy.start()
    for copy in copies:
        copy.wait()


def pack_mlp(_, g_ref, u_ref, d_ref, out_ref, sems):
    block = aligned(Place().block(0), LANES)
    rows = g_ref.shape[0]
    copies = [
        pltpu.make_async_copy(ref.at[:, block], out_ref.at[pl.ds(n * rows, rows)], sems.at[n])
        for n, ref in enumerate((g_ref, u_ref, d_ref))
    ]
    for copy in copies:
        copy.start()
    for copy in copies:
        copy.wait()


def unpack_attention(q_ref, k_ref, v_ref, o_ref, *rest):
    pieces, (qkv_ref, out_ref) = rest[:8], rest[8:]
    here = Place()
    width = q_ref.shape[1]

    @pl.when(here.resident == 1)
    def _():
        for i, ref in enumerate((q_ref, k_ref, v_ref)):
            qkv_ref[:, i * width : (i + 1) * width] = ref[...]
        out_ref[...] = o_ref[...]

    @pl.when(here.resident == 0)
    def _():
        for n, piece in enumerate(pieces):
            block = aligned(here.block(n), LANES)
            for j in range(3 * width // LANES):
                qkv_ref[block, j * LANES : (j + 1) * LANES] = piece[j * LANES : (j + 1) * LANES]
            out_ref[:, block] = piece[3 * width :]


def unpack_mlp(g_ref, u_ref, d_ref, *rest):
    pieces, outs, sems = rest[:8], rest[8:11], rest[11]
    here = Place()
    rows = g_ref.shape[0]

    @pl.when(here.resident == 1)
    def _():
        copies = [
            pltpu.make_async_copy(ref, out.at[pl.ds(0, rows)], sems.at[n])
            for n, (ref, out) in enumerate(zip((g_ref, u_ref, d_ref), outs))
        ]
        for copy in copies:
            copy.start()
        for out in outs:
            out[rows:] = jnp.zeros((out.shape[0] - rows, out.shape[1]), low)
        for copy in copies:
            copy.wait()

    @pl.when(here.resident == 0)
    def _():
        copies = [
            pltpu.make_async_copy(
                piece.at[pl.ds(i * rows, rows)],
                out.at[pl.ds(0, rows), aligned(here.block(n), LANES)],
                sems.at[3 * n + i],
            )
            for n, piece in enumerate(pieces)
            for i, out in enumerate(outs)
        ]
        for copy in copies:
            copy.start()
        for out in outs:
            out[rows:] = jnp.zeros((out.shape[0] - rows, out.shape[1]), low)
        for copy in copies:
            copy.wait()


def head_pair(rows):
    lane = lax.broadcasted_iota(jnp.int32, rows.shape, 1)
    zero = jnp.zeros_like(rows)
    return jnp.concatenate(
        [jnp.where(lane < HEAD_DIM, rows, zero), jnp.where(lane < HEAD_DIM, zero, rows)], axis=0
    )


def unstack(stacked):
    half = stacked.shape[0] // 2
    lane = lax.broadcasted_iota(jnp.int32, (half, stacked.shape[1]), 1)
    return jnp.where(lane < HEAD_DIM, stacked[:half], stacked[half:])


def band(first, has_halo):
    shape = (2 * WINDOW, 2 * WINDOW)
    row = lax.broadcasted_iota(jnp.int32, shape, 0) % WINDOW
    col = lax.broadcasted_iota(jnp.int32, shape, 1)
    mask = (col > row) & (col <= row + WINDOW)
    if first:
        mask = mask & ((col >= WINDOW) | (has_halo > 0))
    return mask


def softmax(scores, mask):
    scores = jnp.where(mask, scores * HEAD_DIM ** (-0.5), very_low)
    expo = jnp.exp(scores - jnp.max(scores, axis=-1, keepdims=True))
    return expo * (1.0 / jnp.sum(expo, axis=-1, keepdims=True))


def place(ref, seq, part, halo, own, pair, change):
    rows = own.shape[0]
    ref[seq, 0:WINDOW] = change(halo[...])
    ref[seq, pl.ds(pl.multiple_of(WINDOW + rows * part, WINDOW), rows)] = change(own[...])
    ref[seq, pl.ds(pl.multiple_of(WINDOW + rows * (1 - part), WINDOW), rows)] = change(pair[...])


def forward_kernel(
    gain_ref, qkv_w, out_w, halo0, own0, pair0, halo1, own1, pair1,
    normed_ref, qkv_ref, mixed_ref, mine_own, mine_pair, sib_own, sib_pair,
):
    here = Place()
    part, has_halo = here.part, here.side
    gain = gain_ref[...].astype(full)

    def norm(rows):
        return rms_norm(rows.astype(full), gain).astype(low)

    place(normed_ref, 0, part, halo0, own0, pair0, norm)
    place(normed_ref, 1, part, halo1, own1, pair1, norm)
    seqs, rows, width3 = qkv_ref.shape
    width = width3 // 3
    for seq in (1, 0):
        qkv_ref[seq] = mat(normed_ref[seq], qkv_w[...]).astype(low)
    plain, first = band(False, 0), band(True, has_halo)
    units = [(lane, top) for top in range(0, rows - WINDOW, WINDOW) for lane in range(0, width, LANES)]
    for seq in (1, 0):
        for start in range(0, len(units), 4):
            group = units[start : start + 4]
            scores = []
            for lane, top in group:
                q = qkv_ref[seq, top + WINDOW : top + 2 * WINDOW, lane : lane + LANES]
                k = qkv_ref[seq, top : top + 2 * WINDOW, width + lane : width + lane + LANES]
                scores.append(mat_right(head_pair(q), k))
            probs = [
                softmax(s, plain if top else first).astype(low)
                for s, (lane, top) in zip(scores, group)
            ]
            for p, (lane, top) in zip(probs, group):
                at = 2 * width + lane
                v = qkv_ref[seq, top : top + 2 * WINDOW, at : at + LANES]
                mixed_ref[seq, top : top + WINDOW, lane : lane + LANES] = unstack(mat(p, v)).astype(low)
        half = (rows - WINDOW) // 2
        for target, which in ((sib_own if seq else mine_own, part), (sib_pair if seq else mine_pair, 1 - part)):
            target[...] = mat(mixed_ref[seq, aligned(which, half)], out_w[...]).astype(low)


def backward_kernel(
    bg00, bg01, bg10, bg11, out_w, mixed_ref, qkv_ref, normed_ref,
    out_ref, first_ref, mixed_grad,
):
    here = Place()
    has_halo = here.side
    seqs, rows, width3 = qkv_ref.shape
    width = width3 // 3
    factor = HEAD_DIM ** (-0.5)
    half = bg00.shape[0]
    for seq, pair in enumerate(((bg00, bg01), (bg10, bg11))):
        for ref, which in zip(pair, (here.part, 1 - here.part)):
            mixed_grad[seq, aligned(which, half)] = mat_right(ref[...], out_w[...]).astype(low)
    plain, first = band(False, 0), band(True, has_halo)
    for seq in range(seqs):
        out_ref[seq, 0:WINDOW, 0:width] = jnp.zeros((WINDOW, width), low)
        tails = {}
        for lane in range(0, width, LANES):
            tails[lane] = (jnp.zeros((WINDOW, LANES), full), jnp.zeros((WINDOW, LANES), full))
        for top0 in range(0, rows - WINDOW, 2 * WINDOW):
            group = [(lane, top0 + w) for w in (0, WINDOW) for lane in range(0, width, LANES)]
            loaded, scores, prob_grads = [], [], []
            for lane, top in group:
                q = head_pair(qkv_ref[seq, top + WINDOW : top + 2 * WINDOW, lane : lane + LANES])
                k = qkv_ref[seq, top : top + 2 * WINDOW, width + lane : width + lane + LANES]
                v = qkv_ref[seq, top : top + 2 * WINDOW, 2 * width + lane : 2 * width + lane + LANES]
                g = head_pair(mixed_grad[seq, top : top + WINDOW, lane : lane + LANES])
                loaded.append((q, k, g))
                scores.append(mat_right(q, k))
                prob_grads.append(mat_right(g, v))
            probs = [softmax(s, plain if top else first) for s, (lane, top) in zip(scores, group)]
            score_grads = [
                (p * (pg - jnp.sum(p * pg, axis=-1, keepdims=True))).astype(low)
                for p, pg in zip(probs, prob_grads)
            ]
            for p, sg, (q, k, g), (lane, top) in zip(probs, score_grads, loaded, group):
                q_grad = unstack(mat(sg, k)) * factor
                k_grad = mat_left(sg, q) * factor
                v_grad = mat_left(p.astype(low), g)
                k_tail, v_tail = tails[lane]
                out_ref[seq, top + WINDOW : top + 2 * WINDOW, lane : lane + LANES] = q_grad.astype(low)
                at = width + lane
                out_ref[seq, top : top + WINDOW, at : at + LANES] = (k_tail + k_grad[:WINDOW]).astype(low)
                at = 2 * width + lane
                out_ref[seq, top : top + WINDOW, at : at + LANES] = (v_tail + v_grad[:WINDOW]).astype(low)
                tails[lane] = (k_grad[WINDOW:], v_grad[WINDOW:])
        for lane, (k_tail, v_tail) in tails.items():
            at = width + lane
            out_ref[seq, rows - WINDOW : rows, at : at + LANES] = k_tail.astype(low)
            at = 2 * width + lane
            out_ref[seq, rows - WINDOW : rows, at : at + LANES] = v_tail.astype(low)
    attention_role(here.part, here.role(0), first_ref, (bg00, bg01, bg10, bg11), mixed_ref, out_ref, normed_ref)


def attention_role(part, quarter, target, grads, mixed_ref, qkv_grad_ref, normed_ref):
    seqs, rows, width3 = qkv_grad_ref.shape
    block = aligned(quarter, target.shape[0])
    total = mat_left(normed_ref[0, :, block], qkv_grad_ref[0])
    total += mat_left(normed_ref[1, :, block], qkv_grad_ref[1])
    target[:, :width3] = total.astype(low)
    half = grads[0].shape[0]
    total = None
    for n, ref in enumerate(grads):
        seq, i = divmod(n, 2)
        term = mat_left(ref[:, block], mixed_ref[seq, aligned(1 - part if i else part, half)])
        total = term if total is None else total + term
    target[:, width3:] = total.astype(low)


def attention_grads_kernel(
    bg00, bg01, bg10, bg11, mixed_ref, qkv_grad_ref, normed_ref, one_ref, two_ref, own_ref
):
    here = Place()
    for n, ref in enumerate((one_ref, two_ref, own_ref)):
        attention_role(
            here.part, here.role(1 + n), ref, (bg00, bg01, bg10, bg11), mixed_ref, qkv_grad_ref, normed_ref
        )


def normed_grad_kernel(_, grad_ref, qkv_w, mine_ref, sib_ref):
    part = Place().part
    half = (grad_ref.shape[1] - WINDOW) // 2
    for seq, target in ((1, sib_ref), (0, mine_ref)):
        target[0:WINDOW] = mat_right(grad_ref[seq, 0:WINDOW], qkv_w[...]).astype(target.dtype)
        for i, which in enumerate((part, 1 - part)):
            at = pl.ds(pl.multiple_of(WINDOW + half * which, WINDOW), half)
            target[WINDOW + i * half : WINDOW + (i + 1) * half] = mat_right(
                grad_ref[seq, at], qkv_w[...]
            ).astype(target.dtype)


def mlp_kernel(
    mid0, mid1, dy0, dy1, gate_w, up_w, down_w, mine_ref, theirs_ref, hidden_ref, gg_ref, ug_ref
):
    rows = mid0.shape[0]
    for n, (mid, dy, target) in enumerate(((mid1, dy1, theirs_ref), (mid0, dy0, mine_ref))):
        at = pl.ds((1 - n) * rows, rows)
        gate = mat_right(mid[...], gate_w[...])
        up = mat_right(mid[...], up_w[...])
        back = mat_right(dy[...], down_w[...])
        sig = 1.0 / (1.0 + jnp.exp(-gate))
        silu = gate * sig
        hidden_ref[at] = (silu * up).astype(low)
        ug = (back * silu).astype(low)
        gg = (back * up * sig * (1.0 + gate * (1.0 - sig))).astype(low)
        ug_ref[at] = ug
        gg_ref[at] = gg
        target[...] = (mat(gg, gate_w[...]) + mat(ug, up_w[...])).astype(target.dtype)


def mlp_role(quarter, target, rows, tables, mids, dys):
    block = aligned(quarter, target.shape[1])
    (h0, g0, u0), (h1, g1, u1) = tables

    def total(left0, left1, right):
        right = [r[:, block] for r in right]
        return (
            mat_left(left0[...], jnp.concatenate(right[:2], axis=0))
            + mat_left(left1[...], jnp.concatenate(right[2:], axis=0))
        )[:rows].astype(low)

    target[0:rows] = total(g0, g1, mids)
    target[rows : 2 * rows] = total(u0, u1, mids)
    target[2 * rows : 3 * rows] = total(h0, h1, dys)


def mlp_grads_kernel(roles, _, h0, g0, u0, h1, g1, u1, *rest):
    mids, dys, targets = rest[:4], rest[4:8], rest[8:]
    rows = targets[0].shape[0] // 3
    here = Place()
    for role, target in zip(roles, targets):
        mlp_role(here.role(role), target, rows, ((h0, g0, u0), (h1, g1, u1)), mids, dys)


def split_kernel(axis, total_ref, arrived_ref, keep_ref, give_ref):
    core = Place().core
    size = total_ref.shape[axis] // 2
    for which, ref in ((core, keep_ref), (1 - core, give_ref)):
        at = (slice(None),) * axis + (aligned(which, size),)
        ref[...] = (total_ref[at].astype(full) + arrived_ref[at].astype(full)).astype(low)


def choose_kernel(keep_ref, help_ref, out_ref):
    here = Place()

    @pl.when(here.resident == 1)
    def _():
        out_ref[...] = keep_ref[...]

    @pl.when(here.resident == 0)
    def _():
        out_ref[...] = help_ref[...]


def middle_kernel(gain_ref, token_ref, sum_ref, arrived_ref, middle_ref, mid_ref):
    middle = token_ref[...].astype(full) + (sum_ref[...].astype(full) + arrived_ref[...].astype(full))
    middle_ref[...] = middle
    mid_ref[...] = rms_norm(middle, gain_ref[...].astype(full)).astype(low)


def middle_grad_kernel(gain_ref, dy_ref, middle_ref, sum_ref, arrived_ref, grad_ref, low_ref, gain_part_ref):
    grad = sum_ref[...].astype(full) + arrived_ref[...].astype(full)
    pull, gain_part_ref[...] = rms_pull(middle_ref[...], gain_ref[...].astype(full), grad)
    total = dy_ref[...].astype(full) + pull
    grad_ref[...] = total
    low_ref[...] = total.astype(low)


def add_kernel(*refs):
    terms, out = refs[:-1], refs[-1]
    total = terms[0][...].astype(full)
    for term in terms[1:]:
        total = total + term[...].astype(full)
    out[...] = total.astype(out.dtype)


def mlp_out_kernel(_, own_ref, pair_ref, down_w, mine_own, mine_pair, sib_own, sib_pair):
    rows = mine_own.shape[0]
    for ref, mine, sib in ((own_ref, mine_own, sib_own), (pair_ref, mine_pair, sib_pair)):
        sib[...] = mat(ref[rows:], down_w[...]).astype(low)
        mine[...] = mat(ref[:rows], down_w[...]).astype(mine.dtype)


def output_kernel(middle_ref, mine_ref, sib_ref, pair_ref, out_ref, scratch, sem):
    total = middle_ref[...] + mine_ref[...] + sib_ref[...].astype(full) + pair_ref[...].astype(full)
    scratch[...] = total.astype(low)
    copy = pltpu.make_async_copy(scratch, out_ref, sem)
    copy.start()
    copy.wait()


def normed_sum_kernel(mine_ref, sib_ref, own_ref, halo_ref, away_ref):
    rows = own_ref.shape[0]

    def total(top, size):
        return mine_ref[top : top + size] + sib_ref[top : top + size].astype(full)

    halo = total(0, WINDOW)
    halo_ref[...] = halo
    away_ref[:WINDOW] = halo.astype(low)
    own_ref[...] = total(WINDOW, rows)
    away_ref[WINDOW:] = total(WINDOW + rows, rows).astype(low)


def halo_kernel(halo_ref, arrived_ref, out_ref):
    out_ref[...] = (halo_ref[...] + arrived_ref[:WINDOW].astype(full)).astype(low)


def input_grad_kernel(
    token_ref, gain_ref, middle_grad_ref, own_ref, arrived_ref, halo_ref, mlp_gain_ref,
    out_ref, gains_ref, scratch, sem,
):
    rows = own_ref.shape[0]
    scratch[...] = own_ref[...] + arrived_ref[WINDOW:].astype(full)
    scratch[rows - WINDOW :] = scratch[rows - WINDOW :] + halo_ref[...].astype(full)
    pull, gain = rms_pull(token_ref[...].astype(full), gain_ref[...].astype(full), scratch[...])
    gains_ref[0:1] = gain
    gains_ref[1:2] = mlp_gain_ref[...]
    scratch[...] = middle_grad_ref[...] + pull
    copy = pltpu.make_async_copy(scratch, out_ref, sem)
    copy.start()
    copy.wait()


def finish_attention(*rest):
    here = Place()
    pieces, (gq, gk, gv, go, gq_s, gk_s, gv_s, go_s, sems) = rest[:8], rest[8:]
    width = gq.shape[1]
    for n, piece in enumerate(pieces):
        block = aligned(here.block(n), LANES)
        for i, ref in enumerate((gq_s, gk_s, gv_s)):
            ref[block] = piece[:, i * width : (i + 1) * width].astype(full)
        go_s[:, block] = piece[:, 3 * width :].astype(full).T
    copies = [
        pltpu.make_async_copy(src, dst, sems.at[n])
        for n, (src, dst) in enumerate(((gq_s, gq), (gk_s, gk), (gv_s, gv), (go_s, go)))
    ]
    for copy in copies:
        copy.start()
    for copy in copies:
        copy.wait()


def finish_mlp(*rest):
    here = Place()
    pieces, (gg, gu, gd, gg_s, gu_s, gd_s, sems) = rest[:8], rest[8:]
    rows = gg.shape[0]
    copies = []
    for i, (ref, out) in enumerate(((gg_s, gg), (gu_s, gu), (gd_s, gd))):
        for n, piece in enumerate(pieces):
            ref[:, aligned(here.block(n), LANES)] = piece[i * rows : (i + 1) * rows].astype(full)
        copies.append(pltpu.make_async_copy(ref, out, sems.at[i]))
        copies[-1].start()
    for copy in copies:
        copy.wait()


def build(n_dp, n_t):
    extra = [1 << k for k in range(3, n_dp.bit_length() - 1)]

    def perm(target):
        pairs = []
        for d in range(n_dp):
            for t in range(n_t):
                to = target(d, t)
                if to is not None:
                    pairs.append((d * n_t + t, to[0] * n_t + to[1]))
        return pairs

    def sender(target):
        return functools.partial(lax.ppermute, axis_name=AXES, perm=perm(target))

    send_core = sender(lambda d, t: (d ^ 1, t))
    send_pair = sender(lambda d, t: (d, t ^ 1))
    send_far = sender(lambda d, t: (d, t ^ 2))
    send_owner = sender(lambda d, t: (d, t ^ 2) if (d & 1) != (t >> 1) else None)
    send_help = sender(lambda d, t: (d ^ 1, t) if (d & 1) == (t >> 1) else None)
    send_one = sender(lambda d, t: (d ^ (4 if d & 1 else 2), t))
    send_two = sender(lambda d, t: (d ^ (2 if d & 1 else 4), t))
    send_extra = [sender(lambda d, t, bit=bit: (d ^ bit, t)) for bit in extra]

    def local(
        tokens, gain_attn, w_query, w_key, w_value, w_out, gain_mlp, w_gate, w_up, w_down, out_grad
    ):
        own_rows, depth = tokens.shape
        hidden_cols = w_gate.shape[1]
        head_cols = w_query.shape[1]
        padded = -(-hidden_cols // 256) * 256
        def spread(piece, to_core, late=None):
            one = send_one(piece)
            two = send_two(piece)
            both = send_two(after(one, two))
            mine = [piece, one, two, both]
            if late is not None:
                mine[3] = after(both, late)
            return mine + [to_core(p) for p in mine]

        gate_t, up_t = w_gate.T, w_up.T
        stay = functools.partial(pltpu.with_memory_space_constraint, memory_space=pltpu.HBM)
        packed = call(
            pack_attention,
            [((3 * head_cols + w_out.shape[0], LANES), low)],
            tuple(stay(w) for w in (w_query, w_key, w_value, w_out)),
            scratch=[pltpu.SemaphoreType.DMA((7,))],
            anywhere=4,
        )[0]
        attn_piece = send_far(packed)
        token_pair = send_pair(after(tokens, packed))
        tail = after(tokens, packed)[own_rows - WINDOW :]
        halo = sender(lambda d_, t_: (d_, 2) if t_ == 1 else None)(tail) + sender(
            lambda d_, t_: (d_, 3) if t_ == 1 else None
        )(tail)
        token_sib = send_core(after(tokens, packed))
        packed = call(
            pack_mlp,
            [((3 * hidden_cols, LANES), low)],
            (packed, stay(gate_t), stay(up_t), stay(w_down)),
            scratch=[pltpu.SemaphoreType.DMA((3,))],
            anywhere=4,
        )[0]
        mlp_piece = send_far(packed)
        dy, dy_pair = out_grad, send_pair(after(out_grad, attn_piece))
        pieces = spread(attn_piece, send_help, mlp_piece)
        halo_sib, token_pair_sib = send_core(halo), send_core(after(token_pair, pieces[1]))
        halo_sib = after(halo_sib, dy_pair)
        qkv_w, out_w = call(
            unpack_attention,
            [((depth, 3 * head_cols), low), (w_out.shape, low)],
            (w_query, w_key, w_value, w_out, *pieces),
        )

        ext = WINDOW + 2 * own_rows
        chunk = ((own_rows, depth), low)
        normed, qkv, mixed, mine_own, mine_pair, sib_own, sib_pair = call(
            forward_kernel,
            [((2, ext, depth), low), ((2, ext, 3 * head_cols), low), ((2, 2 * own_rows, head_cols), low)]
            + [chunk] * 4,
            (gain_attn.reshape(1, depth), qkv_w, out_w, halo, tokens, token_pair, halo_sib, token_sib, token_pair_sib),
        )

        def add(*terms, dtype=low):
            return call(add_kernel, [(terms[0].shape, dtype)], terms)[0]

        sum_own = add(mine_own, send_core(sib_own))
        sum_pair = add(mine_pair, send_core(sib_pair))
        arrived_pair = send_pair(sum_own)
        arrived_own = send_pair(sum_pair)

        pieces = spread(after(mlp_piece, sum_pair), send_help)
        dy_sib, dy_pair_sib = send_core(after(dy, sum_pair)), send_core(after(dy_pair, sum_pair))
        gate_w, up_w, down_w = call(
            unpack_mlp,
            [((padded, depth), low)] * 3,
            (gate_t, up_t, w_down, *pieces),
            scratch=[pltpu.SemaphoreType.DMA((24,))],
            anywhere=11,
        )

        mlp_gain = gain_mlp.reshape(1, depth)
        wide = ((own_rows, depth), full)
        middle_pair, mid_pair = call(middle_kernel, [wide, chunk], (mlp_gain, token_pair, sum_pair, arrived_pair))
        middle_own, mid_own = call(middle_kernel, [wide, chunk], (mlp_gain, tokens, sum_own, arrived_own))
        mid_pair_sib, mid_own_sib = send_core(mid_pair), send_core(mid_own)

        def feed_forward(mid, mid_sib, dy, dy_sib):
            return call(
                mlp_kernel,
                [chunk, chunk] + [((2 * own_rows, padded), low)] * 3,
                (mid, mid_sib, dy, dy_sib, gate_w, up_w, down_w),
            )

        mine, sib, *tables_pair = feed_forward(mid_pair, after(mid_pair_sib, arrived_own), dy_pair, dy_pair_sib)
        sum_pair = add(mine, send_core(sib))
        arrived_own = send_pair(sum_pair)
        mine, sib, *tables_own = feed_forward(mid_own, after(mid_own_sib, sum_pair), dy, dy_sib)
        sum_own = add(mine, send_core(sib))
        arrived_pair = send_pair(sum_own)

        grad_args = (sum_own, *tables_pair, *tables_own, mid_pair, mid_pair_sib,
                     mid_own, mid_own_sib, dy_pair, dy_pair_sib, dy, dy_sib)
        quarter = ((3 * hidden_cols, depth // 4), low)
        mlp_parts = call(
            functools.partial(mlp_grads_kernel, (0,)), [quarter], grad_args
        )
        mlp_parts += call(
            functools.partial(mlp_grads_kernel, (1, 2, 3)), [quarter] * 3, (mlp_parts[0],) + grad_args[1:]
        )
        mlp_far, mlp_near = send_one(mlp_parts[0]), send_one(mlp_parts[1])

        gain_row = ((1, depth), full)
        middle_grad, branch_own, gain_own = call(
            middle_grad_kernel, [wide, chunk, gain_row], (mlp_gain, dy, middle_own, sum_own, after(arrived_own, mlp_parts[1]))
        )
        _, branch_pair, _ = call(
            middle_grad_kernel, [wide, chunk, gain_row], (mlp_gain, dy_pair, middle_pair, sum_pair, after(arrived_pair, branch_own))
        )
        branch_own_sib, branch_pair_sib = send_core(branch_own), send_core(branch_pair)
        mlp_two = add(mlp_parts[2], after(mlp_far, branch_own))
        mlp_last = send_two(mlp_two)

        bgs = (branch_own, branch_pair, branch_own_sib, branch_pair_sib)
        quarter = ((depth // 4, 4 * head_cols), low)
        qkv_grad, diag = call(
            backward_kernel,
            [((2, ext, 3 * head_cols), low), quarter],
            (*bgs, out_w, mixed, qkv, normed),
            scratch=[pltpu.VMEM((2, 2 * own_rows, head_cols), low)],
        )
        far = send_one(diag)
        _, one, two, last_own = [diag] + call(
            attention_grads_kernel,
            [quarter] * 3,
            (*bgs, mixed, qkv_grad, normed),
        )
        near = send_one(one)
        grad_mine, grad_sib = call(
            normed_grad_kernel,
            [((ext, depth), full), ((ext, depth), low)],
            (one, qkv_grad, qkv_w),
        )
        grad_arrived = send_core(grad_sib)

        def to_owner(total):
            for send in send_extra:
                total = add(total, send(total))
            return total, send_owner(total)

        def to_both(total, arrived, axis):
            shape = list(total.shape)
            shape[axis] //= 2
            half = (tuple(shape), low)
            keep, give = call(functools.partial(split_kernel, axis), [half, half], (total, arrived))
            return call(choose_kernel, [half], (keep, send_help(give)))[0]

        mlp_total, mlp_arrived = to_owner(add(mlp_parts[3], mlp_near, after(mlp_last, diag)))
        two = add(two, far)
        last = send_two(two)
        grad_own, grad_halo, grad_away = call(
            normed_sum_kernel,
            [wide, ((WINDOW, depth), full), ((WINDOW + own_rows, depth), low)],
            (grad_mine, after(grad_arrived, two)),
        )
        grad_arrived = send_pair(grad_away)
        total, arrived = to_owner(add(last_own, near, last))
        mlp_half = to_both(mlp_total, after(mlp_arrived, total), 1)
        mlp_pieces = spread(mlp_half, send_core)
        half = to_both(total, after(arrived, mlp_half), 0)
        pieces = spread(half, send_core)
        grad_arrived = after(grad_arrived, total)

        mine_own, mine_pair, sib_own, sib_pair = call(
            mlp_out_kernel,
            [wide, chunk, chunk, chunk],
            (mlp_parts[1], tables_own[0], tables_pair[0], down_w),
        )
        arrived_own = send_core(sib_own)
        sum_pair = add(mine_pair, send_core(sib_pair))
        arrived_pair = send_pair(after(sum_pair, total))
        output = call(
            output_kernel,
            [chunk + (0,)],
            (middle_own, mine_own, arrived_own, after(arrived_pair, half)),
            scratch=[pltpu.VMEM(*chunk), pltpu.SemaphoreType.DMA],
        )[0]

        halo_grad = sender(lambda d_, t_: (d_, 1) if t_ == 2 else None)(
            call(halo_kernel, [((WINDOW, depth), low)], (grad_halo, grad_arrived))[0]
        )
        input_grad, gains = call(
            input_grad_kernel,
            [wide + (0,), ((2, depth), full)],
            (tokens, gain_attn.reshape(1, depth), middle_grad, grad_own, grad_arrived, halo_grad, gain_own),
            scratch=[pltpu.VMEM(*wide), pltpu.SemaphoreType.DMA],
        )

        shape = (hidden_cols, depth)
        grad_gate, grad_up, grad_down = call(
            finish_mlp,
            [(shape, full, 0)] * 3,
            mlp_pieces,
            scratch=[pltpu.VMEM(shape, full)] * 3 + [pltpu.SemaphoreType.DMA((3,))],
        )
        grad_query, grad_key, grad_value, grad_out = call(
            finish_attention,
            [(w_query.shape, full, 0)] * 3 + [(w_out.shape, full, 0)],
            pieces,
            scratch=[pltpu.VMEM(w_query.shape, full)] * 3
            + [pltpu.VMEM(w_out.shape, full), pltpu.SemaphoreType.DMA((4,))],
        )

        gains = after(gains, half)
        for send in [send_core, send_one, send_two, send_pair, send_far] + send_extra:
            gains = add(gains, send(gains), dtype=full)
        return (
            output,
            input_grad,
            gains[0],
            grad_query,
            grad_key,
            grad_value,
            grad_out,
            gains[1],
            grad_gate.T,
            grad_up.T,
            grad_down,
        )

    return local


def solution(mesh):
    both = P(("dp", "tensor"), None)
    columns, rows = P(None, "tensor"), P("tensor", None)
    return jax.shard_map(
        build(mesh.shape["dp"], mesh.shape["tensor"]),
        mesh=mesh,
        in_specs=(both, P(), columns, columns, columns, rows, P(), columns, columns, rows, both),
        out_specs=(both, both, P(), columns, columns, columns, rows, P(), columns, columns, rows),
        check_vma=False,
    )
```

```python
import functools

import jax
import jax.numpy as jnp
from jax import lax
from jax.experimental import pallas as pl
from jax.experimental.pallas import tpu as pltpu
from jax.sharding import PartitionSpec as P

HEAD_DIM = 64
WINDOW = 64
LANES = 128

norm_eps = 1e-05
very_low = -1e30
AXES = ("dp", "tensor")
low = jnp.bfloat16
ORDER = {
    "unpacka": ("ca2",),
    "gc": ("hh",),
    "cfa1": ("fhh", "ba1",),
    "zm1": ("zm0",),
    "gx": ("zg1",),
    "zy": ("zt", "h3",),
    "ca2": ("zy",),
    "cba1": ("ba2",),
    "cn": ("zo",),
    "hh": ("bs2", "b3", "out", "bt", "hk",),
    "cba0": ("fhc", "ba2", "ba3",),
    "so": ("a1", "ca2", "ca3",),
    "kp": ("fo",),
    "w1": ("a3",),
    "hk": ("zn",),
    "g1": ("fsp",),
    "a2": ("h2",),
    "zm0": ("unpacka",),
    "ko": ("cqo",),
    "fps": ("unpackf",),
    "cop": ("f2",),
    "ag": ("bwd",),
    "ba3": ("ba1",),
    "x0": ("zg1",),
    "ch": ("packf",),
    "ct": ("pack", "h3",),
    "cfa0": ("x1",),
    "cba3": ("bhs", "bhc",),
    "cyp": ("attend",),
}
COST = {
    "ko": 16,
    "unpackf": 1,
    "mo": 16,
    "fso": 2,
    "g1": 1,
    "hk": 4,
    "bwd": 1,
    "kp": 1,
    "mq": 2,
    "bt": 2,
    "sp": 4,
}
full = jnp.float32


def mat(left, right):
    return jnp.dot(left, right, preferred_element_type=full)


def mat_left(left, right):
    return lax.dot_general(left, right, (((0,), (0,)), ((), ())), preferred_element_type=full)


def mat_right(left, right):
    return lax.dot_general(left, right, (((1,), (1,)), ((), ())), preferred_element_type=full)


def rms_scale(values):
    return lax.rsqrt(jnp.mean(values * values, axis=-1, keepdims=True) + norm_eps)


def rms_norm(values, gain):
    return values * rms_scale(values) * gain


def rms_pull(values, gain, grad):
    scale = rms_scale(values)
    unit = values * scale
    scaled = grad * gain
    inner = jnp.mean(scaled * unit, axis=-1, keepdims=True)
    return scale * (scaled - unit * inner), jnp.sum(grad * unit, axis=0, keepdims=True)


def after(value, event):
    return lax.optimization_barrier((value, event))[0]


def aligned(index, size):
    return pl.ds(pl.multiple_of(index * size, size), size)


class Place:
    def __init__(self):
        d, t = lax.axis_index("dp"), lax.axis_index("tensor")
        self.z, self.core, self.part, self.side = t, d & 1, t & 1, (t >> 1) & 1
        self.x, self.y = (d >> 1) & 1, (d >> 2) & 1
        self.resident = 1 - (self.core ^ self.side)

    def quarter(self, one, two, other=0):
        core = self.core ^ other
        flip_x = (1 - core) * one + core * two
        flip_y = (1 - core) * two + core * one
        return 2 * (self.y ^ flip_y) + (self.x ^ flip_x)

    def block(self, n):
        other = n // 4
        return 2 * self.quarter(n % 2, n % 4 // 2, other) + (self.core ^ other)

    def role(self, n):
        return self.quarter((1, 1, 0, 0)[n], (1, 0, 1, 0)[n])


def call(kernel, outs, args, scratch=(), anywhere=0, limit=24, cost=0):
    specs = [pl.BlockSpec(memory_space=pl.ANY)] * anywhere + [
        pl.BlockSpec(memory_space=pltpu.VMEM)
    ] * (len(args) - anywhere)
    shapes = [jax.ShapeDtypeStruct(o[0], o[1]) for o in outs]
    places = [
        pl.BlockSpec(memory_space=pl.ANY if len(o) > 2 else pltpu.VMEM) for o in outs
    ]
    results = pl.pallas_call(
        kernel,
        out_shape=shapes,
        in_specs=specs,
        out_specs=places,
        scratch_shapes=list(scratch),
        compiler_params=pltpu.CompilerParams(vmem_limit_bytes=limit << 20),
        cost_estimate=pl.CostEstimate(flops=cost * 1153000000, bytes_accessed=0, transcendentals=0),
    )(*args)
    return list(results)


def pack_attention(q_ref, k_ref, v_ref, o_ref, out_ref, sems):
    block = aligned(Place().block(0), LANES)
    moves = []
    for i, ref in enumerate((q_ref, k_ref, v_ref)):
        for j in range(2):
            moves.append((ref.at[block, pl.ds(j * LANES, LANES)], (2 * i + j) * LANES, LANES))
    moves.append((o_ref.at[:, block], 6 * LANES, o_ref.shape[0]))
    copies = [
        pltpu.make_async_copy(src, out_ref.at[pl.ds(top, size)], sems.at[n])
        for n, (src, top, size) in enumerate(moves)
    ]
    for copy in copies:
        copy.start()
    for copy in copies:
        copy.wait()


def pack_mlp(_, g_ref, u_ref, d_ref, out_ref, sems):
    block = aligned(Place().block(0), LANES)
    rows = g_ref.shape[0]
    copies = [
        pltpu.make_async_copy(ref.at[:, block], out_ref.at[pl.ds(n * rows, rows)], sems.at[n])
        for n, ref in enumerate((g_ref, u_ref, d_ref))
    ]
    for copy in copies:
        copy.start()
    for copy in copies:
        copy.wait()


def unpack_attention(q_ref, k_ref, v_ref, o_ref, *rest):
    pieces, (qkv_ref, out_ref) = rest[:8], rest[8:]
    here = Place()
    width = q_ref.shape[1]

    @pl.when(here.resident == 1)
    def _():
        for i, ref in enumerate((q_ref, k_ref, v_ref)):
            qkv_ref[:, i * width : (i + 1) * width] = ref[...]
        out_ref[...] = o_ref[...]

    @pl.when(here.resident == 0)
    def _():
        for n, piece in enumerate(pieces):
            block = aligned(here.block(n), LANES)
            for j in range(3 * width // LANES):
                qkv_ref[block, j * LANES : (j + 1) * LANES] = piece[j * LANES : (j + 1) * LANES]
            out_ref[:, block] = piece[3 * width :]


def unpack_mlp(g_ref, u_ref, d_ref, *rest):
    pieces, outs, sems = rest[:8], rest[8:11], rest[11]
    here = Place()
    rows = g_ref.shape[0]

    @pl.when(here.resident == 1)
    def _():
        copies = [
            pltpu.make_async_copy(ref, out.at[pl.ds(0, rows)], sems.at[n])
            for n, (ref, out) in enumerate(zip((g_ref, u_ref, d_ref), outs))
        ]
        for copy in copies:
            copy.start()
        for out in outs:
            out[rows:] = jnp.zeros((out.shape[0] - rows, out.shape[1]), low)
        for copy in copies:
            copy.wait()

    @pl.when(here.resident == 0)
    def _():
        copies = [
            pltpu.make_async_copy(
                pieces[n].at[pl.ds(i * rows, rows)],
                out.at[pl.ds(0, rows), aligned(here.block(n), LANES)],
                sems.at[3 * n + i],
            )
            for n in range(8)
            for i, out in enumerate(outs)
        ]
        for copy in copies:
            copy.start()
        for out in outs:
            out[rows:] = jnp.zeros((out.shape[0] - rows, out.shape[1]), low)
        for copy in copies:
            copy.wait()


def head_pair(rows):
    lane = lax.broadcasted_iota(jnp.int32, rows.shape, 1)
    zero = jnp.zeros_like(rows)
    return jnp.concatenate(
        [jnp.where(lane < HEAD_DIM, rows, zero), jnp.where(lane < HEAD_DIM, zero, rows)], axis=0
    )


def unstack(stacked):
    half = stacked.shape[0] // 2
    lane = lax.broadcasted_iota(jnp.int32, (half, stacked.shape[1]), 1)
    return jnp.where(lane < HEAD_DIM, stacked[:half], stacked[half:])


def band(first, has_halo):
    shape = (2 * WINDOW, 2 * WINDOW)
    row = lax.broadcasted_iota(jnp.int32, shape, 0) % WINDOW
    col = lax.broadcasted_iota(jnp.int32, shape, 1)
    mask = (col > row) & (col <= row + WINDOW)
    if first:
        mask = mask & ((col >= WINDOW) | (has_halo > 0))
    return mask


def softmax(scores, mask):
    scores = jnp.where(mask, scores * HEAD_DIM ** (-0.5), very_low)
    expo = jnp.exp(scores - jnp.max(scores, axis=-1, keepdims=True))
    return expo * (1.0 / jnp.sum(expo, axis=-1, keepdims=True))


def place(ref, seq, part, halo, own, pair, change):
    rows = own.shape[0]
    ref[seq, 0:WINDOW] = change(halo[...])
    ref[seq, pl.ds(pl.multiple_of(WINDOW + rows * part, WINDOW), rows)] = change(own[...])
    ref[seq, pl.ds(pl.multiple_of(WINDOW + rows * (1 - part), WINDOW), rows)] = change(pair[...])


def forward_kernel(
    gain_ref, qkv_w, out_w, halo0, own0, pair0, halo1, own1, pair1,
    normed_ref, qkv_ref, mixed_ref, mine_own, mine_pair, sib_own, sib_pair,
):
    here = Place()
    part, has_halo = here.part, here.side
    gain = gain_ref[...].astype(full)

    def norm(rows):
        return rms_norm(rows.astype(full), gain).astype(low)

    place(normed_ref, 0, part, halo0, own0, pair0, norm)
    place(normed_ref, 1, part, halo1, own1, pair1, norm)
    seqs, rows, width3 = qkv_ref.shape
    width = width3 // 3
    for seq in (1, 0):
        qkv_ref[seq] = mat(normed_ref[seq], qkv_w[...]).astype(low)
    plain, first = band(False, 0), band(True, has_halo)
    units = [(lane, top) for top in range(0, rows - WINDOW, WINDOW) for lane in range(0, width, LANES)]
    for seq in (1, 0):
        for start in range(0, len(units), 4):
            group = units[start : start + 4]
            scores = []
            for lane, top in group:
                q = qkv_ref[seq, top + WINDOW : top + 2 * WINDOW, lane : lane + LANES]
                k = qkv_ref[seq, top : top + 2 * WINDOW, width + lane : width + lane + LANES]
                scores.append(mat_right(head_pair(q), k))
            probs = [
                softmax(s, plain if top else first).astype(low)
                for s, (lane, top) in zip(scores, group)
            ]
            for p, (lane, top) in zip(probs, group):
                at = 2 * width + lane
                v = qkv_ref[seq, top : top + 2 * WINDOW, at : at + LANES]
                mixed_ref[seq, top : top + WINDOW, lane : lane + LANES] = unstack(mat(p, v)).astype(low)
        half = (rows - WINDOW) // 2
        for target, which in ((sib_own if seq else mine_own, part), (sib_pair if seq else mine_pair, 1 - part)):
            target[...] = mat(mixed_ref[seq, aligned(which, half)], out_w[...]).astype(low)


def backward_kernel(
    bg00, bg01, bg10, bg11, out_w, mixed_ref, qkv_ref, normed_ref,
    out_ref, first_ref, mixed_grad,
):
    here = Place()
    has_halo = here.side
    seqs, rows, width3 = qkv_ref.shape
    width = width3 // 3
    factor = HEAD_DIM ** (-0.5)
    half = bg00.shape[0]
    for seq, pair in enumerate(((bg00, bg01), (bg10, bg11))):
        for ref, which in zip(pair, (here.part, 1 - here.part)):
            mixed_grad[seq, aligned(which, half)] = mat_right(ref[...], out_w[...]).astype(low)
    plain, first = band(False, 0), band(True, has_halo)
    for seq in range(seqs):
        out_ref[seq, 0:WINDOW, 0:width] = jnp.zeros((WINDOW, width), low)
        tails = {}
        for lane in range(0, width, LANES):
            tails[lane] = (jnp.zeros((WINDOW, LANES), full), jnp.zeros((WINDOW, LANES), full))
        for top0 in range(0, rows - WINDOW, 2 * WINDOW):
            group = [(lane, top0 + w) for w in (0, WINDOW) for lane in range(0, width, LANES)]
            loaded, scores, prob_grads = [], [], []
            for lane, top in group:
                q = head_pair(qkv_ref[seq, top + WINDOW : top + 2 * WINDOW, lane : lane + LANES])
                k = qkv_ref[seq, top : top + 2 * WINDOW, width + lane : width + lane + LANES]
                v = qkv_ref[seq, top : top + 2 * WINDOW, 2 * width + lane : 2 * width + lane + LANES]
                g = head_pair(mixed_grad[seq, top : top + WINDOW, lane : lane + LANES])
                loaded.append((q, k, g))
                scores.append(mat_right(q, k))
                prob_grads.append(mat_right(g, v))
            probs = [softmax(s, plain if top else first) for s, (lane, top) in zip(scores, group)]
            score_grads = [
                (p * (pg - jnp.sum(p * pg, axis=-1, keepdims=True))).astype(low)
                for p, pg in zip(probs, prob_grads)
            ]
            for p, sg, (q, k, g), (lane, top) in zip(probs, score_grads, loaded, group):
                q_grad = unstack(mat(sg, k)) * factor
                k_grad = mat_left(sg, q) * factor
                v_grad = mat_left(p.astype(low), g)
                k_tail, v_tail = tails[lane]
                out_ref[seq, top + WINDOW : top + 2 * WINDOW, lane : lane + LANES] = q_grad.astype(low)
                at = width + lane
                out_ref[seq, top : top + WINDOW, at : at + LANES] = (k_tail + k_grad[:WINDOW]).astype(low)
                at = 2 * width + lane
                out_ref[seq, top : top + WINDOW, at : at + LANES] = (v_tail + v_grad[:WINDOW]).astype(low)
                tails[lane] = (k_grad[WINDOW:], v_grad[WINDOW:])
        for lane, (k_tail, v_tail) in tails.items():
            at = width + lane
            out_ref[seq, rows - WINDOW : rows, at : at + LANES] = k_tail.astype(low)
            at = 2 * width + lane
            out_ref[seq, rows - WINDOW : rows, at : at + LANES] = v_tail.astype(low)
    attention_role(here.part, here.role(0), first_ref, (bg00, bg01, bg10, bg11), mixed_ref, out_ref, normed_ref)


def attention_role(part, quarter, target, grads, mixed_ref, qkv_grad_ref, normed_ref):
    seqs, rows, width3 = qkv_grad_ref.shape
    block = aligned(quarter, target.shape[0])
    total = mat_left(normed_ref[0, :, block], qkv_grad_ref[0])
    total += mat_left(normed_ref[1, :, block], qkv_grad_ref[1])
    target[:, :width3] = total.astype(low)
    half = grads[0].shape[0]
    total = None
    for n, ref in enumerate(grads):
        seq, i = divmod(n, 2)
        term = mat_left(ref[:, block], mixed_ref[seq, aligned(1 - part if i else part, half)])
        total = term if total is None else total + term
    target[:, width3:] = total.astype(low)


def attention_grads_kernel(
    bg00, bg01, bg10, bg11, mixed_ref, qkv_grad_ref, normed_ref, one_ref, two_ref, own_ref
):
    here = Place()
    for n, ref in enumerate((one_ref, two_ref, own_ref)):
        attention_role(
            here.part, here.role(1 + n), ref, (bg00, bg01, bg10, bg11), mixed_ref, qkv_grad_ref, normed_ref
        )


def normed_grad_kernel(qkv_w, grad_ref, mine_ref, sib_ref):
    part = Place().part
    half = (grad_ref.shape[1] - WINDOW) // 2
    for seq, target in ((1, sib_ref), (0, mine_ref)):
        target[0:WINDOW] = mat_right(grad_ref[seq, 0:WINDOW], qkv_w[...]).astype(target.dtype)
        for i, which in enumerate((part, 1 - part)):
            at = pl.ds(pl.multiple_of(WINDOW + half * which, WINDOW), half)
            target[WINDOW + i * half : WINDOW + (i + 1) * half] = mat_right(
                grad_ref[seq, at], qkv_w[...]
            ).astype(target.dtype)


def mlp_kernel(gate_w, up_w, down_w, mid, dy, target, hidden_ref, gg_ref, ug_ref):
    gate = mat_right(mid[...], gate_w[...])
    up = mat_right(mid[...], up_w[...])
    back = mat_right(dy[...], down_w[...])
    sig = 1.0 / (1.0 + jnp.exp(-gate))
    silu = gate * sig
    hidden_ref[...] = (silu * up).astype(low)
    ug = (back * silu).astype(low)
    gg = (back * up * sig * (1.0 + gate * (1.0 - sig))).astype(low)
    ug_ref[...] = ug
    gg_ref[...] = gg
    target[...] = (mat(gg, gate_w[...]) + mat(ug, up_w[...])).astype(low)


def mlp_grads_kernel(roles, *rest):
    hiddens, ggs, ugs, mids, dys, targets = (rest[i : i + 4] for i in range(0, 24, 4))
    rows = targets[0].shape[0] // 3
    here = Place()
    for role, target in zip(roles, targets):
        block = aligned(here.role(role), target.shape[1])
        for i, (lefts, rights) in enumerate(((ggs, mids), (ugs, mids), (hiddens, dys))):
            total = None
            for left, right in zip(lefts, rights):
                term = mat_left(left[...], right[:, block])
                total = term if total is None else total + term
            target[i * rows : (i + 1) * rows] = total[:rows].astype(low)


def split_kernel(axis, total_ref, arrived_ref, keep_ref, give_ref):
    core = Place().core
    size = total_ref.shape[axis] // 2
    for which, ref in ((core, keep_ref), (1 - core, give_ref)):
        at = (slice(None),) * axis + (aligned(which, size),)
        ref[...] = (total_ref[at].astype(full) + arrived_ref[at].astype(full)).astype(low)


def choose_kernel(keep_ref, help_ref, out_ref):
    here = Place()

    @pl.when(here.resident == 1)
    def _():
        out_ref[...] = keep_ref[...]

    @pl.when(here.resident == 0)
    def _():
        out_ref[...] = help_ref[...]


def middle_kernel(gain_ref, token_ref, sum_ref, arrived_ref, middle_ref, mid_ref):
    middle = token_ref[...].astype(full) + (sum_ref[...].astype(full) + arrived_ref[...].astype(full))
    middle_ref[...] = middle
    mid_ref[...] = rms_norm(middle, gain_ref[...].astype(full)).astype(low)


def middle_grad_kernel(gain_ref, dy_ref, middle_ref, sum_ref, arrived_ref, grad_ref, low_ref, gain_part_ref):
    grad = sum_ref[...].astype(full) + arrived_ref[...].astype(full)
    pull, gain_part_ref[...] = rms_pull(middle_ref[...], gain_ref[...].astype(full), grad)
    total = dy_ref[...].astype(full) + pull
    grad_ref[...] = total
    low_ref[...] = total.astype(low)


def add_kernel(*refs):
    terms, out = refs[:-1], refs[-1]
    total = terms[0][...].astype(full)
    for term in terms[1:]:
        total = total + term[...].astype(full)
    out[...] = total.astype(out.dtype)


def mlp_out_kernel(down_w, own, own_sib, pair, pair_sib, *outs):
    for ref, out in zip((own, own_sib, pair, pair_sib), outs):
        out[...] = mat(ref[...], down_w[...]).astype(out.dtype)


def ordered_sum_kernel(which, *refs):
    terms, out, scratch = refs[:4], refs[4], refs[5]
    here = Place()
    for n, term in enumerate(terms):
        scratch[here.quarter(n % 2, n // 2) if which else (here.z + n) % 4] = term[...]
    out[...] = scratch[0] + scratch[1] + scratch[2] + scratch[3]


def output_kernel(middle_ref, mine_ref, sib_ref, pair_ref, out_ref, scratch, sem):
    total = middle_ref[...] + mine_ref[...] + sib_ref[...].astype(full) + pair_ref[...].astype(full)
    scratch[...] = total.astype(low)
    copy = pltpu.make_async_copy(scratch, out_ref, sem)
    copy.start()
    copy.wait()


def normed_sum_kernel(mine_ref, sib_ref, own_ref, halo_ref, away_ref):
    rows = own_ref.shape[0]

    def total(top, size):
        return mine_ref[top : top + size] + sib_ref[top : top + size].astype(full)

    halo = total(0, WINDOW)
    halo_ref[...] = halo
    away_ref[:WINDOW] = halo.astype(low)
    own_ref[...] = total(WINDOW, rows)
    away_ref[WINDOW:] = total(WINDOW + rows, rows).astype(low)


def halo_kernel(halo_ref, arrived_ref, out_ref):
    out_ref[...] = (halo_ref[...] + arrived_ref[:WINDOW].astype(full)).astype(low)


def input_grad_kernel(
    gain_ref, token_ref, middle_grad_ref, own_ref, arrived_ref, mlp_gain_ref, halo_ref,
    out_ref, gains_ref, scratch, sem,
):
    rows = own_ref.shape[0]
    scratch[...] = own_ref[...] + arrived_ref[WINDOW:].astype(full)
    scratch[rows - WINDOW :] = scratch[rows - WINDOW :] + halo_ref[...].astype(full)
    pull, gain = rms_pull(token_ref[...].astype(full), gain_ref[...].astype(full), scratch[...])
    gains_ref[0:1] = gain
    gains_ref[1:2] = mlp_gain_ref[...]
    scratch[...] = middle_grad_ref[...] + pull
    copy = pltpu.make_async_copy(scratch, out_ref, sem)
    copy.start()
    copy.wait()


def finish_attention(*rest):
    here = Place()
    pieces, (gq, gk, gv, go, gq_s, gk_s, gv_s, go_s, sems) = rest[:8], rest[8:]
    width = gq.shape[1]
    for n, piece in enumerate(pieces):
        block = aligned(here.block(n), LANES)
        for i, ref in enumerate((gq_s, gk_s, gv_s)):
            ref[block] = piece[:, i * width : (i + 1) * width].astype(full)
        go_s[:, block] = piece[:, 3 * width :].astype(full).T
    copies = [
        pltpu.make_async_copy(src, dst, sems.at[n])
        for n, (src, dst) in enumerate(((gq_s, gq), (gk_s, gk), (gv_s, gv), (go_s, go)))
    ]
    for copy in copies:
        copy.start()
    for copy in copies:
        copy.wait()


def finish_mlp(*rest):
    here = Place()
    pieces, (gg, gu, gd, gg_s, gu_s, gd_s, sems) = rest[:8], rest[8:]
    rows = gg.shape[0]
    copies = []
    for i, (ref, out) in enumerate(((gg_s, gg), (gu_s, gu), (gd_s, gd))):
        for n, piece in enumerate(pieces):
            ref[:, aligned(here.block(n), LANES)] = piece[i * rows : (i + 1) * rows].astype(full)
        copies.append(pltpu.make_async_copy(ref, out, sems.at[i]))
        copies[-1].start()
    for copy in copies:
        copy.wait()


def build(n_dp, n_t):
    extra = [1 << k for k in range(3, n_dp.bit_length() - 1)]

    def perm(target):
        pairs = []
        for d in range(n_dp):
            for t in range(n_t):
                to = target(d, t)
                if to is not None:
                    pairs.append((d * n_t + t, to[0] * n_t + to[1]))
        return pairs

    def sender(target):
        return functools.partial(lax.ppermute, axis_name=AXES, perm=perm(target))

    send_core = sender(lambda d, t: (d ^ 1, t))
    send_pair = sender(lambda d, t: (d, t ^ 1))
    send_far = sender(lambda d, t: (d, t ^ 2))
    send_owner = sender(lambda d, t: (d, t ^ 2) if (d & 1) != (t >> 1) else None)
    send_help = sender(lambda d, t: (d ^ 1, t) if (d & 1) == (t >> 1) else None)
    send_one = sender(lambda d, t: (d ^ (4 if d & 1 else 2), t))
    send_two = sender(lambda d, t: (d ^ (2 if d & 1 else 4), t))
    send_diagonal = sender(lambda d, t: (d ^ 6, t))
    send_back = [sender(lambda d, t, k=k: (d, (t - k) % n_t)) for k in range(1, 4)]
    send_extra = [sender(lambda d, t, bit=bit: (d ^ bit, t)) for bit in extra]

    def local(
        tokens, gain_attn, w_query, w_key, w_value, w_out, gain_mlp, w_gate, w_up, w_down, out_grad
    ):
        own_rows, depth = tokens.shape
        hidden_cols = w_gate.shape[1]
        head_cols = w_query.shape[1]
        padded = -(-hidden_cols // 256) * 256
        ext = WINDOW + 2 * own_rows
        made = {}

        def tied(name, value):
            events = tuple(made[event] for event in ORDER.get(name, ()))
            return after(value, events) if events else value

        def move(name, send, value):
            made[name] = send(tied(name, value))
            return made[name]

        def run(name, kernel, outs, args, **options):
            args = list(args)
            args[-1] = tied(name, args[-1])
            results = call(kernel, outs, args, cost=COST.get(name, 0), **options)
            made[name] = results[0]
            return results if len(results) > 1 else results[0]

        def add(name, *terms, dtype=low):
            return run(name, add_kernel, [(terms[0].shape, dtype)], terms)

        def three(name, piece):
            one = move(name + "1", send_one, piece)
            two = move(name + "2", send_two, piece)
            return [piece, one, two, move(name + "3", send_two, one)]

        def to_core(name, send, pieces):
            return [move(name + str(n), send, piece) for n, piece in enumerate(pieces)]

        def hold(array):
            return pltpu.with_memory_space_constraint(array, pltpu.HBM)

        gate_t, up_t = w_gate.T, w_up.T
        packed = call(
            pack_attention,
            [((3 * head_cols + w_out.shape[0], LANES), low)],
            tuple(hold(w) for w in (w_query, w_key, w_value, w_out)),
            scratch=[pltpu.SemaphoreType.DMA((7,))],
            anywhere=4,
        )[0]
        made["pack"] = packed
        attn = move("za", send_far, packed)
        first_tokens = after(tokens, packed)
        token_pair = move("zt", send_pair, first_tokens)
        tail = first_tokens[own_rows - WINDOW :]
        halo = move("h2", sender(lambda d_, t_: (d_, 2) if t_ == 1 else None), tail) + move(
            "h3", sender(lambda d_, t_: (d_, 3) if t_ == 1 else None), tail
        )
        token_sib = move("ct", send_core, first_tokens)
        wide_packed = call(
            pack_mlp,
            [((3 * hidden_cols, LANES), low)],
            (packed, hold(gate_t), hold(up_t), hold(w_down)),
            scratch=[pltpu.SemaphoreType.DMA((3,))],
            anywhere=4,
        )[0]
        made["packf"] = wide_packed
        wide = move("zw", send_far, wide_packed)
        dy, dy_pair = out_grad, move("zy", send_pair, out_grad)
        mine = three("a", attn)
        pieces = mine + to_core("ca", send_help, mine)
        halo_sib = move("ch", send_core, halo)
        token_pair_sib = move("cp", send_core, token_pair)
        qkv_w, out_w = run(
            "unpacka",
            unpack_attention,
            [((depth, 3 * head_cols), low), (w_out.shape, low)],
            (w_query, w_key, w_value, w_out, *pieces),
        )

        chunk, wide_chunk = ((own_rows, depth), low), ((own_rows, depth), full)
        normed, qkv, mixed, mine_own, mine_pair, sib_own, sib_pair = run(
            "attend",
            forward_kernel,
            [((2, ext, depth), low), ((2, ext, 3 * head_cols), low), ((2, 2 * own_rows, head_cols), low)]
            + [chunk] * 4,
            (gain_attn.reshape(1, depth), qkv_w, out_w, halo, tokens, token_pair,
             halo_sib, token_sib, token_pair_sib),
        )
        mlp_gain = gain_mlp.reshape(1, depth)
        sum_pair = add("sp", mine_pair, move("cqp", send_core, sib_pair))
        sum_own = add("so", mine_own, move("cqo", send_core, sib_own))
        arrived_own = move("zb0", send_pair, sum_pair)
        arrived_pair = move("zb1", send_pair, sum_own)
        wides = three("w", wide)
        dy_sib = move("cy", send_core, dy)
        dy_pair_sib = move("cyp", send_core, dy_pair)
        weights = to_core("cw", send_help, wides)
        middle_own, mid_own = run(
            "ko", middle_kernel, [wide_chunk, chunk], (mlp_gain, tokens, sum_own, arrived_own)
        )
        mid_own_sib = move("cmo", send_core, mid_own)
        gate_w, up_w, down_w = run(
            "unpackf",
            unpack_mlp,
            [((padded, depth), low)] * 3,
            (gate_t, up_t, w_down, *wides, *weights),
            scratch=[pltpu.SemaphoreType.DMA((24,))],
            anywhere=11,
        )

        def feed_forward(name, mid, dy):
            return run(
                name,
                mlp_kernel,
                [chunk] + [((own_rows, padded), low)] * 3,
                (gate_w, up_w, down_w, mid, dy),
            )

        part_sib, *tables_own_sib = feed_forward("fos", mid_own_sib, dy_sib)
        arrived = move("cfo", send_core, part_sib)
        part, *tables_own = feed_forward("fo", mid_own, dy)
        sum_own = add("fso", part, arrived)
        grad_pair = move("zm0", send_pair, sum_own)
        middle_pair, mid_pair = run(
            "kp", middle_kernel, [wide_chunk, chunk], (mlp_gain, token_pair, sum_pair, arrived_pair)
        )
        mid_pair_sib = move("cmp", send_core, mid_pair)
        part_sib, *tables_pair_sib = feed_forward("fps", mid_pair_sib, dy_pair_sib)
        arrived = move("cfp", send_core, part_sib)
        part, *tables_pair = feed_forward("fp", mid_pair, dy_pair)
        sum_pair = add("fsp", part, arrived)
        grad_own = move("zm1", send_pair, sum_pair)

        tables = [tables_own, tables_own_sib, tables_pair, tables_pair_sib]
        grad_args = [table[i] for i in range(3) for table in tables]
        grad_args += [mid_own, mid_own_sib, mid_pair, mid_pair_sib, dy, dy_sib, dy_pair, dy_pair_sib]
        quarter = ((3 * hidden_cols, depth // 4), low)
        mlp_diag = run("g0", functools.partial(mlp_grads_kernel, (0,)), [quarter], grad_args)
        mlp_far = move("f1", send_one, mlp_diag)
        mlp_one, mlp_two, mlp_own = run(
            "g1", functools.partial(mlp_grads_kernel, (1, 2, 3)), [quarter] * 3, grad_args
        )
        mlp_near = move("f2", send_one, mlp_one)
        out_own, out_own_sib, out_pair, out_pair_sib = run(
            "mo",
            mlp_out_kernel,
            [wide_chunk, chunk, chunk, chunk],
            (down_w, *[table[0] for table in tables]),
        )
        out_own_arrived = move("coo", send_core, out_own_sib)
        out_sum = add("os", out_pair, move("cop", send_core, out_pair_sib))

        gain_row = ((1, depth), full)
        _, branch_pair, _ = run(
            "mp",
            middle_grad_kernel,
            [wide_chunk, chunk, gain_row],
            (mlp_gain, dy_pair, middle_pair, sum_pair, grad_pair),
        )
        branch_pair_sib = move("cbp", send_core, branch_pair)
        middle_grad, branch_own, gain_own = run(
            "mq",
            middle_grad_kernel,
            [wide_chunk, chunk, gain_row],
            (mlp_gain, dy, middle_own, sum_own, grad_own),
        )
        branch_own_sib = move("cbo", send_core, branch_own)
        out_arrived = move("zo", send_pair, out_sum)
        mlp_two = add("fs2", mlp_two, mlp_far)
        mlp_last = move("f3", send_two, mlp_two)

        bgs = (branch_own, branch_pair, branch_own_sib, branch_pair_sib)
        quarter = ((depth // 4, 4 * head_cols), low)
        qkv_grad, diag = run(
            "bwd",
            backward_kernel,
            [((2, ext, 3 * head_cols), low), quarter],
            (*bgs, out_w, mixed, qkv, normed),
            scratch=[pltpu.VMEM((2, 2 * own_rows, head_cols), low)],
        )
        far = move("b1", send_one, diag)
        one, two, last_own = run(
            "ag", attention_grads_kernel, [quarter] * 3, (*bgs, mixed, qkv_grad, normed)
        )
        near = move("b2", send_one, one)

        def everywhere(name, total):
            for n, send in enumerate(send_extra):
                total = add(name + "e%d" % n, total, send(total), dtype=total.dtype)
            return total

        mlp_total = everywhere("fx", add("ft", mlp_own, mlp_near, mlp_last))
        mlp_arrived = move("zf", send_owner, mlp_total)
        two = add("bs2", two, far)
        last = move("b3", send_two, two)
        grad_mine, grad_sib = run(
            "nk", normed_grad_kernel, [((ext, depth), full), ((ext, depth), low)], (qkv_w, qkv_grad)
        )
        grad_own, grad_halo, grad_away = run(
            "ns",
            normed_sum_kernel,
            [wide_chunk, ((WINDOW, depth), full), ((WINDOW + own_rows, depth), low)],
            (grad_mine, move("cn", send_core, grad_sib)),
        )
        grad_arrived = move("zn", send_pair, grad_away)
        output = run(
            "out",
            output_kernel,
            [chunk + (0,)],
            (middle_own, out_own, out_own_arrived, out_arrived),
            scratch=[pltpu.VMEM(*chunk), pltpu.SemaphoreType.DMA],
        )
        total = everywhere("bx", add("bt", last_own, near, last))
        total_arrived = move("zg", send_owner, total)

        halo_sum = run("hk", halo_kernel, [((WINDOW, depth), low)], (grad_halo, grad_arrived))
        halo_grad = move("hh", sender(lambda d_, t_: (d_, 1) if t_ == 2 else None), halo_sum)
        input_grad, gains = run(
            "ik",
            input_grad_kernel,
            [wide_chunk + (0,), ((2, depth), full)],
            (gain_attn.reshape(1, depth), tokens, middle_grad, grad_own, grad_arrived, gain_own, halo_grad),
            scratch=[pltpu.VMEM(*wide_chunk), pltpu.SemaphoreType.DMA],
        )

        def sum_of_four(name, which, *terms):
            shape = terms[0].shape
            return run(
                name,
                functools.partial(ordered_sum_kernel, which),
                [(shape, full)],
                terms,
                scratch=[pltpu.VMEM((4,) + shape, full)],
            )

        gains = add("gc", gains, move("cg", send_core, gains), dtype=full)
        gains = sum_of_four(
            "gz", 0, gains, *[move("zg%d" % n, send, gains) for n, send in enumerate(send_back)]
        )
        gains = sum_of_four(
            "gx", 1, gains, move("x0", send_one, gains), move("x1", send_two, gains),
            move("x2", send_diagonal, gains),
        )
        gains = everywhere("gy", gains)

        def to_both(name, total, arrived, axis):
            shape = list(total.shape)
            shape[axis] //= 2
            half = (tuple(shape), low)
            keep, give = run(
                name + "s", functools.partial(split_kernel, axis), [half, half], (total, arrived)
            )
            return run(name + "c", choose_kernel, [half], (keep, move(name + "h", send_help, give)))

        mlp_mine = three("fa", to_both("fh", mlp_total, mlp_arrived, 1))
        mine = three("ba", to_both("bh", total, total_arrived, 0))
        mlp_pieces = mlp_mine + to_core("cfa", send_core, mlp_mine)
        shape = (hidden_cols, depth)
        grad_gate, grad_up, grad_down = run(
            "finf",
            finish_mlp,
            [(shape, full, 0)] * 3,
            mlp_pieces,
            scratch=[pltpu.VMEM(shape, full)] * 3 + [pltpu.SemaphoreType.DMA((3,))],
        )
        pieces = mine + to_core("cba", send_core, mine)
        grad_query, grad_key, grad_value, grad_out = run(
            "finb",
            finish_attention,
            [(w_query.shape, full, 0)] * 3 + [(w_out.shape, full, 0)],
            pieces,
            scratch=[pltpu.VMEM(w_query.shape, full)] * 3
            + [pltpu.VMEM(w_out.shape, full), pltpu.SemaphoreType.DMA((4,))],
        )
        return (
            output,
            input_grad,
            gains[0],
            grad_query,
            grad_key,
            grad_value,
            grad_out,
            gains[1],
            grad_gate.T,
            grad_up.T,
            grad_down,
        )

    return local


def solution(mesh):
    both = P(("dp", "tensor"), None)
    columns, rows = P(None, "tensor"), P("tensor", None)
    return jax.shard_map(
        build(mesh.shape["dp"], mesh.shape["tensor"]),
        mesh=mesh,
        in_specs=(both, P(), columns, columns, columns, rows, P(), columns, columns, rows, both),
        out_specs=(both, both, P(), columns, columns, columns, rows, P(), columns, columns, rows),
        check_vma=False,
    )
```

```python
import functools

import jax
import jax.numpy as jnp
from jax import lax
from jax.experimental import pallas as pl
from jax.experimental.pallas import tpu as pltpu
from jax.sharding import PartitionSpec as P

HEAD_DIM = 64
WINDOW = 64
LANES = 128

norm_eps = 1e-05
very_low = -1e30
AXES = ("dp", "tensor")
low = jnp.bfloat16
ORDER = {
    "unpacka": ("a3", "ca2",),
    "cfa1": ("fhs", "fhh", "bhc",),
    "zm1": ("zm0",),
    "zy": ("zt",),
    "ca2": ("zy",),
    "cn": ("zo",),
    "so": ("a1",),
    "kp": ("fo",),
    "a2": ("h2",),
    "zm0": ("unpacka",),
    "cyp": ("cqp",),
    "fps": ("unpackf",),
    "cop": ("f2",),
    "ag": ("cop", "f3", "bwd",),
    "a3": ("zt", "h3", "h4",),
    "cfa2": ("out", "ba2", "cfa0",),
    "cp": ("h3",),
    "ca3": ("pack",),
    "sp": ("a3",),
    "fos": ("unpackf",),
    "nk": ("ft",),
    "zg": ("bt",),
    "ca1": ("a1", "a3",),
    "fa2": ("fhs",),
    "zw": ("za",),
    "w1": ("a2",),
    "h3": ("za",),
    "fhc": ("cn", "fhs",),
    "y2": ("y0",),
    "cmp": ("cqp",),
    "bwd": ("kp",),
    "zb0": ("a1",),
    "cw2": ("attend",),
    "cmo": ("unpackf",),
}
COST = {
    "ko": 8,
    "unpackf": 1,
    "mo": 16,
    "g1": 16,
    "hk": 4,
    "bwd": 1,
    "kp": 1,
    "mq": 2,
    "fsp": 2,
    "fps": 1,
    "ft": 1,
    "bhs": 2,
    "fo": 1,
}
full = jnp.float32


def mat(left, right):
    return jnp.dot(left, right, preferred_element_type=full)


def mat_left(left, right):
    return lax.dot_general(left, right, (((0,), (0,)), ((), ())), preferred_element_type=full)


def mat_right(left, right):
    return lax.dot_general(left, right, (((1,), (1,)), ((), ())), preferred_element_type=full)


def rms_scale(values):
    return lax.rsqrt(jnp.mean(values * values, axis=-1, keepdims=True) + norm_eps)


def rms_norm(values, gain):
    return values * rms_scale(values) * gain


def rms_pull(values, gain, grad):
    scale = rms_scale(values)
    unit = values * scale
    scaled = grad * gain
    inner = jnp.mean(scaled * unit, axis=-1, keepdims=True)
    return scale * (scaled - unit * inner)


def after(value, event):
    return lax.optimization_barrier((value, event))[0]


def aligned(index, size):
    return pl.ds(pl.multiple_of(index * size, size), size)


class Place:
    def __init__(self):
        d, t = lax.axis_index("dp"), lax.axis_index("tensor")
        self.z, self.core, self.part, self.side = t, d & 1, t & 1, (t >> 1) & 1
        self.x, self.y = (d >> 1) & 1, (d >> 2) & 1
        self.resident = 1 - (self.core ^ self.side)

    def quarter(self, one, two, other=0):
        core = self.core ^ other
        flip_x = (1 - core) * one + core * two
        flip_y = (1 - core) * two + core * one
        return 2 * (self.y ^ flip_y) + (self.x ^ flip_x)

    def block(self, n):
        other = n // 4
        return 2 * self.quarter(n % 2, n % 4 // 2, other) + (self.core ^ other)

    def role(self, n):
        return self.quarter((1, 1, 0, 0)[n], (1, 0, 1, 0)[n])


class Later:
    def __init__(self, name, index):
        self.name, self.index = name, index


def call(kernel, outs, args, scratch=(), anywhere=0, limit=24, cost=0):
    specs = [pl.BlockSpec(memory_space=pl.ANY)] * anywhere + [
        pl.BlockSpec(memory_space=pltpu.VMEM)
    ] * (len(args) - anywhere)
    shapes = [jax.ShapeDtypeStruct(o[0], o[1]) for o in outs]
    places = [
        pl.BlockSpec(memory_space=pl.ANY if len(o) > 2 else pltpu.VMEM) for o in outs
    ]
    results = pl.pallas_call(
        kernel,
        out_shape=shapes,
        in_specs=specs,
        out_specs=places,
        scratch_shapes=list(scratch),
        compiler_params=pltpu.CompilerParams(vmem_limit_bytes=limit << 20),
        cost_estimate=pl.CostEstimate(flops=cost * 1153000000, bytes_accessed=0, transcendentals=0),
    )(*args)
    return list(results)


def pack_attention(q_ref, k_ref, v_ref, o_ref, out_ref, sems):
    block = aligned(Place().block(0), LANES)
    moves = []
    for i, ref in enumerate((q_ref, k_ref, v_ref)):
        for j in range(2):
            moves.append((ref.at[block, pl.ds(j * LANES, LANES)], (2 * i + j) * LANES, LANES))
    moves.append((o_ref.at[:, block], 6 * LANES, o_ref.shape[0]))
    copies = [
        pltpu.make_async_copy(src, out_ref.at[pl.ds(top, size)], sems.at[n])
        for n, (src, top, size) in enumerate(moves)
    ]
    for copy in copies:
        copy.start()
    for copy in copies:
        copy.wait()


def pack_mlp(_, g_ref, u_ref, d_ref, out_ref, sems):
    block = aligned(Place().block(0), LANES)
    rows = g_ref.shape[0]
    copies = [
        pltpu.make_async_copy(ref.at[:, block], out_ref.at[pl.ds(n * rows, rows)], sems.at[n])
        for n, ref in enumerate((g_ref, u_ref, d_ref))
    ]
    for copy in copies:
        copy.start()
    for copy in copies:
        copy.wait()


def unpack_attention(q_ref, k_ref, v_ref, o_ref, *rest):
    pieces, (qkv_ref, out_ref) = rest[:8], rest[8:]
    here = Place()
    width = q_ref.shape[1]

    @pl.when(here.resident == 1)
    def _():
        for i, ref in enumerate((q_ref, k_ref, v_ref)):
            qkv_ref[:, i * width : (i + 1) * width] = ref[...]
        out_ref[...] = o_ref[...]

    @pl.when(here.resident == 0)
    def _():
        for n, piece in enumerate(pieces):
            block = aligned(here.block(n), LANES)
            for j in range(3 * width // LANES):
                qkv_ref[block, j * LANES : (j + 1) * LANES] = piece[j * LANES : (j + 1) * LANES]
            out_ref[:, block] = piece[3 * width :]


def unpack_mlp(g_ref, u_ref, d_ref, *rest):
    pieces, outs, sems = rest[:8], rest[8:11], rest[11]
    here = Place()
    rows = g_ref.shape[0]

    @pl.when(here.resident == 1)
    def _():
        copies = [
            pltpu.make_async_copy(ref, out.at[pl.ds(0, rows)], sems.at[n])
            for n, (ref, out) in enumerate(zip((g_ref, u_ref, d_ref), outs))
        ]
        for copy in copies:
            copy.start()
        for out in outs:
            out[rows:] = jnp.zeros((out.shape[0] - rows, out.shape[1]), low)
        for copy in copies:
            copy.wait()

    @pl.when(here.resident == 0)
    def _():
        copies = [
            pltpu.make_async_copy(
                pieces[n].at[pl.ds(i * rows, rows)],
                out.at[pl.ds(0, rows), aligned(here.block(n), LANES)],
                sems.at[3 * n + i],
            )
            for n in range(8)
            for i, out in enumerate(outs)
        ]
        for copy in copies:
            copy.start()
        for out in outs:
            out[rows:] = jnp.zeros((out.shape[0] - rows, out.shape[1]), low)
        for copy in copies:
            copy.wait()


def head_pair(rows):
    lane = lax.broadcasted_iota(jnp.int32, rows.shape, 1)
    zero = jnp.zeros_like(rows)
    return jnp.concatenate(
        [jnp.where(lane < HEAD_DIM, rows, zero), jnp.where(lane < HEAD_DIM, zero, rows)], axis=0
    )


def unstack(stacked):
    half = stacked.shape[0] // 2
    lane = lax.broadcasted_iota(jnp.int32, (half, stacked.shape[1]), 1)
    return jnp.where(lane < HEAD_DIM, stacked[:half], stacked[half:])


def band(first, has_halo):
    shape = (2 * WINDOW, 2 * WINDOW)
    row = lax.broadcasted_iota(jnp.int32, shape, 0) % WINDOW
    col = lax.broadcasted_iota(jnp.int32, shape, 1)
    mask = (col > row) & (col <= row + WINDOW)
    if first:
        mask = mask & ((col >= WINDOW) | (has_halo > 0))
    return mask


def softmax(scores, mask):
    scores = jnp.where(mask, scores * HEAD_DIM ** (-0.5), very_low)
    expo = jnp.exp(scores - jnp.max(scores, axis=-1, keepdims=True))
    return expo * (1.0 / jnp.sum(expo, axis=-1, keepdims=True))


def place(ref, seq, part, halo, own, pair, change):
    rows = own.shape[0]
    ref[seq, 0:WINDOW] = change(halo[...])
    ref[seq, pl.ds(pl.multiple_of(WINDOW + rows * part, WINDOW), rows)] = change(own[...])
    ref[seq, pl.ds(pl.multiple_of(WINDOW + rows * (1 - part), WINDOW), rows)] = change(pair[...])


def forward_kernel(
    gain_ref, qkv_w, out_w, halo0, own0, pair0, halo1, own1, pair1,
    normed_ref, qkv_ref, mixed_ref, mine_own, mine_pair, sib_own, sib_pair,
):
    here = Place()
    part, has_halo = here.part, here.side
    gain = gain_ref[...].astype(full)

    def norm(rows):
        return rms_norm(rows.astype(full), gain).astype(low)

    place(normed_ref, 0, part, halo0, own0, pair0, norm)
    place(normed_ref, 1, part, halo1, own1, pair1, norm)
    seqs, rows, width3 = qkv_ref.shape
    width = width3 // 3
    for seq in (1, 0):
        qkv_ref[seq] = mat(normed_ref[seq], qkv_w[...]).astype(low)
    plain, first = band(False, 0), band(True, has_halo)
    units = [(lane, top) for top in range(0, rows - WINDOW, WINDOW) for lane in range(0, width, LANES)]
    for seq in (1, 0):
        for start in range(0, len(units), 4):
            group = units[start : start + 4]
            scores = []
            for lane, top in group:
                q = qkv_ref[seq, top + WINDOW : top + 2 * WINDOW, lane : lane + LANES]
                k = qkv_ref[seq, top : top + 2 * WINDOW, width + lane : width + lane + LANES]
                scores.append(mat_right(head_pair(q), k))
            probs = [
                softmax(s, plain if top else first).astype(low)
                for s, (lane, top) in zip(scores, group)
            ]
            for p, (lane, top) in zip(probs, group):
                at = 2 * width + lane
                v = qkv_ref[seq, top : top + 2 * WINDOW, at : at + LANES]
                mixed_ref[seq, top : top + WINDOW, lane : lane + LANES] = unstack(mat(p, v)).astype(low)
        half = (rows - WINDOW) // 2
        for target, which in ((sib_own if seq else mine_own, part), (sib_pair if seq else mine_pair, 1 - part)):
            target[...] = mat(mixed_ref[seq, aligned(which, half)], out_w[...]).astype(low)


def backward_kernel(
    bg00, bg01, bg10, bg11, out_w, mixed_ref, qkv_ref, normed_ref,
    out_ref, first_ref, mixed_grad,
):
    here = Place()
    has_halo = here.side
    seqs, rows, width3 = qkv_ref.shape
    width = width3 // 3
    factor = HEAD_DIM ** (-0.5)
    half = bg00.shape[0]
    for seq, pair in enumerate(((bg00, bg01), (bg10, bg11))):
        for ref, which in zip(pair, (here.part, 1 - here.part)):
            mixed_grad[seq, aligned(which, half)] = mat_right(ref[...], out_w[...]).astype(low)
    plain, first = band(False, 0), band(True, has_halo)
    for seq in range(seqs):
        out_ref[seq, 0:WINDOW, 0:width] = jnp.zeros((WINDOW, width), low)
        tails = {}
        for lane in range(0, width, LANES):
            tails[lane] = (jnp.zeros((WINDOW, LANES), full), jnp.zeros((WINDOW, LANES), full))
        for top0 in range(0, rows - WINDOW, 2 * WINDOW):
            group = [(lane, top0 + w) for w in (0, WINDOW) for lane in range(0, width, LANES)]
            loaded, scores, prob_grads = [], [], []
            for lane, top in group:
                q = head_pair(qkv_ref[seq, top + WINDOW : top + 2 * WINDOW, lane : lane + LANES])
                k = qkv_ref[seq, top : top + 2 * WINDOW, width + lane : width + lane + LANES]
                v = qkv_ref[seq, top : top + 2 * WINDOW, 2 * width + lane : 2 * width + lane + LANES]
                g = head_pair(mixed_grad[seq, top : top + WINDOW, lane : lane + LANES])
                loaded.append((q, k, g))
                scores.append(mat_right(q, k))
                prob_grads.append(mat_right(g, v))
            probs = [softmax(s, plain if top else first) for s, (lane, top) in zip(scores, group)]
            score_grads = [
                (p * (pg - jnp.sum(p * pg, axis=-1, keepdims=True))).astype(low)
                for p, pg in zip(probs, prob_grads)
            ]
            for p, sg, (q, k, g), (lane, top) in zip(probs, score_grads, loaded, group):
                q_grad = unstack(mat(sg, k)) * factor
                k_grad = mat_left(sg, q) * factor
                v_grad = mat_left(p.astype(low), g)
                k_tail, v_tail = tails[lane]
                out_ref[seq, top + WINDOW : top + 2 * WINDOW, lane : lane + LANES] = q_grad.astype(low)
                at = width + lane
                out_ref[seq, top : top + WINDOW, at : at + LANES] = (k_tail + k_grad[:WINDOW]).astype(low)
                at = 2 * width + lane
                out_ref[seq, top : top + WINDOW, at : at + LANES] = (v_tail + v_grad[:WINDOW]).astype(low)
                tails[lane] = (k_grad[WINDOW:], v_grad[WINDOW:])
        for lane, (k_tail, v_tail) in tails.items():
            at = width + lane
            out_ref[seq, rows - WINDOW : rows, at : at + LANES] = k_tail.astype(low)
            at = 2 * width + lane
            out_ref[seq, rows - WINDOW : rows, at : at + LANES] = v_tail.astype(low)
    attention_role(here.part, here.role(0), first_ref, (bg00, bg01, bg10, bg11), mixed_ref, out_ref, normed_ref)


def attention_role(part, quarter, target, grads, mixed_ref, qkv_grad_ref, normed_ref):
    seqs, rows, width3 = qkv_grad_ref.shape
    block = aligned(quarter, target.shape[0])
    total = mat_left(normed_ref[0, :, block], qkv_grad_ref[0])
    total += mat_left(normed_ref[1, :, block], qkv_grad_ref[1])
    target[:, :width3] = total.astype(low)
    half = grads[0].shape[0]
    total = None
    for n, ref in enumerate(grads):
        seq, i = divmod(n, 2)
        term = mat_left(ref[:, block], mixed_ref[seq, aligned(1 - part if i else part, half)])
        total = term if total is None else total + term
    target[:, width3:] = total.astype(low)


def attention_grads_kernel(
    bg00, bg01, bg10, bg11, mixed_ref, qkv_grad_ref, normed_ref, one_ref, two_ref, own_ref
):
    here = Place()
    for n, ref in enumerate((one_ref, two_ref, own_ref)):
        attention_role(
            here.part, here.role(1 + n), ref, (bg00, bg01, bg10, bg11), mixed_ref, qkv_grad_ref, normed_ref
        )


def normed_grad_kernel(qkv_w, grad_ref, mine_ref, sib_ref):
    part = Place().part
    half = (grad_ref.shape[1] - WINDOW) // 2
    for seq, target in ((1, sib_ref), (0, mine_ref)):
        target[0:WINDOW] = mat_right(grad_ref[seq, 0:WINDOW], qkv_w[...]).astype(target.dtype)
        for i, which in enumerate((part, 1 - part)):
            at = pl.ds(pl.multiple_of(WINDOW + half * which, WINDOW), half)
            target[WINDOW + i * half : WINDOW + (i + 1) * half] = mat_right(
                grad_ref[seq, at], qkv_w[...]
            ).astype(target.dtype)


def mlp_kernel(gate_w, up_w, down_w, mid, dy, target, hidden_ref, gg_ref, ug_ref):
    gate = mat_right(mid[...], gate_w[...])
    up = mat_right(mid[...], up_w[...])
    back = mat_right(dy[...], down_w[...])
    sig = 1.0 / (1.0 + jnp.exp(-gate))
    silu = gate * sig
    hidden_ref[...] = (silu * up).astype(low)
    ug = (back * silu).astype(low)
    gg = (back * up * sig * (1.0 + gate * (1.0 - sig))).astype(low)
    ug_ref[...] = ug
    gg_ref[...] = gg
    target[...] = (mat(gg, gate_w[...]) + mat(ug, up_w[...])).astype(low)


def mlp_grads_kernel(roles, *rest):
    hiddens, ggs, ugs, mids, dys, targets = (rest[i : i + 4] for i in range(0, 24, 4))
    rows = targets[0].shape[0] // 3
    here = Place()
    for role, target in zip(roles, targets):
        block = aligned(here.role(role), target.shape[1])
        for i, (lefts, rights) in enumerate(((ggs, mids), (ugs, mids), (hiddens, dys))):
            total = None
            for left, right in zip(lefts, rights):
                term = mat_left(left[...], right[:, block])
                total = term if total is None else total + term
            target[i * rows : (i + 1) * rows] = total[:rows].astype(low)


def split_kernel(axis, total_ref, arrived_ref, keep_ref, give_ref):
    core = Place().core
    size = total_ref.shape[axis] // 2
    for which, ref in ((core, keep_ref), (1 - core, give_ref)):
        at = (slice(None),) * axis + (aligned(which, size),)
        ref[...] = (total_ref[at].astype(full) + arrived_ref[at].astype(full)).astype(low)


def choose_kernel(keep_ref, help_ref, out_ref):
    here = Place()

    @pl.when(here.resident == 1)
    def _():
        out_ref[...] = keep_ref[...]

    @pl.when(here.resident == 0)
    def _():
        out_ref[...] = help_ref[...]


def middle_kernel(gain_ref, token_ref, sum_ref, arrived_ref, middle_ref, mid_ref):
    middle = token_ref[...].astype(full) + (sum_ref[...].astype(full) + arrived_ref[...].astype(full))
    middle_ref[...] = middle
    mid_ref[...] = rms_norm(middle, gain_ref[...].astype(full)).astype(low)


def middle_grad_kernel(gain_ref, dy_ref, middle_ref, sum_ref, arrived_ref, grad_ref, low_ref):
    grad = sum_ref[...].astype(full) + arrived_ref[...].astype(full)
    pull = rms_pull(middle_ref[...], gain_ref[...].astype(full), grad)
    total = dy_ref[...].astype(full) + pull
    grad_ref[...] = total
    low_ref[...] = total.astype(low)


def add_kernel(*refs):
    terms, out = refs[:-1], refs[-1]
    total = terms[0][...].astype(full)
    for term in terms[1:]:
        total = total + term[...].astype(full)
    out[...] = total.astype(out.dtype)


def mlp_out_kernel(down_w, own, own_sib, pair, pair_sib, *outs):
    for ref, out in zip((own, own_sib, pair, pair_sib), outs):
        out[...] = mat(ref[...], down_w[...]).astype(out.dtype)


def ordered_sum_kernel(*refs):
    terms, out, scratch = refs[:-2], refs[-2], refs[-1]
    here = Place()
    for n, term in enumerate(terms):
        scratch[here.z ^ n] = term[...]
    total = scratch[0]
    for n in range(1, len(terms)):
        total = total + scratch[n]
    out[...] = total


def output_kernel(middle_ref, mine_ref, sib_ref, pair_ref, out_ref, scratch, sem):
    total = middle_ref[...] + mine_ref[...] + sib_ref[...].astype(full) + pair_ref[...].astype(full)
    scratch[...] = total.astype(low)
    copy = pltpu.make_async_copy(scratch, out_ref, sem)
    copy.start()
    copy.wait()


def normed_sum_kernel(mine_ref, sib_ref, own_ref, halo_ref, away_ref):
    rows = own_ref.shape[0]

    def total(top, size):
        return mine_ref[top : top + size] + sib_ref[top : top + size].astype(full)

    halo = total(0, WINDOW)
    halo_ref[...] = halo
    away_ref[:WINDOW] = halo.astype(low)
    own_ref[...] = total(WINDOW, rows)
    away_ref[WINDOW:] = total(WINDOW + rows, rows).astype(low)


def halo_kernel(halo_ref, arrived_ref, out_ref):
    out_ref[...] = (halo_ref[...] + arrived_ref[:WINDOW].astype(full)).astype(low)


def input_grad_kernel(
    gain_ref, token_ref, middle_grad_ref, own_ref, arrived_ref, halo_ref, out_ref, scratch, sem
):
    rows = own_ref.shape[0]
    scratch[...] = own_ref[...] + arrived_ref[WINDOW:].astype(full)
    scratch[rows - WINDOW :] = scratch[rows - WINDOW :] + halo_ref[...].astype(full)
    pull = rms_pull(token_ref[...].astype(full), gain_ref[...].astype(full), scratch[...])
    scratch[...] = middle_grad_ref[...] + pull
    copy = pltpu.make_async_copy(scratch, out_ref, sem)
    copy.start()
    copy.wait()


def finish_attention(gain_ref, mlp_part_ref, q_ref, k_ref, v_ref, *rest):
    pieces, (gq, gk, gv, go, part, gq_s, gk_s, gv_s, go_s, sems) = rest[:8], rest[8:]
    width = gq.shape[1]
    here = Place()
    part[1:2] = mlp_part_ref[...]
    for n, piece in enumerate(pieces):
        block = aligned(here.block(n), LANES)
        sums = None
        for i, (ref, weight) in enumerate(((gq_s, q_ref), (gk_s, k_ref), (gv_s, v_ref))):
            grad = piece[:, i * width : (i + 1) * width].astype(full)
            ref[block] = grad
            term = jnp.sum(grad * weight[block].astype(full), axis=1, keepdims=True)
            sums = term if sums is None else sums + term
        go_s[:, block] = piece[:, 3 * width :].astype(full).T
        row = jnp.broadcast_to(sums, (LANES, LANES)).T[0:1]
        part[0:1, block] = row / gain_ref[:, block].astype(full)
    copies = [
        pltpu.make_async_copy(src, dst, sems.at[n])
        for n, (src, dst) in enumerate(((gq_s, gq), (gk_s, gk), (gv_s, gv), (go_s, go)))
    ]
    for copy in copies:
        copy.start()
    for copy in copies:
        copy.wait()


def finish_mlp(gain_ref, g_ref, u_ref, *rest):
    pieces, (gg, gu, gd, part, gg_s, gu_s, gd_s, sems) = rest[:8], rest[8:]
    rows = gg.shape[0]
    here = Place()
    copies, sums = [], 0.0
    for i, (ref, out, weight) in enumerate(((gg_s, gg, g_ref), (gu_s, gu, u_ref), (gd_s, gd, None))):
        for n, piece in enumerate(pieces):
            ref[:, aligned(here.block(n), LANES)] = piece[i * rows : (i + 1) * rows].astype(full)
        copies.append(pltpu.make_async_copy(ref, out, sems.at[i]))
        copies[-1].start()
        if weight is not None:
            sums = sums + jnp.sum(ref[...] * weight[...].astype(full), axis=0, keepdims=True)
    part[...] = sums / gain_ref[...].astype(full)
    for copy in copies:
        copy.wait()


def build(n_dp, n_t):
    extra = [1 << k for k in range(3, n_dp.bit_length() - 1)]

    def perm(target):
        pairs = []
        for d in range(n_dp):
            for t in range(n_t):
                to = target(d, t)
                if to is not None:
                    pairs.append((d * n_t + t, to[0] * n_t + to[1]))
        return pairs

    def sender(target):
        return functools.partial(lax.ppermute, axis_name=AXES, perm=perm(target))

    send_core = sender(lambda d, t: (d ^ 1, t))
    send_pair = sender(lambda d, t: (d, t ^ 1))
    send_far = sender(lambda d, t: (d, t ^ 2))
    send_owner = sender(lambda d, t: (d, t ^ 2) if (d & 1) != (t >> 1) else None)
    send_help = send_core
    send_one = sender(lambda d, t: (d ^ (4 if d & 1 else 2), t))
    send_two = sender(lambda d, t: (d ^ (2 if d & 1 else 4), t))
    send_cross = [sender(lambda d, t, k=k: (d, t ^ k)) for k in range(1, n_t)]
    send_extra = [sender(lambda d, t, bit=bit: (d ^ bit, t)) for bit in extra]

    def local(
        tokens, gain_attn, w_query, w_key, w_value, w_out, gain_mlp, w_gate, w_up, w_down, out_grad
    ):
        own_rows, depth = tokens.shape
        hidden_cols = w_gate.shape[1]
        head_cols = w_query.shape[1]
        padded = -(-hidden_cols // 256) * 256
        ext = WINDOW + 2 * own_rows
        plans, made = {}, {}

        def value(item):
            return emit(item.name)[item.index] if isinstance(item, Later) else item

        def emit(name):
            if name not in made:
                function, args = plans[name]
                args = [value(arg) for arg in args]
                events = tuple(emit(event)[0] for event in ORDER.get(name, ()))
                if events:
                    args[-1] = after(args[-1], events)
                made[name] = function(*args)
            return made[name]

        def move(name, send, item):
            plans[name] = (lambda array: (send(array),)), [item]
            return Later(name, 0)

        def run(name, kernel, outs, args, **options):
            plans[name] = (
                lambda *arrays: tuple(call(kernel, outs, arrays, cost=COST.get(name, 0), **options))
            ), list(args)
            results = [Later(name, n) for n in range(len(outs))]
            return results if len(results) > 1 else results[0]

        def add(name, shape, *terms, dtype=low):
            return run(name, add_kernel, [(shape, dtype)], terms)

        chunk, wide_chunk = ((own_rows, depth), low), ((own_rows, depth), full)

        def three(name, piece):
            one = move(name + "1", send_one, piece)
            two = move(name + "2", send_two, piece)
            return [piece, one, two, move(name + "3", send_two, one)]

        def to_core(name, send, pieces):
            return [move(name + str(n), send, piece) for n, piece in enumerate(pieces)]

        def hold(array):
            return pltpu.with_memory_space_constraint(array, pltpu.HBM)

        gate_t, up_t = w_gate.T, w_up.T
        packed = call(
            pack_attention,
            [((3 * head_cols + w_out.shape[0], LANES), low)],
            tuple(hold(w) for w in (w_query, w_key, w_value, w_out)),
            scratch=[pltpu.SemaphoreType.DMA((7,))],
            anywhere=4,
        )[0]
        made["pack"] = (packed,)
        attn = move("za", send_far, packed)
        first_tokens = after(tokens, packed)
        token_pair = move("zt", send_pair, first_tokens)
        tail = first_tokens[own_rows - WINDOW :]
        halo = add(
            "h4",
            tail.shape,
            move("h2", sender(lambda d_, t_: (d_, 2) if t_ == 1 else None), tail),
            move("h3", sender(lambda d_, t_: (d_, 3) if t_ == 1 else None), tail),
        )
        token_sib = move("ct", send_core, first_tokens)
        wide_packed = call(
            pack_mlp,
            [((3 * hidden_cols, LANES), low)],
            (packed, hold(gate_t), hold(up_t), hold(w_down)),
            scratch=[pltpu.SemaphoreType.DMA((3,))],
            anywhere=4,
        )[0]
        made["packf"] = (wide_packed,)
        wide = move("zw", send_far, wide_packed)
        dy, dy_pair = out_grad, move("zy", send_pair, out_grad)
        mine = three("a", attn)
        pieces = mine + to_core("ca", send_help, mine)
        halo_sib = move("ch", send_core, halo)
        token_pair_sib = move("cp", send_core, token_pair)
        qkv_w, out_w = run(
            "unpacka",
            unpack_attention,
            [((depth, 3 * head_cols), low), (w_out.shape, low)],
            (w_query, w_key, w_value, w_out, *pieces),
        )

        normed, qkv, mixed, mine_own, mine_pair, sib_own, sib_pair = run(
            "attend",
            forward_kernel,
            [((2, ext, depth), low), ((2, ext, 3 * head_cols), low), ((2, 2 * own_rows, head_cols), low)]
            + [chunk] * 4,
            (gain_attn.reshape(1, depth), qkv_w, out_w, halo, tokens, token_pair,
             halo_sib, token_sib, token_pair_sib),
        )
        mlp_gain = gain_mlp.reshape(1, depth)
        sum_pair = add("sp", chunk[0], mine_pair, move("cqp", send_core, sib_pair))
        sum_own = add("so", chunk[0], mine_own, move("cqo", send_core, sib_own))
        arrived_own = move("zb0", send_pair, sum_pair)
        arrived_pair = move("zb1", send_pair, sum_own)
        wides = three("w", wide)
        dy_sib = move("cy", send_core, dy)
        dy_pair_sib = move("cyp", send_core, dy_pair)
        weights = to_core("cw", send_help, wides)
        middle_own, mid_own = run(
            "ko", middle_kernel, [wide_chunk, chunk], (mlp_gain, tokens, sum_own, arrived_own)
        )
        mid_own_sib = move("cmo", send_core, mid_own)
        gate_w, up_w, down_w = run(
            "unpackf",
            unpack_mlp,
            [((padded, depth), low)] * 3,
            (gate_t, up_t, w_down, *wides, *weights),
            scratch=[pltpu.SemaphoreType.DMA((24,))],
            anywhere=11,
        )

        def feed_forward(name, mid, dy):
            return run(
                name,
                mlp_kernel,
                [chunk] + [((own_rows, padded), low)] * 3,
                (gate_w, up_w, down_w, mid, dy),
            )

        part_sib, *tables_own_sib = feed_forward("fos", mid_own_sib, dy_sib)
        arrived = move("cfo", send_core, part_sib)
        part, *tables_own = feed_forward("fo", mid_own, dy)
        sum_own = add("fso", chunk[0], part, arrived)
        grad_pair = move("zm0", send_pair, sum_own)
        middle_pair, mid_pair = run(
            "kp", middle_kernel, [wide_chunk, chunk], (mlp_gain, token_pair, sum_pair, arrived_pair)
        )
        mid_pair_sib = move("cmp", send_core, mid_pair)
        part_sib, *tables_pair_sib = feed_forward("fps", mid_pair_sib, dy_pair_sib)
        arrived = move("cfp", send_core, part_sib)
        part, *tables_pair = feed_forward("fp", mid_pair, dy_pair)
        sum_pair = add("fsp", chunk[0], part, arrived)
        grad_own = move("zm1", send_pair, sum_pair)

        tables = [tables_own, tables_own_sib, tables_pair, tables_pair_sib]
        grad_args = [table[i] for i in range(3) for table in tables]
        grad_args += [mid_own, mid_own_sib, mid_pair, mid_pair_sib, dy, dy_sib, dy_pair, dy_pair_sib]
        quarter = ((3 * hidden_cols, depth // 4), low)
        mlp_diag = run("g0", functools.partial(mlp_grads_kernel, (0,)), [quarter], grad_args)
        mlp_far = move("f1", send_one, mlp_diag)
        mlp_one, mlp_two, mlp_own = run(
            "g1", functools.partial(mlp_grads_kernel, (1, 2, 3)), [quarter] * 3, grad_args
        )
        mlp_near = move("f2", send_one, mlp_one)
        out_own, out_own_sib, out_pair, out_pair_sib = run(
            "mo",
            mlp_out_kernel,
            [wide_chunk, chunk, chunk, chunk],
            (down_w, *[table[0] for table in tables]),
        )
        out_own_arrived = move("coo", send_core, out_own_sib)
        out_sum = add("os", chunk[0], out_pair, move("cop", send_core, out_pair_sib))

        _, branch_pair = run(
            "mp",
            middle_grad_kernel,
            [wide_chunk, chunk],
            (mlp_gain, dy_pair, middle_pair, sum_pair, grad_pair),
        )
        branch_pair_sib = move("cbp", send_core, branch_pair)
        middle_grad, branch_own = run(
            "mq",
            middle_grad_kernel,
            [wide_chunk, chunk],
            (mlp_gain, dy, middle_own, sum_own, grad_own),
        )
        branch_own_sib = move("cbo", send_core, branch_own)
        out_arrived = move("zo", send_pair, out_sum)
        mlp_two = add("fs2", quarter[0], mlp_two, mlp_far)
        mlp_last = move("f3", send_two, mlp_two)

        bgs = (branch_own, branch_pair, branch_own_sib, branch_pair_sib)
        quarter = ((depth // 4, 4 * head_cols), low)
        qkv_grad, diag = run(
            "bwd",
            backward_kernel,
            [((2, ext, 3 * head_cols), low), quarter],
            (*bgs, out_w, mixed, qkv, normed),
            scratch=[pltpu.VMEM((2, 2 * own_rows, head_cols), low)],
        )
        far = move("b1", send_one, diag)
        one, two, last_own = run(
            "ag", attention_grads_kernel, [quarter] * 3, (*bgs, mixed, qkv_grad, normed)
        )
        near = move("b2", send_one, one)

        def everywhere(name, shape, total, dtype=low):
            for n, send in enumerate(send_extra):
                total = add(name + "a%d" % n, shape, total, move(name + "e%d" % n, send, total), dtype=dtype)
            return total

        mlp_shape = (3 * hidden_cols, depth // 4)
        mlp_total = everywhere("fx", mlp_shape, add("ft", mlp_shape, mlp_own, mlp_near, mlp_last))
        mlp_arrived = move("zf", send_owner, mlp_total)
        two = add("bs2", quarter[0], two, far)
        last = move("b3", send_two, two)
        grad_mine, grad_sib = run(
            "nk", normed_grad_kernel, [((ext, depth), full), ((ext, depth), low)], (qkv_w, qkv_grad)
        )
        grad_own, grad_halo, grad_away = run(
            "ns",
            normed_sum_kernel,
            [wide_chunk, ((WINDOW, depth), full), ((WINDOW + own_rows, depth), low)],
            (grad_mine, move("cn", send_core, grad_sib)),
        )
        grad_arrived = move("zn", send_pair, grad_away)
        output = run(
            "out",
            output_kernel,
            [chunk + (0,)],
            (middle_own, out_own, out_own_arrived, out_arrived),
            scratch=[pltpu.VMEM(*chunk), pltpu.SemaphoreType.DMA],
        )
        total = everywhere("bx", quarter[0], add("bt", quarter[0], last_own, near, last))
        total_arrived = move("zg", send_owner, total)

        def to_both(name, shape, total, arrived, axis):
            shape = list(shape)
            shape[axis] //= 2
            half = (tuple(shape), low)
            keep, give = run(
                name + "s", functools.partial(split_kernel, axis), [half, half], (total, arrived)
            )
            return run(name + "c", choose_kernel, [half], (keep, move(name + "h", send_help, give)))

        mlp_mine = three("fa", to_both("fh", mlp_shape, mlp_total, mlp_arrived, 1))
        mine = three("ba", to_both("bh", quarter[0], total, total_arrived, 0))
        halo_sum = run("hk", halo_kernel, [((WINDOW, depth), low)], (grad_halo, grad_arrived))
        halo_grad = move("hh", sender(lambda d_, t_: (d_, 1) if t_ == 2 else None), halo_sum)
        input_grad = run(
            "ik",
            input_grad_kernel,
            [wide_chunk + (0,)],
            (gain_attn.reshape(1, depth), tokens, middle_grad, grad_own, grad_arrived, halo_grad),
            scratch=[pltpu.VMEM(*wide_chunk), pltpu.SemaphoreType.DMA],
        )
        mlp_pieces = mlp_mine + to_core("cfa", send_core, mlp_mine)
        shape = (hidden_cols, depth)
        part_row = ((1, depth), full)
        grad_gate, grad_up, grad_down, mlp_part = run(
            "finf",
            finish_mlp,
            [(shape, full, 0)] * 3 + [part_row],
            (mlp_gain, gate_t, up_t, *mlp_pieces),
            scratch=[pltpu.VMEM(shape, full)] * 3 + [pltpu.SemaphoreType.DMA((3,))],
        )
        pieces = mine + to_core("cba", send_core, mine)
        gain_shape = (2, depth)
        grad_query, grad_key, grad_value, grad_out, part = run(
            "finb",
            finish_attention,
            [(w_query.shape, full, 0)] * 3 + [(w_out.shape, full, 0), (gain_shape, full)],
            (gain_attn.reshape(1, depth), mlp_part, w_query, w_key, w_value, *pieces),
            scratch=[pltpu.VMEM(w_query.shape, full)] * 3
            + [pltpu.VMEM(w_out.shape, full), pltpu.SemaphoreType.DMA((4,))],
        )
        gains = run(
            "gz",
            ordered_sum_kernel,
            [(gain_shape, full)],
            (part, *[move("y%d" % n, send, part) for n, send in enumerate(send_cross)]),
            scratch=[pltpu.VMEM((n_t,) + gain_shape, full)],
        )
        for name in plans:
            emit(name)
        gains = value(gains)
        return (
            value(output),
            value(input_grad),
            gains[0],
            value(grad_query),
            value(grad_key),
            value(grad_value),
            value(grad_out),
            gains[1],
            value(grad_gate).T,
            value(grad_up).T,
            value(grad_down),
        )

    return local


def solution(mesh):
    both = P(("dp", "tensor"), None)
    columns, rows = P(None, "tensor"), P("tensor", None)
    return jax.shard_map(
        build(mesh.shape["dp"], mesh.shape["tensor"]),
        mesh=mesh,
        in_specs=(both, P(), columns, columns, columns, rows, P(), columns, columns, rows, both),
        out_specs=(both, both, P(), columns, columns, columns, rows, P(), columns, columns, rows),
        check_vma=False,
    )
```

```python
import functools

import jax
import jax.numpy as jnp
from jax import lax
from jax.experimental import pallas as pl
from jax.experimental.pallas import tpu as pltpu
from jax.sharding import PartitionSpec as P

HEAD_DIM = 64
WINDOW = 64
LANES = 128

norm_eps = 1e-05
very_low = -1e30
AXES = ("dp", "tensor")
low = jnp.bfloat16
ORDER = {
    "unpacka": ("a3", "ch",),
    "cfa1": ("fhh", "bhc",),
    "ca2": ("zy",),
    "so": ("a1",),
    "kp": ("ch", "fo",),
    "a2": ("h2",),
    "zm": ("unpacka",),
    "cyp": ("cqp",),
    "fps": ("unpackf",),
    "cop": ("g1", "f2", "coo",),
    "ag": ("cop", "f3", "bwd",),
    "a3": ("zt", "h3", "packf",),
    "cfa2": ("ba2", "cfa0",),
    "ca3": ("pack",),
    "fos": ("unpackf",),
    "nk": ("bwd", "ft",),
    "cw0": ("w3",),
    "zg": ("cn", "bt",),
    "ca1": ("a1", "a3",),
    "zw": ("za",),
    "fhc": ("cn",),
    "cmp": ("cqp",),
    "bwd": ("kp",),
    "bs2": ("cbo",),
    "zn": ("cn",),
    "fa2": ("b1",),
    "cfo": ("fps",),
    "ch": ("pack",),
    "ba1": ("bhc",),
    "cfp": ("cfo",),
    "packf": ("h2",),
    "ik": ("bhc",),
    "hk": ("cba3",),
    "h3": ("pack",),
    "zy": ("pack",),
    "finf": ("zg",),
}
COST = {
    "ko": 8,
    "mo": 16,
    "g1": 2,
    "hk": 4,
    "bwd": 8,
    "kp": 16,
    "mq": 8,
    "fs": 2,
    "fps": 2,
    "ft": 1,
    "bhs": 2,
    "fo": 2,
    "fhs": 16,
    "so": 2,
    "nk": 1,
    "fos": 16,
    "fs2": 8,
    "finb": 1,
    "bt": 4,
    "g0": 16,
}
full = jnp.float32


def mat(left, right):
    return jnp.dot(left, right, preferred_element_type=full)


def mat_left(left, right):
    return lax.dot_general(left, right, (((0,), (0,)), ((), ())), preferred_element_type=full)


def mat_right(left, right):
    return lax.dot_general(left, right, (((1,), (1,)), ((), ())), preferred_element_type=full)


def rms_scale(values):
    return lax.rsqrt(jnp.mean(values * values, axis=-1, keepdims=True) + norm_eps)


def rms_norm(values, gain):
    return values * rms_scale(values) * gain


def rms_pull(values, gain, grad):
    scale = rms_scale(values)
    unit = values * scale
    scaled = grad * gain
    inner = jnp.mean(scaled * unit, axis=-1, keepdims=True)
    return scale * (scaled - unit * inner)


def after(value, event):
    return lax.optimization_barrier((value, event))[0]


def aligned(index, size):
    return pl.ds(pl.multiple_of(index * size, size), size)


class Place:
    def __init__(self):
        d, t = lax.axis_index("dp"), lax.axis_index("tensor")
        self.z, self.core, self.part, self.side = t, d & 1, t & 1, (t >> 1) & 1
        self.x, self.y = (d >> 1) & 1, (d >> 2) & 1
        self.resident = 1 - (self.core ^ self.side)

    def quarter(self, one, two, other=0):
        core = self.core ^ other
        flip_x = (1 - core) * one + core * two
        flip_y = (1 - core) * two + core * one
        return 2 * (self.y ^ flip_y) + (self.x ^ flip_x)

    def block(self, n):
        other = n // 4
        return 2 * self.quarter(n % 2, n % 4 // 2, other) + (self.core ^ other)

    def role(self, n):
        return self.quarter((1, 1, 0, 0)[n], (1, 0, 1, 0)[n])


class Later:
    def __init__(self, name, index):
        self.name, self.index = name, index


def call(kernel, outs, args, scratch=(), anywhere=0, limit=24, cost=0):
    specs = [pl.BlockSpec(memory_space=pl.ANY)] * anywhere + [
        pl.BlockSpec(memory_space=pltpu.VMEM)
    ] * (len(args) - anywhere)
    shapes = [jax.ShapeDtypeStruct(o[0], o[1]) for o in outs]
    places = [
        pl.BlockSpec(memory_space=pl.ANY if len(o) > 2 else pltpu.VMEM) for o in outs
    ]
    results = pl.pallas_call(
        kernel,
        out_shape=shapes,
        in_specs=specs,
        out_specs=places,
        scratch_shapes=list(scratch),
        compiler_params=pltpu.CompilerParams(vmem_limit_bytes=limit << 20),
        cost_estimate=pl.CostEstimate(flops=cost * 1153000000, bytes_accessed=0, transcendentals=0),
    )(*args)
    return list(results)


def pack_attention(q_ref, k_ref, v_ref, o_ref, out_ref, sems):
    block = aligned(Place().block(0), LANES)
    moves = []
    for i, ref in enumerate((q_ref, k_ref, v_ref)):
        for j in range(2):
            moves.append((ref.at[block, pl.ds(j * LANES, LANES)], (2 * i + j) * LANES, LANES))
    moves.append((o_ref.at[:, block], 6 * LANES, o_ref.shape[0]))
    copies = [
        pltpu.make_async_copy(src, out_ref.at[pl.ds(top, size)], sems.at[n])
        for n, (src, top, size) in enumerate(moves)
    ]
    for copy in copies:
        copy.start()
    for copy in copies:
        copy.wait()


def pack_mlp(_, g_ref, u_ref, d_ref, out_ref, sems):
    block = aligned(Place().block(0), LANES)
    rows = g_ref.shape[0]
    copies = [
        pltpu.make_async_copy(ref.at[:, block], out_ref.at[pl.ds(n * rows, rows)], sems.at[n])
        for n, ref in enumerate((g_ref, u_ref, d_ref))
    ]
    for copy in copies:
        copy.start()
    for copy in copies:
        copy.wait()


def unpack_attention(q_ref, k_ref, v_ref, o_ref, *rest):
    pieces, (qkv_ref, out_ref) = rest[:8], rest[8:]
    here = Place()
    width = q_ref.shape[1]

    @pl.when(here.resident == 1)
    def _():
        for i, ref in enumerate((q_ref, k_ref, v_ref)):
            qkv_ref[:, i * width : (i + 1) * width] = ref[...]
        out_ref[...] = o_ref[...]

    @pl.when(here.resident == 0)
    def _():
        for n, piece in enumerate(pieces):
            block = aligned(here.block(n), LANES)
            for j in range(3 * width // LANES):
                qkv_ref[block, j * LANES : (j + 1) * LANES] = piece[j * LANES : (j + 1) * LANES]
            out_ref[:, block] = piece[3 * width :]


def unpack_mlp(g_ref, u_ref, d_ref, *rest):
    pieces, outs, sems = rest[:8], rest[8:11], rest[11]
    here = Place()
    rows = g_ref.shape[0]

    @pl.when(here.resident == 1)
    def _():
        copies = [
            pltpu.make_async_copy(ref, out.at[pl.ds(0, rows)], sems.at[n])
            for n, (ref, out) in enumerate(zip((g_ref, u_ref, d_ref), outs))
        ]
        for copy in copies:
            copy.start()
        for out in outs:
            out[rows:] = jnp.zeros((out.shape[0] - rows, out.shape[1]), low)
        for copy in copies:
            copy.wait()

    @pl.when(here.resident == 0)
    def _():
        copies = [
            pltpu.make_async_copy(
                pieces[n].at[pl.ds(i * rows, rows)],
                out.at[pl.ds(0, rows), aligned(here.block(n), LANES)],
                sems.at[3 * n + i],
            )
            for n in range(8)
            for i, out in enumerate(outs)
        ]
        for copy in copies:
            copy.start()
        for out in outs:
            out[rows:] = jnp.zeros((out.shape[0] - rows, out.shape[1]), low)
        for copy in copies:
            copy.wait()


def head_pair(rows):
    lane = lax.broadcasted_iota(jnp.int32, rows.shape, 1)
    zero = jnp.zeros_like(rows)
    return jnp.concatenate(
        [jnp.where(lane < HEAD_DIM, rows, zero), jnp.where(lane < HEAD_DIM, zero, rows)], axis=0
    )


def unstack(stacked):
    half = stacked.shape[0] // 2
    lane = lax.broadcasted_iota(jnp.int32, (half, stacked.shape[1]), 1)
    return jnp.where(lane < HEAD_DIM, stacked[:half], stacked[half:])


def band(first, has_halo):
    shape = (2 * WINDOW, 2 * WINDOW)
    row = lax.broadcasted_iota(jnp.int32, shape, 0) % WINDOW
    col = lax.broadcasted_iota(jnp.int32, shape, 1)
    mask = (col > row) & (col <= row + WINDOW)
    if first:
        mask = mask & ((col >= WINDOW) | (has_halo > 0))
    return mask


def softmax(scores, mask):
    scores = jnp.where(mask, scores * HEAD_DIM ** (-0.5), very_low)
    expo = jnp.exp(scores - jnp.max(scores, axis=-1, keepdims=True))
    return expo * (1.0 / jnp.sum(expo, axis=-1, keepdims=True))


def place(ref, seq, part, halo, own, pair, change):
    rows = own.shape[0]
    ref[seq, 0:WINDOW] = change(halo[...])
    ref[seq, pl.ds(pl.multiple_of(WINDOW + rows * part, WINDOW), rows)] = change(own[...])
    ref[seq, pl.ds(pl.multiple_of(WINDOW + rows * (1 - part), WINDOW), rows)] = change(pair[...])


def forward_kernel(
    gain_ref, qkv_w, out_w, halo0, own0, pair0, halo1, own1, pair1,
    normed_ref, qkv_ref, mixed_ref, mine_own, mine_pair, sib_own, sib_pair,
):
    here = Place()
    part, has_halo = here.part, here.side
    gain = gain_ref[...].astype(full)

    def norm(rows):
        return rms_norm(rows.astype(full), gain).astype(low)

    place(normed_ref, 0, part, halo0, own0, pair0, norm)
    place(normed_ref, 1, part, halo1, own1, pair1, norm)
    seqs, rows, width3 = qkv_ref.shape
    width = width3 // 3
    for seq in (1, 0):
        qkv_ref[seq] = mat(normed_ref[seq], qkv_w[...]).astype(low)
    plain, first = band(False, 0), band(True, has_halo)
    units = [(lane, top) for top in range(0, rows - WINDOW, WINDOW) for lane in range(0, width, LANES)]
    for seq in (1, 0):
        for start in range(0, len(units), 4):
            group = units[start : start + 4]
            scores = []
            for lane, top in group:
                q = qkv_ref[seq, top + WINDOW : top + 2 * WINDOW, lane : lane + LANES]
                k = qkv_ref[seq, top : top + 2 * WINDOW, width + lane : width + lane + LANES]
                scores.append(mat_right(head_pair(q), k))
            probs = [
                softmax(s, plain if top else first).astype(low)
                for s, (lane, top) in zip(scores, group)
            ]
            for p, (lane, top) in zip(probs, group):
                at = 2 * width + lane
                v = qkv_ref[seq, top : top + 2 * WINDOW, at : at + LANES]
                mixed_ref[seq, top : top + WINDOW, lane : lane + LANES] = unstack(mat(p, v)).astype(low)
        half = (rows - WINDOW) // 2
        for target, which in ((sib_own if seq else mine_own, part), (sib_pair if seq else mine_pair, 1 - part)):
            target[...] = mat(mixed_ref[seq, aligned(which, half)], out_w[...]).astype(low)


def backward_kernel(
    bg00, bg01, bg10, bg11, out_w, mixed_ref, qkv_ref, normed_ref,
    out_ref, first_ref, mixed_grad,
):
    here = Place()
    has_halo = here.side
    seqs, rows, width3 = qkv_ref.shape
    width = width3 // 3
    factor = HEAD_DIM ** (-0.5)
    half = bg00.shape[0]
    for seq, pair in enumerate(((bg00, bg01), (bg10, bg11))):
        for ref, which in zip(pair, (here.part, 1 - here.part)):
            mixed_grad[seq, aligned(which, half)] = mat_right(ref[...], out_w[...]).astype(low)
    plain, first = band(False, 0), band(True, has_halo)
    for seq in range(seqs):
        out_ref[seq, 0:WINDOW, 0:width] = jnp.zeros((WINDOW, width), low)
        tails = {}
        for lane in range(0, width, LANES):
            tails[lane] = (jnp.zeros((WINDOW, LANES), full), jnp.zeros((WINDOW, LANES), full))
        for top0 in range(0, rows - WINDOW, 2 * WINDOW):
            group = [(lane, top0 + w) for w in (0, WINDOW) for lane in range(0, width, LANES)]
            loaded, scores, prob_grads = [], [], []
            for lane, top in group:
                q = head_pair(qkv_ref[seq, top + WINDOW : top + 2 * WINDOW, lane : lane + LANES])
                k = qkv_ref[seq, top : top + 2 * WINDOW, width + lane : width + lane + LANES]
                v = qkv_ref[seq, top : top + 2 * WINDOW, 2 * width + lane : 2 * width + lane + LANES]
                g = head_pair(mixed_grad[seq, top : top + WINDOW, lane : lane + LANES])
                loaded.append((q, k, g))
                scores.append(mat_right(q, k))
                prob_grads.append(mat_right(g, v))
            probs = [softmax(s, plain if top else first) for s, (lane, top) in zip(scores, group)]
            score_grads = [
                (p * (pg - jnp.sum(p * pg, axis=-1, keepdims=True))).astype(low)
                for p, pg in zip(probs, prob_grads)
            ]
            for p, sg, (q, k, g), (lane, top) in zip(probs, score_grads, loaded, group):
                q_grad = unstack(mat(sg, k)) * factor
                k_grad = mat_left(sg, q) * factor
                v_grad = mat_left(p.astype(low), g)
                k_tail, v_tail = tails[lane]
                out_ref[seq, top + WINDOW : top + 2 * WINDOW, lane : lane + LANES] = q_grad.astype(low)
                at = width + lane
                out_ref[seq, top : top + WINDOW, at : at + LANES] = (k_tail + k_grad[:WINDOW]).astype(low)
                at = 2 * width + lane
                out_ref[seq, top : top + WINDOW, at : at + LANES] = (v_tail + v_grad[:WINDOW]).astype(low)
                tails[lane] = (k_grad[WINDOW:], v_grad[WINDOW:])
        for lane, (k_tail, v_tail) in tails.items():
            at = width + lane
            out_ref[seq, rows - WINDOW : rows, at : at + LANES] = k_tail.astype(low)
            at = 2 * width + lane
            out_ref[seq, rows - WINDOW : rows, at : at + LANES] = v_tail.astype(low)
    attention_role(here.part, here.role(0), first_ref, (bg00, bg01, bg10, bg11), mixed_ref, out_ref, normed_ref)


def attention_role(part, quarter, target, grads, mixed_ref, qkv_grad_ref, normed_ref):
    seqs, rows, width3 = qkv_grad_ref.shape
    block = aligned(quarter, target.shape[0])
    total = mat_left(normed_ref[0, :, block], qkv_grad_ref[0])
    total += mat_left(normed_ref[1, :, block], qkv_grad_ref[1])
    target[:, :width3] = total.astype(low)
    half = grads[0].shape[0]
    total = None
    for n, ref in enumerate(grads):
        seq, i = divmod(n, 2)
        term = mat_left(ref[:, block], mixed_ref[seq, aligned(1 - part if i else part, half)])
        total = term if total is None else total + term
    target[:, width3:] = total.astype(low)


def attention_grads_kernel(
    bg00, bg01, bg10, bg11, mixed_ref, qkv_grad_ref, normed_ref, one_ref, two_ref, own_ref
):
    here = Place()
    for n, ref in enumerate((one_ref, two_ref, own_ref)):
        attention_role(
            here.part, here.role(1 + n), ref, (bg00, bg01, bg10, bg11), mixed_ref, qkv_grad_ref, normed_ref
        )


def normed_grad_kernel(qkv_w, grad_ref, mine_ref, sib_ref):
    part = Place().part
    half = (grad_ref.shape[1] - WINDOW) // 2
    for seq, target in ((1, sib_ref), (0, mine_ref)):
        target[0:WINDOW] = mat_right(grad_ref[seq, 0:WINDOW], qkv_w[...]).astype(target.dtype)
        for i, which in enumerate((part, 1 - part)):
            at = pl.ds(pl.multiple_of(WINDOW + half * which, WINDOW), half)
            target[WINDOW + i * half : WINDOW + (i + 1) * half] = mat_right(
                grad_ref[seq, at], qkv_w[...]
            ).astype(target.dtype)


def mlp_kernel(gate_w, up_w, down_w, mid, dy, target, hidden_ref, gg_ref, ug_ref):
    gate = mat_right(mid[...], gate_w[...])
    up = mat_right(mid[...], up_w[...])
    back = mat_right(dy[...], down_w[...])
    sig = 1.0 / (1.0 + jnp.exp(-gate))
    silu = gate * sig
    hidden_ref[...] = (silu * up).astype(low)
    ug = (back * silu).astype(low)
    gg = (back * up * sig * (1.0 + gate * (1.0 - sig))).astype(low)
    ug_ref[...] = ug
    gg_ref[...] = gg
    target[...] = (mat(gg, gate_w[...]) + mat(ug, up_w[...])).astype(low)


def mlp_grads_kernel(roles, *rest):
    hiddens, ggs, ugs, mids, dys, targets = (rest[i : i + 4] for i in range(0, 24, 4))
    rows = targets[0].shape[0] // 3
    here = Place()
    for role, target in zip(roles, targets):
        block = aligned(here.role(role), target.shape[1])
        for i, (lefts, rights) in enumerate(((ggs, mids), (ugs, mids), (hiddens, dys))):
            total = None
            for left, right in zip(lefts, rights):
                term = mat_left(left[...], right[:, block])
                total = term if total is None else total + term
            target[i * rows : (i + 1) * rows] = total[:rows].astype(low)


def split_kernel(axis, total_ref, arrived_ref, keep_ref, give_ref):
    core = Place().core
    size = total_ref.shape[axis] // 2
    for which, ref in ((core, keep_ref), (1 - core, give_ref)):
        at = (slice(None),) * axis + (aligned(which, size),)
        ref[...] = (total_ref[at].astype(full) + arrived_ref[at].astype(full)).astype(low)


def choose_kernel(keep_ref, help_ref, out_ref):
    here = Place()

    @pl.when(here.resident == 1)
    def _():
        out_ref[...] = keep_ref[...]

    @pl.when(here.resident == 0)
    def _():
        out_ref[...] = help_ref[...]


def middle_kernel(gain_ref, token_ref, sum_ref, arrived_ref, middle_ref, mid_ref):
    middle = token_ref[...].astype(full) + (sum_ref[...].astype(full) + arrived_ref[...].astype(full))
    middle_ref[...] = middle
    mid_ref[...] = rms_norm(middle, gain_ref[...].astype(full)).astype(low)


def stack_kernel(own, own_sib, pair, pair_sib, out):
    rows = own.shape[0]
    out[:rows] = (own[...].astype(full) + own_sib[...].astype(full)).astype(low)
    out[rows:] = (pair[...].astype(full) + pair_sib[...].astype(full)).astype(low)


def middle_grad_kernel(
    gain_ref, dy, dy_pair, middle, middle_pair, sum_ref, arrived_ref, grad_ref, low_ref, low_pair_ref
):
    rows = dy.shape[0]
    gain = gain_ref[...].astype(full)
    for n, (up, values) in enumerate(((dy, middle), (dy_pair, middle_pair))):
        here, there = pl.ds(n * rows, rows), pl.ds((1 - n) * rows, rows)
        grad = sum_ref[here].astype(full) + arrived_ref[there].astype(full)
        total = up[...].astype(full) + rms_pull(values[...], gain, grad)
        if n == 0:
            grad_ref[...] = total
        (low_pair_ref if n else low_ref)[...] = total.astype(low)


def add_kernel(*refs):
    terms, out = refs[:-1], refs[-1]
    total = terms[0][...].astype(full)
    for term in terms[1:]:
        total = total + term[...].astype(full)
    out[...] = total.astype(out.dtype)


def mlp_out_kernel(down_w, own, own_sib, pair, pair_sib, *outs):
    for ref, out in zip((own, own_sib, pair, pair_sib), outs):
        out[...] = mat(ref[...], down_w[...]).astype(out.dtype)


def output_kernel(middle_ref, mine_ref, sib_ref, pair_ref, out_ref, scratch, sem):
    rows = out_ref.shape[0]
    total = middle_ref[...] + mine_ref[...] + sib_ref[...].astype(full)
    total = total + pair_ref[WINDOW + rows :].astype(full)
    scratch[...] = total.astype(low)
    copy = pltpu.make_async_copy(scratch, out_ref, sem)
    copy.start()
    copy.wait()


def normed_sum_kernel(out_pair, out_pair_sib, mine_ref, sib_ref, own_ref, halo_ref, away_ref):
    rows = own_ref.shape[0]

    def total(top, size):
        return mine_ref[top : top + size] + sib_ref[top : top + size].astype(full)

    halo = total(0, WINDOW)
    halo_ref[...] = halo
    away_ref[:WINDOW] = halo.astype(low)
    own_ref[...] = total(WINDOW, rows)
    away_ref[WINDOW : WINDOW + rows] = total(WINDOW + rows, rows).astype(low)
    away_ref[WINDOW + rows :] = (out_pair[...].astype(full) + out_pair_sib[...].astype(full)).astype(low)


def halo_kernel(halo_ref, arrived_ref, out_ref):
    out_ref[...] = (halo_ref[...] + arrived_ref[:WINDOW].astype(full)).astype(low)


def input_grad_kernel(
    gain_ref, token_ref, middle_grad_ref, own_ref, arrived_ref, halo_ref, out_ref, scratch, sem
):
    rows = own_ref.shape[0]
    scratch[...] = own_ref[...] + arrived_ref[WINDOW : WINDOW + rows].astype(full)
    scratch[rows - WINDOW :] = scratch[rows - WINDOW :] + halo_ref[...].astype(full)
    pull = rms_pull(token_ref[...].astype(full), gain_ref[...].astype(full), scratch[...])
    scratch[...] = middle_grad_ref[...] + pull
    copy = pltpu.make_async_copy(scratch, out_ref, sem)
    copy.start()
    copy.wait()


def gains_kernel(attn_gain, mlp_gain, q_ref, k_ref, v_ref, g_ref, u_ref, *rest):
    mlp_pieces, attn_pieces, part = rest[:8], rest[8:16], rest[16]
    width, rows = q_ref.shape[1], g_ref.shape[0]
    here = Place()
    for n, piece in enumerate(attn_pieces):
        block = aligned(here.block(n), LANES)
        sums = None
        for i, weight in enumerate((q_ref, k_ref, v_ref)):
            term = piece[:, i * width : (i + 1) * width].astype(full) * weight[block].astype(full)
            sums = term if sums is None else sums + term
        sums = jnp.sum(sums, axis=1, keepdims=True)
        row = jnp.broadcast_to(sums, (LANES, LANES)).T[0:1]
        part[0:1, block] = row / attn_gain[:, block].astype(full)
    for n, piece in enumerate(mlp_pieces):
        block = aligned(here.block(n), LANES)
        sums = piece[0:rows].astype(full) * g_ref[:, block].astype(full)
        sums = sums + piece[rows : 2 * rows].astype(full) * u_ref[:, block].astype(full)
        part[1:2, block] = jnp.sum(sums, axis=0, keepdims=True) / mlp_gain[:, block].astype(full)


def finish_attention(*rest):
    pieces, (gq, gk, gv, go, gq_s, gk_s, gv_s, go_s, sems) = rest[:8], rest[8:]
    width = gq.shape[1]
    here = Place()
    for n, piece in enumerate(pieces):
        block = aligned(here.block(n), LANES)
        for i, ref in enumerate((gq_s, gk_s, gv_s)):
            ref[block] = piece[:, i * width : (i + 1) * width].astype(full)
        go_s[:, block] = piece[:, 3 * width :].astype(full).T
    copies = [
        pltpu.make_async_copy(src, dst, sems.at[n])
        for n, (src, dst) in enumerate(((gq_s, gq), (gk_s, gk), (gv_s, gv), (go_s, go)))
    ]
    for copy in copies:
        copy.start()
    for copy in copies:
        copy.wait()


def finish_mlp(*rest):
    pieces, (gg, gu, gd, gg_s, gu_s, gd_s, sems) = rest[:8], rest[8:]
    rows = gg.shape[0]
    here = Place()
    copies = []
    for i, (ref, out) in enumerate(((gg_s, gg), (gu_s, gu), (gd_s, gd))):
        for n, piece in enumerate(pieces):
            ref[:, aligned(here.block(n), LANES)] = piece[i * rows : (i + 1) * rows].astype(full)
        copies.append(pltpu.make_async_copy(ref, out, sems.at[i]))
        copies[-1].start()
    for copy in copies:
        copy.wait()


def build(n_dp, n_t):
    extra = [1 << k for k in range(3, n_dp.bit_length() - 1)]

    def perm(target):
        pairs = []
        for d in range(n_dp):
            for t in range(n_t):
                to = target(d, t)
                if to is not None:
                    pairs.append((d * n_t + t, to[0] * n_t + to[1]))
        return pairs

    def sender(target):
        return functools.partial(lax.ppermute, axis_name=AXES, perm=perm(target))

    send_core = sender(lambda d, t: (d ^ 1, t))
    send_pair = sender(lambda d, t: (d, t ^ 1))
    send_far = sender(lambda d, t: (d, t ^ 2))
    send_owner = sender(lambda d, t: (d, t ^ 2) if (d & 1) != (t >> 1) else None)
    send_help = send_core
    send_one = sender(lambda d, t: (d ^ (4 if d & 1 else 2), t))
    send_two = sender(lambda d, t: (d ^ (2 if d & 1 else 4), t))
    send_cross = [sender(lambda d, t, k=k: (d, t ^ k)) for k in (1, 2)]
    send_extra = [sender(lambda d, t, bit=bit: (d ^ bit, t)) for bit in extra]

    def local(
        tokens, gain_attn, w_query, w_key, w_value, w_out, gain_mlp, w_gate, w_up, w_down, out_grad
    ):
        own_rows, depth = tokens.shape
        hidden_cols = w_gate.shape[1]
        head_cols = w_query.shape[1]
        padded = -(-hidden_cols // 256) * 256
        ext = WINDOW + 2 * own_rows
        plans, made = {}, {}

        def value(item):
            return emit(item.name)[item.index] if isinstance(item, Later) else item

        def emit(name):
            if name not in made:
                function, args = plans[name]
                args = [value(arg) for arg in args]
                events = tuple(emit(event)[0] for event in ORDER.get(name, ()))
                if events:
                    args[-1] = after(args[-1], events)
                made[name] = function(*args)
            return made[name]

        def move(name, send, item):
            plans[name] = (lambda array: (send(array),)), [item]
            return Later(name, 0)

        def run(name, kernel, outs, args, **options):
            plans[name] = (
                lambda *arrays: tuple(call(kernel, outs, arrays, cost=COST.get(name, 0), **options))
            ), list(args)
            results = [Later(name, n) for n in range(len(outs))]
            return results if len(results) > 1 else results[0]

        def add(name, shape, *terms, dtype=low):
            return run(name, add_kernel, [(shape, dtype)], terms)

        chunk, wide_chunk = ((own_rows, depth), low), ((own_rows, depth), full)

        def three(name, piece):
            one = move(name + "1", send_one, piece)
            two = move(name + "2", send_two, piece)
            return [piece, one, two, move(name + "3", send_two, one)]

        def to_core(name, send, pieces):
            return [move(name + str(n), send, piece) for n, piece in enumerate(pieces)]

        def hold(array):
            return pltpu.with_memory_space_constraint(array, pltpu.HBM)

        gate_t, up_t = w_gate.T, w_up.T
        packed = call(
            pack_attention,
            [((3 * head_cols + w_out.shape[0], LANES), low)],
            tuple(hold(w) for w in (w_query, w_key, w_value, w_out)),
            scratch=[pltpu.SemaphoreType.DMA((7,))],
            anywhere=4,
        )[0]
        made["pack"] = (packed,)
        attn = move("za", send_far, packed)
        first_tokens = after(tokens, packed)
        token_pair = move("zt", send_pair, first_tokens)
        tail = first_tokens[own_rows - WINDOW :]
        halo = add(
            "h4",
            tail.shape,
            move("h2", sender(lambda d_, t_: (d_, 2) if t_ == 1 else None), tail),
            move("h3", sender(lambda d_, t_: (d_, 3) if t_ == 1 else None), tail),
        )
        token_sib = move("ct", send_core, first_tokens)
        wide_packed = call(
            pack_mlp,
            [((3 * hidden_cols, LANES), low)],
            (packed, hold(gate_t), hold(up_t), hold(w_down)),
            scratch=[pltpu.SemaphoreType.DMA((3,))],
            anywhere=4,
        )[0]
        made["packf"] = (wide_packed,)
        wide = move("zw", send_far, wide_packed)
        dy, dy_pair = out_grad, move("zy", send_pair, out_grad)
        mine = three("a", attn)
        pieces = mine + to_core("ca", send_help, mine)
        halo_sib = move("ch", send_core, halo)
        token_pair_sib = move("cp", send_core, token_pair)
        qkv_w, out_w = run(
            "unpacka",
            unpack_attention,
            [((depth, 3 * head_cols), low), (w_out.shape, low)],
            (w_query, w_key, w_value, w_out, *pieces),
        )

        normed, qkv, mixed, mine_own, mine_pair, sib_own, sib_pair = run(
            "attend",
            forward_kernel,
            [((2, ext, depth), low), ((2, ext, 3 * head_cols), low), ((2, 2 * own_rows, head_cols), low)]
            + [chunk] * 4,
            (gain_attn.reshape(1, depth), qkv_w, out_w, halo, tokens, token_pair,
             halo_sib, token_sib, token_pair_sib),
        )
        mlp_gain = gain_mlp.reshape(1, depth)
        sum_pair = add("sp", chunk[0], mine_pair, move("cqp", send_core, sib_pair))
        sum_own = add("so", chunk[0], mine_own, move("cqo", send_core, sib_own))
        arrived_own = move("zb0", send_pair, sum_pair)
        arrived_pair = move("zb1", send_pair, sum_own)
        wides = three("w", wide)
        dy_sib = move("cy", send_core, dy)
        dy_pair_sib = move("cyp", send_core, dy_pair)
        weights = to_core("cw", send_help, wides)
        middle_own, mid_own = run(
            "ko", middle_kernel, [wide_chunk, chunk], (mlp_gain, tokens, sum_own, arrived_own)
        )
        mid_own_sib = move("cmo", send_core, mid_own)
        gate_w, up_w, down_w = run(
            "unpackf",
            unpack_mlp,
            [((padded, depth), low)] * 3,
            (gate_t, up_t, w_down, *wides, *weights),
            scratch=[pltpu.SemaphoreType.DMA((24,))],
            anywhere=11,
        )

        def feed_forward(name, mid, dy):
            return run(
                name,
                mlp_kernel,
                [chunk] + [((own_rows, padded), low)] * 3,
                (gate_w, up_w, down_w, mid, dy),
            )

        part_sib, *tables_own_sib = feed_forward("fos", mid_own_sib, dy_sib)
        arrived_own_part = move("cfo", send_core, part_sib)
        part_own, *tables_own = feed_forward("fo", mid_own, dy)
        middle_pair, mid_pair = run(
            "kp", middle_kernel, [wide_chunk, chunk], (mlp_gain, token_pair, sum_pair, arrived_pair)
        )
        mid_pair_sib = move("cmp", send_core, mid_pair)
        part_sib, *tables_pair_sib = feed_forward("fps", mid_pair_sib, dy_pair_sib)
        arrived_pair_part = move("cfp", send_core, part_sib)
        part_pair, *tables_pair = feed_forward("fp", mid_pair, dy_pair)
        part_sum = run(
            "fs",
            stack_kernel,
            [((2 * own_rows, depth), low)],
            (part_own, arrived_own_part, part_pair, arrived_pair_part),
        )
        part_arrived = move("zm", send_pair, part_sum)

        tables = [tables_own, tables_own_sib, tables_pair, tables_pair_sib]
        grad_args = [table[i] for i in range(3) for table in tables]
        grad_args += [mid_own, mid_own_sib, mid_pair, mid_pair_sib, dy, dy_sib, dy_pair, dy_pair_sib]
        quarter = ((3 * hidden_cols, depth // 4), low)
        mlp_diag = run("g0", functools.partial(mlp_grads_kernel, (0,)), [quarter], grad_args)
        mlp_far = move("f1", send_one, mlp_diag)
        mlp_one, mlp_two, mlp_own = run(
            "g1", functools.partial(mlp_grads_kernel, (1, 2, 3)), [quarter] * 3, grad_args
        )
        mlp_near = move("f2", send_one, mlp_one)
        out_own, out_own_sib, out_pair, out_pair_sib = run(
            "mo",
            mlp_out_kernel,
            [wide_chunk, chunk, chunk, chunk],
            (down_w, *[table[0] for table in tables]),
        )
        out_own_arrived = move("coo", send_core, out_own_sib)
        out_pair_arrived = move("cop", send_core, out_pair_sib)

        middle_grad, branch_own, branch_pair = run(
            "mq",
            middle_grad_kernel,
            [wide_chunk, chunk, chunk],
            (mlp_gain, dy, dy_pair, middle_own, middle_pair, part_sum, part_arrived),
        )
        branch_pair_sib = move("cbp", send_core, branch_pair)
        branch_own_sib = move("cbo", send_core, branch_own)
        mlp_two = add("fs2", quarter[0], mlp_two, mlp_far)
        mlp_last = move("f3", send_two, mlp_two)

        bgs = (branch_own, branch_pair, branch_own_sib, branch_pair_sib)
        quarter = ((depth // 4, 4 * head_cols), low)
        qkv_grad, diag = run(
            "bwd",
            backward_kernel,
            [((2, ext, 3 * head_cols), low), quarter],
            (*bgs, out_w, mixed, qkv, normed),
            scratch=[pltpu.VMEM((2, 2 * own_rows, head_cols), low)],
        )
        far = move("b1", send_one, diag)
        one, two, last_own = run(
            "ag", attention_grads_kernel, [quarter] * 3, (*bgs, mixed, qkv_grad, normed)
        )
        near = move("b2", send_one, one)

        def everywhere(name, shape, total, dtype=low):
            for n, send in enumerate(send_extra):
                total = add(name + "a%d" % n, shape, total, move(name + "e%d" % n, send, total), dtype=dtype)
            return total

        mlp_shape = (3 * hidden_cols, depth // 4)
        mlp_total = everywhere("fx", mlp_shape, add("ft", mlp_shape, mlp_own, mlp_near, mlp_last))
        mlp_arrived = move("zf", send_owner, mlp_total)
        two = add("bs2", quarter[0], two, far)
        last = move("b3", send_two, two)
        grad_mine, grad_sib = run(
            "nk", normed_grad_kernel, [((ext, depth), full), ((ext, depth), low)], (qkv_w, qkv_grad)
        )
        grad_own, grad_halo, grad_away = run(
            "ns",
            normed_sum_kernel,
            [wide_chunk, ((WINDOW, depth), full), ((WINDOW + 2 * own_rows, depth), low)],
            (out_pair, out_pair_arrived, grad_mine, move("cn", send_core, grad_sib)),
        )
        grad_arrived = move("zn", send_pair, grad_away)
        output = run(
            "out",
            output_kernel,
            [chunk + (0,)],
            (middle_own, out_own, out_own_arrived, grad_arrived),
            scratch=[pltpu.VMEM(*chunk), pltpu.SemaphoreType.DMA],
        )
        total = everywhere("bx", quarter[0], add("bt", quarter[0], last_own, near, last))
        total_arrived = move("zg", send_owner, total)

        def to_both(name, shape, total, arrived, axis):
            shape = list(shape)
            shape[axis] //= 2
            half = (tuple(shape), low)
            keep, give = run(
                name + "s", functools.partial(split_kernel, axis), [half, half], (total, arrived)
            )
            return run(name + "c", choose_kernel, [half], (keep, move(name + "h", send_help, give)))

        mlp_mine = three("fa", to_both("fh", mlp_shape, mlp_total, mlp_arrived, 1))
        mine = three("ba", to_both("bh", quarter[0], total, total_arrived, 0))
        halo_sum = run("hk", halo_kernel, [((WINDOW, depth), low)], (grad_halo, grad_arrived))
        halo_grad = move("hh", sender(lambda d_, t_: (d_, 1) if t_ == 2 else None), halo_sum)
        input_grad = run(
            "ik",
            input_grad_kernel,
            [wide_chunk + (0,)],
            (gain_attn.reshape(1, depth), tokens, middle_grad, grad_own, grad_arrived, halo_grad),
            scratch=[pltpu.VMEM(*wide_chunk), pltpu.SemaphoreType.DMA],
        )
        mlp_pieces = mlp_mine + to_core("cfa", send_core, mlp_mine)
        shape = (hidden_cols, depth)
        pieces = mine + to_core("cba", send_core, mine)
        gain_shape = (2, depth)
        gains = run(
            "pg",
            gains_kernel,
            [(gain_shape, full)],
            (gain_attn.reshape(1, depth), mlp_gain, w_query, w_key, w_value, gate_t, up_t, *mlp_pieces, *pieces),
        )
        grad_gate, grad_up, grad_down = run(
            "finf",
            finish_mlp,
            [(shape, full, 0)] * 3,
            mlp_pieces,
            scratch=[pltpu.VMEM(shape, full)] * 3 + [pltpu.SemaphoreType.DMA((3,))],
        )
        grad_query, grad_key, grad_value, grad_out = run(
            "finb",
            finish_attention,
            [(w_query.shape, full, 0)] * 3 + [(w_out.shape, full, 0)],
            pieces,
            scratch=[pltpu.VMEM(w_query.shape, full)] * 3
            + [pltpu.VMEM(w_out.shape, full), pltpu.SemaphoreType.DMA((4,))],
        )
        for n, send in enumerate(send_cross):
            gains = add("g%s" % "ab"[n], gain_shape, gains, move("y%d" % n, send, gains), dtype=full)
        for name in plans:
            emit(name)
        gains = value(gains)
        return (
            value(output),
            value(input_grad),
            gains[0],
            value(grad_query),
            value(grad_key),
            value(grad_value),
            value(grad_out),
            gains[1],
            value(grad_gate).T,
            value(grad_up).T,
            value(grad_down),
        )

    return local


def solution(mesh):
    both = P(("dp", "tensor"), None)
    columns, rows = P(None, "tensor"), P("tensor", None)
    return jax.shard_map(
        build(mesh.shape["dp"], mesh.shape["tensor"]),
        mesh=mesh,
        in_specs=(both, P(), columns, columns, columns, rows, P(), columns, columns, rows, both),
        out_specs=(both, both, P(), columns, columns, columns, rows, P(), columns, columns, rows),
        check_vma=False,
    )
```

```python
import functools

import jax
import jax.numpy as jnp
from jax import lax
from jax.experimental import pallas as pl
from jax.experimental.pallas import tpu as pltpu
from jax.sharding import PartitionSpec as P

HEAD_DIM = 64
WINDOW = 64
LANES = 128

norm_eps = 1e-05
very_low = -1e30
AXES = ("dp", "tensor")
low = jnp.bfloat16
ORDER = {
    "unpacka": ("a3", "ch",),
    "cfa1": ("fhh", "bhc",),
    "ca2": ("zy", "ca0",),
    "so": ("a1",),
    "kp": ("ch", "fo",),
    "a2": ("h2",),
    "zm": ("unpacka",),
    "cyp": ("cqp",),
    "fps": ("unpackf",),
    "cop": ("g1", "f2", "coo",),
    "ag": ("f3", "bwd",),
    "a3": ("zt", "h3", "packf",),
    "cfa2": ("ba2", "cfa0",),
    "ca3": ("pack",),
    "fos": ("unpackf",),
    "nk": ("ft",),
    "cw0": ("w3",),
    "zg": ("cn", "bt",),
    "ca1": ("a3",),
    "zw": ("za",),
    "w1": ("a2",),
    "h3": ("za",),
    "fhc": ("cn",),
    "cmp": ("cqp",),
    "bwd": ("kp",),
    "bs2": ("cbo",),
    "zn": ("cn",),
    "ba3": ("bhh",),
    "fa2": ("b1",),
    "cfo": ("fps",),
    "ch": ("pack",),
    "ba1": ("bhc",),
    "cfp": ("cfo",),
    "ik": ("bhc",),
    "a1": ("packf",),
    "zy": ("pack",),
    "out": ("bt",),
}
COST = {
    "ko": 8,
    "mo": 2,
    "g1": 2,
    "hk": 4,
    "bwd": 1,
    "kp": 4,
    "mq": 8,
    "fs": 2,
    "fps": 2,
    "ft": 1,
    "bhs": 2,
    "fo": 1,
    "fhs": 1,
    "so": 2,
    "nk": 8,
    "fos": 2,
    "fs2": 8,
    "finb": 4,
    "bt": 4,
    "bhc": 2,
    "bs2": 16,
}
full = jnp.float32


def mat(left, right):
    return jnp.dot(left, right, preferred_element_type=full)


def mat_left(left, right):
    return lax.dot_general(left, right, (((0,), (0,)), ((), ())), preferred_element_type=full)


def mat_right(left, right):
    return lax.dot_general(left, right, (((1,), (1,)), ((), ())), preferred_element_type=full)


def rms_scale(values):
    return lax.rsqrt(jnp.mean(values * values, axis=-1, keepdims=True) + norm_eps)


def rms_norm(values, gain):
    return values * rms_scale(values) * gain


def rms_pull(values, gain, grad):
    scale = rms_scale(values)
    unit = values * scale
    scaled = grad * gain
    inner = jnp.mean(scaled * unit, axis=-1, keepdims=True)
    return scale * (scaled - unit * inner)


def after(value, event):
    return lax.optimization_barrier((value, event))[0]


def aligned(index, size):
    return pl.ds(pl.multiple_of(index * size, size), size)


class Place:
    def __init__(self):
        d, t = lax.axis_index("dp"), lax.axis_index("tensor")
        self.z, self.core, self.part, self.side = t, d & 1, t & 1, (t >> 1) & 1
        self.x, self.y = (d >> 1) & 1, (d >> 2) & 1
        self.resident = 1 - (self.core ^ self.side)

    def quarter(self, one, two, other=0):
        core = self.core ^ other
        flip_x = (1 - core) * one + core * two
        flip_y = (1 - core) * two + core * one
        return 2 * (self.y ^ flip_y) + (self.x ^ flip_x)

    def block(self, n):
        other = n // 4
        return 2 * self.quarter(n % 2, n % 4 // 2, other) + (self.core ^ other)

    def role(self, n):
        return self.quarter((1, 1, 0, 0)[n], (1, 0, 1, 0)[n])


class Later:
    def __init__(self, name, index):
        self.name, self.index = name, index


def call(kernel, outs, args, scratch=(), anywhere=0, limit=24, cost=0):
    specs = [pl.BlockSpec(memory_space=pl.ANY)] * anywhere + [
        pl.BlockSpec(memory_space=pltpu.VMEM)
    ] * (len(args) - anywhere)
    shapes = [jax.ShapeDtypeStruct(o[0], o[1]) for o in outs]
    places = [
        pl.BlockSpec(memory_space=pl.ANY if len(o) > 2 else pltpu.VMEM) for o in outs
    ]
    results = pl.pallas_call(
        kernel,
        out_shape=shapes,
        in_specs=specs,
        out_specs=places,
        scratch_shapes=list(scratch),
        compiler_params=pltpu.CompilerParams(vmem_limit_bytes=limit << 20),
        cost_estimate=pl.CostEstimate(flops=cost * 1153000000, bytes_accessed=0, transcendentals=0),
    )(*args)
    return list(results)


def pack_attention(q_ref, k_ref, v_ref, o_ref, out_ref, sems):
    block = aligned(Place().block(0), LANES)
    moves = []
    for i, ref in enumerate((q_ref, k_ref, v_ref)):
        for j in range(2):
            moves.append((ref.at[block, pl.ds(j * LANES, LANES)], (2 * i + j) * LANES, LANES))
    moves.append((o_ref.at[:, block], 6 * LANES, o_ref.shape[0]))
    copies = [
        pltpu.make_async_copy(src, out_ref.at[pl.ds(top, size)], sems.at[n])
        for n, (src, top, size) in enumerate(moves)
    ]
    for copy in copies:
        copy.start()
    for copy in copies:
        copy.wait()


def pack_mlp(_, g_ref, u_ref, d_ref, out_ref, sems):
    block = aligned(Place().block(0), LANES)
    rows = g_ref.shape[0]
    copies = [
        pltpu.make_async_copy(ref.at[:, block], out_ref.at[pl.ds(n * rows, rows)], sems.at[n])
        for n, ref in enumerate((g_ref, u_ref, d_ref))
    ]
    for copy in copies:
        copy.start()
    for copy in copies:
        copy.wait()


def unpack_attention(q_ref, k_ref, v_ref, o_ref, *rest):
    pieces, (qkv_ref, out_ref) = rest[:8], rest[8:]
    here = Place()
    width = q_ref.shape[1]

    @pl.when(here.resident == 1)
    def _():
        for i, ref in enumerate((q_ref, k_ref, v_ref)):
            qkv_ref[:, i * width : (i + 1) * width] = ref[...]
        out_ref[...] = o_ref[...]

    @pl.when(here.resident == 0)
    def _():
        for n, piece in enumerate(pieces):
            block = aligned(here.block(n), LANES)
            for j in range(3 * width // LANES):
                qkv_ref[block, j * LANES : (j + 1) * LANES] = piece[j * LANES : (j + 1) * LANES]
            out_ref[:, block] = piece[3 * width :]


def unpack_mlp(g_ref, u_ref, d_ref, *rest):
    pieces, outs, sems = rest[:8], rest[8:11], rest[11]
    here = Place()
    rows = g_ref.shape[0]

    @pl.when(here.resident == 1)
    def _():
        copies = [
            pltpu.make_async_copy(ref, out.at[pl.ds(0, rows)], sems.at[n])
            for n, (ref, out) in enumerate(zip((g_ref, u_ref, d_ref), outs))
        ]
        for copy in copies:
            copy.start()
        for out in outs:
            out[rows:] = jnp.zeros((out.shape[0] - rows, out.shape[1]), low)
        for copy in copies:
            copy.wait()

    @pl.when(here.resident == 0)
    def _():
        copies = [
            pltpu.make_async_copy(
                pieces[n].at[pl.ds(i * rows, rows)],
                out.at[pl.ds(0, rows), aligned(here.block(n), LANES)],
                sems.at[3 * n + i],
            )
            for n in range(8)
            for i, out in enumerate(outs)
        ]
        for copy in copies:
            copy.start()
        for out in outs:
            out[rows:] = jnp.zeros((out.shape[0] - rows, out.shape[1]), low)
        for copy in copies:
            copy.wait()


def head_pair(rows):
    lane = lax.broadcasted_iota(jnp.int32, rows.shape, 1)
    zero = jnp.zeros_like(rows)
    return jnp.concatenate(
        [jnp.where(lane < HEAD_DIM, rows, zero), jnp.where(lane < HEAD_DIM, zero, rows)], axis=0
    )


def unstack(stacked):
    half = stacked.shape[0] // 2
    lane = lax.broadcasted_iota(jnp.int32, (half, stacked.shape[1]), 1)
    return jnp.where(lane < HEAD_DIM, stacked[:half], stacked[half:])


def band(first, has_halo):
    shape = (2 * WINDOW, 2 * WINDOW)
    row = lax.broadcasted_iota(jnp.int32, shape, 0) % WINDOW
    col = lax.broadcasted_iota(jnp.int32, shape, 1)
    mask = (col > row) & (col <= row + WINDOW)
    if first:
        mask = mask & ((col >= WINDOW) | (has_halo > 0))
    return mask


def softmax(scores, mask):
    scores = jnp.where(mask, scores * HEAD_DIM ** (-0.5), very_low)
    expo = jnp.exp(scores - jnp.max(scores, axis=-1, keepdims=True))
    return expo * (1.0 / jnp.sum(expo, axis=-1, keepdims=True))


def place(ref, seq, part, halo, own, pair, change):
    rows = own.shape[0]
    ref[seq, 0:WINDOW] = change(halo[...])
    ref[seq, pl.ds(pl.multiple_of(WINDOW + rows * part, WINDOW), rows)] = change(own[...])
    ref[seq, pl.ds(pl.multiple_of(WINDOW + rows * (1 - part), WINDOW), rows)] = change(pair[...])


def forward_kernel(
    gain_ref, qkv_w, out_w, halo0, own0, pair0, halo1, own1, pair1,
    normed_ref, qkv_ref, mixed_ref, mine_own, mine_pair, sib_own, sib_pair,
):
    here = Place()
    part, has_halo = here.part, here.side
    gain = gain_ref[...].astype(full)

    def norm(rows):
        return rms_norm(rows.astype(full), gain).astype(low)

    place(normed_ref, 0, part, halo0, own0, pair0, norm)
    place(normed_ref, 1, part, halo1, own1, pair1, norm)
    seqs, rows, width3 = qkv_ref.shape
    width = width3 // 3
    for seq in (1, 0):
        qkv_ref[seq] = mat(normed_ref[seq], qkv_w[...]).astype(low)
    plain, first = band(False, 0), band(True, has_halo)
    units = [(lane, top) for top in range(0, rows - WINDOW, WINDOW) for lane in range(0, width, LANES)]
    for seq in (1, 0):
        for start in range(0, len(units), 4):
            group = units[start : start + 4]
            scores = []
            for lane, top in group:
                q = qkv_ref[seq, top + WINDOW : top + 2 * WINDOW, lane : lane + LANES]
                k = qkv_ref[seq, top : top + 2 * WINDOW, width + lane : width + lane + LANES]
                scores.append(mat_right(head_pair(q), k))
            probs = [
                softmax(s, plain if top else first).astype(low)
                for s, (lane, top) in zip(scores, group)
            ]
            for p, (lane, top) in zip(probs, group):
                at = 2 * width + lane
                v = qkv_ref[seq, top : top + 2 * WINDOW, at : at + LANES]
                mixed_ref[seq, top : top + WINDOW, lane : lane + LANES] = unstack(mat(p, v)).astype(low)
        half = (rows - WINDOW) // 2
        for target, which in ((sib_own if seq else mine_own, part), (sib_pair if seq else mine_pair, 1 - part)):
            target[...] = mat(mixed_ref[seq, aligned(which, half)], out_w[...]).astype(low)


def backward_kernel(
    bg00, bg01, bg10, bg11, out_w, mixed_ref, qkv_ref, normed_ref,
    out_ref, first_ref, mixed_grad,
):
    here = Place()
    has_halo = here.side
    seqs, rows, width3 = qkv_ref.shape
    width = width3 // 3
    factor = HEAD_DIM ** (-0.5)
    half = bg00.shape[0]
    for seq, pair in enumerate(((bg00, bg01), (bg10, bg11))):
        for ref, which in zip(pair, (here.part, 1 - here.part)):
            mixed_grad[seq, aligned(which, half)] = mat_right(ref[...], out_w[...]).astype(low)
    plain, first = band(False, 0), band(True, has_halo)
    for seq in range(seqs):
        out_ref[seq, 0:WINDOW, 0:width] = jnp.zeros((WINDOW, width), low)
        tails = {}
        for lane in range(0, width, LANES):
            tails[lane] = (jnp.zeros((WINDOW, LANES), full), jnp.zeros((WINDOW, LANES), full))
        for top0 in range(0, rows - WINDOW, 2 * WINDOW):
            group = [(lane, top0 + w) for w in (0, WINDOW) for lane in range(0, width, LANES)]
            loaded, scores, prob_grads = [], [], []
            for lane, top in group:
                q = head_pair(qkv_ref[seq, top + WINDOW : top + 2 * WINDOW, lane : lane + LANES])
                k = qkv_ref[seq, top : top + 2 * WINDOW, width + lane : width + lane + LANES]
                v = qkv_ref[seq, top : top + 2 * WINDOW, 2 * width + lane : 2 * width + lane + LANES]
                g = head_pair(mixed_grad[seq, top : top + WINDOW, lane : lane + LANES])
                loaded.append((q, k, g))
                scores.append(mat_right(q, k))
                prob_grads.append(mat_right(g, v))
            probs = [softmax(s, plain if top else first) for s, (lane, top) in zip(scores, group)]
            score_grads = [
                (p * (pg - jnp.sum(p * pg, axis=-1, keepdims=True))).astype(low)
                for p, pg in zip(probs, prob_grads)
            ]
            for p, sg, (q, k, g), (lane, top) in zip(probs, score_grads, loaded, group):
                q_grad = unstack(mat(sg, k)) * factor
                k_grad = mat_left(sg, q) * factor
                v_grad = mat_left(p.astype(low), g)
                k_tail, v_tail = tails[lane]
                out_ref[seq, top + WINDOW : top + 2 * WINDOW, lane : lane + LANES] = q_grad.astype(low)
                at = width + lane
                out_ref[seq, top : top + WINDOW, at : at + LANES] = (k_tail + k_grad[:WINDOW]).astype(low)
                at = 2 * width + lane
                out_ref[seq, top : top + WINDOW, at : at + LANES] = (v_tail + v_grad[:WINDOW]).astype(low)
                tails[lane] = (k_grad[WINDOW:], v_grad[WINDOW:])
        for lane, (k_tail, v_tail) in tails.items():
            at = width + lane
            out_ref[seq, rows - WINDOW : rows, at : at + LANES] = k_tail.astype(low)
            at = 2 * width + lane
            out_ref[seq, rows - WINDOW : rows, at : at + LANES] = v_tail.astype(low)
    attention_role(here.part, here.role(0), first_ref, (bg00, bg01, bg10, bg11), mixed_ref, out_ref, normed_ref)


def attention_role(part, quarter, target, grads, mixed_ref, qkv_grad_ref, normed_ref):
    seqs, rows, width3 = qkv_grad_ref.shape
    block = aligned(quarter, target.shape[0])
    total = mat_left(normed_ref[0, :, block], qkv_grad_ref[0])
    total += mat_left(normed_ref[1, :, block], qkv_grad_ref[1])
    target[:, :width3] = total.astype(low)
    half = grads[0].shape[0]
    total = None
    for n, ref in enumerate(grads):
        seq, i = divmod(n, 2)
        term = mat_left(ref[:, block], mixed_ref[seq, aligned(1 - part if i else part, half)])
        total = term if total is None else total + term
    target[:, width3:] = total.astype(low)


def attention_grads_kernel(
    bg00, bg01, bg10, bg11, mixed_ref, qkv_grad_ref, normed_ref, one_ref, two_ref, own_ref
):
    here = Place()
    for n, ref in enumerate((one_ref, two_ref, own_ref)):
        attention_role(
            here.part, here.role(1 + n), ref, (bg00, bg01, bg10, bg11), mixed_ref, qkv_grad_ref, normed_ref
        )


def normed_grad_kernel(qkv_w, grad_ref, mine_ref, sib_ref):
    part = Place().part
    half = (grad_ref.shape[1] - WINDOW) // 2
    for seq, target in ((1, sib_ref), (0, mine_ref)):
        target[0:WINDOW] = mat_right(grad_ref[seq, 0:WINDOW], qkv_w[...]).astype(target.dtype)
        for i, which in enumerate((part, 1 - part)):
            at = pl.ds(pl.multiple_of(WINDOW + half * which, WINDOW), half)
            target[WINDOW + i * half : WINDOW + (i + 1) * half] = mat_right(
                grad_ref[seq, at], qkv_w[...]
            ).astype(target.dtype)


def mlp_kernel(gate_w, up_w, down_w, mid, dy, target, hidden_ref, gg_ref, ug_ref):
    gate = mat_right(mid[...], gate_w[...])
    up = mat_right(mid[...], up_w[...])
    back = mat_right(dy[...], down_w[...])
    sig = 1.0 / (1.0 + jnp.exp(-gate))
    silu = gate * sig
    hidden_ref[...] = (silu * up).astype(low)
    ug = (back * silu).astype(low)
    gg = (back * up * sig * (1.0 + gate * (1.0 - sig))).astype(low)
    ug_ref[...] = ug
    gg_ref[...] = gg
    target[...] = (mat(gg, gate_w[...]) + mat(ug, up_w[...])).astype(low)


def mlp_grads_kernel(roles, *rest):
    hiddens, ggs, ugs, mids, dys, targets = (rest[i : i + 4] for i in range(0, 24, 4))
    rows = targets[0].shape[0] // 3
    here = Place()
    for role, target in zip(roles, targets):
        block = aligned(here.role(role), target.shape[1])
        for i, (lefts, rights) in enumerate(((ggs, mids), (ugs, mids), (hiddens, dys))):
            total = None
            for left, right in zip(lefts, rights):
                term = mat_left(left[...], right[:, block])
                total = term if total is None else total + term
            target[i * rows : (i + 1) * rows] = total[:rows].astype(low)


def split_kernel(axis, total_ref, arrived_ref, keep_ref, give_ref):
    core = Place().core
    size = total_ref.shape[axis] // 2
    for which, ref in ((core, keep_ref), (1 - core, give_ref)):
        at = (slice(None),) * axis + (aligned(which, size),)
        ref[...] = (total_ref[at].astype(full) + arrived_ref[at].astype(full)).astype(low)


def choose_kernel(keep_ref, help_ref, out_ref):
    here = Place()

    @pl.when(here.resident == 1)
    def _():
        out_ref[...] = keep_ref[...]

    @pl.when(here.resident == 0)
    def _():
        out_ref[...] = help_ref[...]


def middle_kernel(gain_ref, token_ref, sum_ref, arrived_ref, middle_ref, mid_ref):
    middle = token_ref[...].astype(full) + (sum_ref[...].astype(full) + arrived_ref[...].astype(full))
    middle_ref[...] = middle
    mid_ref[...] = rms_norm(middle, gain_ref[...].astype(full)).astype(low)


def stack_kernel(own, own_sib, pair, pair_sib, out):
    rows = own.shape[0]
    out[:rows] = (own[...].astype(full) + own_sib[...].astype(full)).astype(low)
    out[rows:] = (pair[...].astype(full) + pair_sib[...].astype(full)).astype(low)


def middle_grad_kernel(
    gain_ref, dy, dy_pair, middle, middle_pair, sum_ref, arrived_ref, grad_ref, low_ref, low_pair_ref
):
    rows = dy.shape[0]
    gain = gain_ref[...].astype(full)
    for n, (up, values) in enumerate(((dy, middle), (dy_pair, middle_pair))):
        here, there = pl.ds(n * rows, rows), pl.ds((1 - n) * rows, rows)
        grad = sum_ref[here].astype(full) + arrived_ref[there].astype(full)
        total = up[...].astype(full) + rms_pull(values[...], gain, grad)
        if n == 0:
            grad_ref[...] = total
        (low_pair_ref if n else low_ref)[...] = total.astype(low)


def add_kernel(*refs):
    terms, out = refs[:-1], refs[-1]
    total = terms[0][...].astype(full)
    for term in terms[1:]:
        total = total + term[...].astype(full)
    out[...] = total.astype(out.dtype)


def mlp_out_kernel(down_w, own, own_sib, pair, pair_sib, *outs):
    for ref, out in zip((own, own_sib, pair, pair_sib), outs):
        out[...] = mat(ref[...], down_w[...]).astype(out.dtype)


def output_kernel(middle_ref, mine_ref, sib_ref, pair_ref, out_ref, scratch, sem):
    rows = out_ref.shape[0]
    total = middle_ref[...] + mine_ref[...] + sib_ref[...].astype(full)
    total = total + pair_ref[WINDOW + rows :].astype(full)
    scratch[...] = total.astype(low)
    copy = pltpu.make_async_copy(scratch, out_ref, sem)
    copy.start()
    copy.wait()


def normed_sum_kernel(out_pair, out_pair_sib, mine_ref, sib_ref, own_ref, halo_ref, away_ref):
    rows = own_ref.shape[0]

    def total(top, size):
        return mine_ref[top : top + size] + sib_ref[top : top + size].astype(full)

    halo = total(0, WINDOW)
    halo_ref[...] = halo
    away_ref[:WINDOW] = halo.astype(low)
    own_ref[...] = total(WINDOW, rows)
    away_ref[WINDOW : WINDOW + rows] = total(WINDOW + rows, rows).astype(low)
    away_ref[WINDOW + rows :] = (out_pair[...].astype(full) + out_pair_sib[...].astype(full)).astype(low)


def halo_kernel(halo_ref, arrived_ref, out_ref):
    out_ref[...] = (halo_ref[...] + arrived_ref[:WINDOW].astype(full)).astype(low)


def input_grad_kernel(
    gain_ref, token_ref, middle_grad_ref, own_ref, arrived_ref, halo_ref, out_ref, scratch, sem
):
    rows = own_ref.shape[0]
    scratch[...] = own_ref[...] + arrived_ref[WINDOW : WINDOW + rows].astype(full)
    scratch[rows - WINDOW :] = scratch[rows - WINDOW :] + halo_ref[...].astype(full)
    pull = rms_pull(token_ref[...].astype(full), gain_ref[...].astype(full), scratch[...])
    scratch[...] = middle_grad_ref[...] + pull
    copy = pltpu.make_async_copy(scratch, out_ref, sem)
    copy.start()
    copy.wait()


def gains_kernel(attn_gain, mlp_gain, q_ref, k_ref, v_ref, g_ref, u_ref, *rest):
    mlp_pieces, attn_pieces, part = rest[:8], rest[8:16], rest[16]
    width, rows = q_ref.shape[1], g_ref.shape[0]
    here = Place()
    for n, piece in enumerate(attn_pieces):
        block = aligned(here.block(n), LANES)
        sums = None
        for i, weight in enumerate((q_ref, k_ref, v_ref)):
            term = piece[:, i * width : (i + 1) * width].astype(full) * weight[block].astype(full)
            sums = term if sums is None else sums + term
        sums = jnp.sum(sums, axis=1, keepdims=True)
        row = jnp.broadcast_to(sums, (LANES, LANES)).T[0:1]
        part[0:1, block] = row / attn_gain[:, block].astype(full)
    for n, piece in enumerate(mlp_pieces):
        block = aligned(here.block(n), LANES)
        sums = piece[0:rows].astype(full) * g_ref[:, block].astype(full)
        sums = sums + piece[rows : 2 * rows].astype(full) * u_ref[:, block].astype(full)
        part[1:2, block] = jnp.sum(sums, axis=0, keepdims=True) / mlp_gain[:, block].astype(full)


def finish_attention(*rest):
    pieces, (gq, gk, gv, go, gq_s, gk_s, gv_s, go_s, sems) = rest[:8], rest[8:]
    width = gq.shape[1]
    here = Place()
    for n, piece in enumerate(pieces):
        block = aligned(here.block(n), LANES)
        for i, ref in enumerate((gq_s, gk_s, gv_s)):
            ref[block] = piece[:, i * width : (i + 1) * width].astype(full)
        go_s[:, block] = piece[:, 3 * width :].astype(full).T
    copies = [
        pltpu.make_async_copy(src, dst, sems.at[n])
        for n, (src, dst) in enumerate(((gq_s, gq), (gk_s, gk), (gv_s, gv), (go_s, go)))
    ]
    for copy in copies:
        copy.start()
    for copy in copies:
        copy.wait()


def finish_mlp(*rest):
    pieces, (gg, gu, gd, gg_s, gu_s, gd_s, sems) = rest[:8], rest[8:]
    rows = gg.shape[0]
    here = Place()
    copies = []
    for i, (ref, out) in enumerate(((gg_s, gg), (gu_s, gu), (gd_s, gd))):
        for n, piece in enumerate(pieces):
            ref[:, aligned(here.block(n), LANES)] = piece[i * rows : (i + 1) * rows].astype(full)
        copies.append(pltpu.make_async_copy(ref, out, sems.at[i]))
        copies[-1].start()
    for copy in copies:
        copy.wait()


def build(n_dp, n_t):
    extra = [1 << k for k in range(3, n_dp.bit_length() - 1)]

    def perm(target):
        pairs = []
        for d in range(n_dp):
            for t in range(n_t):
                to = target(d, t)
                if to is not None:
                    pairs.append((d * n_t + t, to[0] * n_t + to[1]))
        return pairs

    def sender(target):
        return functools.partial(lax.ppermute, axis_name=AXES, perm=perm(target))

    send_core = sender(lambda d, t: (d ^ 1, t))
    send_pair = sender(lambda d, t: (d, t ^ 1))
    send_far = sender(lambda d, t: (d, t ^ 2))
    send_owner = sender(lambda d, t: (d, t ^ 2) if (d & 1) != (t >> 1) else None)
    send_help = send_core
    send_one = sender(lambda d, t: (d ^ (4 if d & 1 else 2), t))
    send_two = sender(lambda d, t: (d ^ (2 if d & 1 else 4), t))
    send_cross = [sender(lambda d, t, k=k: (d, t ^ k)) for k in (1, 2)]
    send_extra = [sender(lambda d, t, bit=bit: (d ^ bit, t)) for bit in extra]

    def local(
        tokens, gain_attn, w_query, w_key, w_value, w_out, gain_mlp, w_gate, w_up, w_down, out_grad
    ):
        own_rows, depth = tokens.shape
        hidden_cols = w_gate.shape[1]
        head_cols = w_query.shape[1]
        padded = -(-hidden_cols // 256) * 256
        ext = WINDOW + 2 * own_rows
        plans, made = {}, {}

        def value(item):
            return emit(item.name)[item.index] if isinstance(item, Later) else item

        def emit(name):
            if name not in made:
                function, args = plans[name]
                args = [value(arg) for arg in args]
                events = tuple(emit(event)[0] for event in ORDER.get(name, ()))
                if events:
                    args[-1] = after(args[-1], events)
                made[name] = function(*args)
            return made[name]

        def move(name, send, item):
            plans[name] = (lambda array: (send(array),)), [item]
            return Later(name, 0)

        def run(name, kernel, outs, args, **options):
            plans[name] = (
                lambda *arrays: tuple(call(kernel, outs, arrays, cost=COST.get(name, 0), **options))
            ), list(args)
            results = [Later(name, n) for n in range(len(outs))]
            return results if len(results) > 1 else results[0]

        def add(name, shape, *terms, dtype=low):
            return run(name, add_kernel, [(shape, dtype)], terms)

        chunk, wide_chunk = ((own_rows, depth), low), ((own_rows, depth), full)

        def three(name, piece):
            one = move(name + "1", send_one, piece)
            two = move(name + "2", send_two, piece)
            return [piece, one, two, move(name + "3", send_two, one)]

        def to_core(name, send, pieces):
            return [move(name + str(n), send, piece) for n, piece in enumerate(pieces)]

        def hold(array):
            return pltpu.with_memory_space_constraint(array, pltpu.HBM)

        gate_t, up_t = w_gate.T, w_up.T
        packed = call(
            pack_attention,
            [((3 * head_cols + w_out.shape[0], LANES), low)],
            tuple(hold(w) for w in (w_query, w_key, w_value, w_out)),
            scratch=[pltpu.SemaphoreType.DMA((7,))],
            anywhere=4,
        )[0]
        made["pack"] = (packed,)
        attn = move("za", send_far, packed)
        first_tokens = after(tokens, packed)
        token_pair = move("zt", send_pair, first_tokens)
        tail = first_tokens[own_rows - WINDOW :]
        halo = add(
            "h4",
            tail.shape,
            move("h2", sender(lambda d_, t_: (d_, 2) if t_ == 1 else None), tail),
            move("h3", sender(lambda d_, t_: (d_, 3) if t_ == 1 else None), tail),
        )
        token_sib = move("ct", send_core, first_tokens)
        wide_packed = call(
            pack_mlp,
            [((3 * hidden_cols, LANES), low)],
            (packed, hold(gate_t), hold(up_t), hold(w_down)),
            scratch=[pltpu.SemaphoreType.DMA((3,))],
            anywhere=4,
        )[0]
        made["packf"] = (wide_packed,)
        wide = move("zw", send_far, wide_packed)
        dy, dy_pair = out_grad, move("zy", send_pair, out_grad)
        mine = three("a", attn)
        pieces = mine + to_core("ca", send_help, mine)
        halo_sib = move("ch", send_core, halo)
        token_pair_sib = move("cp", send_core, token_pair)
        qkv_w, out_w = run(
            "unpacka",
            unpack_attention,
            [((depth, 3 * head_cols), low), (w_out.shape, low)],
            (w_query, w_key, w_value, w_out, *pieces),
        )

        normed, qkv, mixed, mine_own, mine_pair, sib_own, sib_pair = run(
            "attend",
            forward_kernel,
            [((2, ext, depth), low), ((2, ext, 3 * head_cols), low), ((2, 2 * own_rows, head_cols), low)]
            + [chunk] * 4,
            (gain_attn.reshape(1, depth), qkv_w, out_w, halo, tokens, token_pair,
             halo_sib, token_sib, token_pair_sib),
        )
        mlp_gain = gain_mlp.reshape(1, depth)
        sum_pair = add("sp", chunk[0], mine_pair, move("cqp", send_core, sib_pair))
        sum_own = add("so", chunk[0], mine_own, move("cqo", send_core, sib_own))
        arrived_own = move("zb0", send_pair, sum_pair)
        arrived_pair = move("zb1", send_pair, sum_own)
        wides = three("w", wide)
        dy_sib = move("cy", send_core, dy)
        dy_pair_sib = move("cyp", send_core, dy_pair)
        weights = to_core("cw", send_help, wides)
        middle_own, mid_own = run(
            "ko", middle_kernel, [wide_chunk, chunk], (mlp_gain, tokens, sum_own, arrived_own)
        )
        mid_own_sib = move("cmo", send_core, mid_own)
        gate_w, up_w, down_w = run(
            "unpackf",
            unpack_mlp,
            [((padded, depth), low)] * 3,
            (gate_t, up_t, w_down, *wides, *weights),
            scratch=[pltpu.SemaphoreType.DMA((24,))],
            anywhere=11,
        )

        def feed_forward(name, mid, dy):
            return run(
                name,
                mlp_kernel,
                [chunk] + [((own_rows, padded), low)] * 3,
                (gate_w, up_w, down_w, mid, dy),
            )

        part_sib, *tables_own_sib = feed_forward("fos", mid_own_sib, dy_sib)
        arrived_own_part = move("cfo", send_core, part_sib)
        part_own, *tables_own = feed_forward("fo", mid_own, dy)
        middle_pair, mid_pair = run(
            "kp", middle_kernel, [wide_chunk, chunk], (mlp_gain, token_pair, sum_pair, arrived_pair)
        )
        mid_pair_sib = move("cmp", send_core, mid_pair)
        part_sib, *tables_pair_sib = feed_forward("fps", mid_pair_sib, dy_pair_sib)
        arrived_pair_part = move("cfp", send_core, part_sib)
        part_pair, *tables_pair = feed_forward("fp", mid_pair, dy_pair)
        part_sum = run(
            "fs",
            stack_kernel,
            [((2 * own_rows, depth), low)],
            (part_own, arrived_own_part, part_pair, arrived_pair_part),
        )
        part_arrived = move("zm", send_pair, part_sum)

        tables = [tables_own, tables_own_sib, tables_pair, tables_pair_sib]
        grad_args = [table[i] for i in range(3) for table in tables]
        grad_args += [mid_own, mid_own_sib, mid_pair, mid_pair_sib, dy, dy_sib, dy_pair, dy_pair_sib]
        quarter = ((3 * hidden_cols, depth // 4), low)
        mlp_diag = run("g0", functools.partial(mlp_grads_kernel, (0,)), [quarter], grad_args)
        mlp_far = move("f1", send_one, mlp_diag)
        mlp_one, mlp_two, mlp_own = run(
            "g1", functools.partial(mlp_grads_kernel, (1, 2, 3)), [quarter] * 3, grad_args
        )
        mlp_near = move("f2", send_one, mlp_one)
        out_own, out_own_sib, out_pair, out_pair_sib = run(
            "mo",
            mlp_out_kernel,
            [wide_chunk, chunk, chunk, chunk],
            (down_w, *[table[0] for table in tables]),
        )
        out_own_arrived = move("coo", send_core, out_own_sib)
        out_pair_arrived = move("cop", send_core, out_pair_sib)

        middle_grad, branch_own, branch_pair = run(
            "mq",
            middle_grad_kernel,
            [wide_chunk, chunk, chunk],
            (mlp_gain, dy, dy_pair, middle_own, middle_pair, part_sum, part_arrived),
        )
        branch_pair_sib = move("cbp", send_core, branch_pair)
        branch_own_sib = move("cbo", send_core, branch_own)
        mlp_two = add("fs2", quarter[0], mlp_two, mlp_far)
        mlp_last = move("f3", send_two, mlp_two)

        bgs = (branch_own, branch_pair, branch_own_sib, branch_pair_sib)
        quarter = ((depth // 4, 4 * head_cols), low)
        qkv_grad, diag = run(
            "bwd",
            backward_kernel,
            [((2, ext, 3 * head_cols), low), quarter],
            (*bgs, out_w, mixed, qkv, normed),
            scratch=[pltpu.VMEM((2, 2 * own_rows, head_cols), low)],
        )
        far = move("b1", send_one, diag)
        one, two, last_own = run(
            "ag", attention_grads_kernel, [quarter] * 3, (*bgs, mixed, qkv_grad, normed)
        )
        near = move("b2", send_one, one)

        def everywhere(name, shape, total, dtype=low):
            for n, send in enumerate(send_extra):
                total = add(name + "a%d" % n, shape, total, move(name + "e%d" % n, send, total), dtype=dtype)
            return total

        mlp_shape = (3 * hidden_cols, depth // 4)
        mlp_total = everywhere("fx", mlp_shape, add("ft", mlp_shape, mlp_own, mlp_near, mlp_last))
        mlp_arrived = move("zf", send_owner, mlp_total)
        two = add("bs2", quarter[0], two, far)
        last = move("b3", send_two, two)
        grad_mine, grad_sib = run(
            "nk", normed_grad_kernel, [((ext, depth), full), ((ext, depth), low)], (qkv_w, qkv_grad)
        )
        grad_own, grad_halo, grad_away = run(
            "ns",
            normed_sum_kernel,
            [wide_chunk, ((WINDOW, depth), full), ((WINDOW + 2 * own_rows, depth), low)],
            (out_pair, out_pair_arrived, grad_mine, move("cn", send_core, grad_sib)),
        )
        grad_arrived = move("zn", send_pair, grad_away)
        output = run(
            "out",
            output_kernel,
            [chunk + (0,)],
            (middle_own, out_own, out_own_arrived, grad_arrived),
            scratch=[pltpu.VMEM(*chunk), pltpu.SemaphoreType.DMA],
        )
        total = everywhere("bx", quarter[0], add("bt", quarter[0], last_own, near, last))
        total_arrived = move("zg", send_owner, total)

        def to_both(name, shape, total, arrived, axis):
            shape = list(shape)
            shape[axis] //= 2
            half = (tuple(shape), low)
            keep, give = run(
                name + "s", functools.partial(split_kernel, axis), [half, half], (total, arrived)
            )
            return run(name + "c", choose_kernel, [half], (keep, move(name + "h", send_help, give)))

        mlp_mine = three("fa", to_both("fh", mlp_shape, mlp_total, mlp_arrived, 1))
        mine = three("ba", to_both("bh", quarter[0], total, total_arrived, 0))
        halo_sum = run("hk", halo_kernel, [((WINDOW, depth), low)], (grad_halo, grad_arrived))
        halo_grad = move("hh", sender(lambda d_, t_: (d_, 1) if t_ == 2 else None), halo_sum)
        input_grad = run(
            "ik",
            input_grad_kernel,
            [wide_chunk + (0,)],
            (gain_attn.reshape(1, depth), tokens, middle_grad, grad_own, grad_arrived, halo_grad),
            scratch=[pltpu.VMEM(*wide_chunk), pltpu.SemaphoreType.DMA],
        )
        mlp_pieces = mlp_mine + to_core("cfa", send_core, mlp_mine)
        shape = (hidden_cols, depth)
        pieces = mine + to_core("cba", send_core, mine)
        gain_shape = (2, depth)
        gains = run(
            "pg",
            gains_kernel,
            [(gain_shape, full)],
            (gain_attn.reshape(1, depth), mlp_gain, w_query, w_key, w_value, gate_t, up_t, *mlp_pieces, *pieces),
        )
        grad_gate, grad_up, grad_down = run(
            "finf",
            finish_mlp,
            [(shape, full, 0)] * 3,
            mlp_pieces,
            scratch=[pltpu.VMEM(shape, full)] * 3 + [pltpu.SemaphoreType.DMA((3,))],
        )
        grad_query, grad_key, grad_value, grad_out = run(
            "finb",
            finish_attention,
            [(w_query.shape, full, 0)] * 3 + [(w_out.shape, full, 0)],
            pieces,
            scratch=[pltpu.VMEM(w_query.shape, full)] * 3
            + [pltpu.VMEM(w_out.shape, full), pltpu.SemaphoreType.DMA((4,))],
        )
        for n, send in enumerate(send_cross):
            gains = add("g%s" % "ab"[n], gain_shape, gains, move("y%d" % n, send, gains), dtype=full)
        for name in plans:
            emit(name)
        gains = value(gains)
        return (
            value(output),
            value(input_grad),
            gains[0],
            value(grad_query),
            value(grad_key),
            value(grad_value),
            value(grad_out),
            gains[1],
            value(grad_gate).T,
            value(grad_up).T,
            value(grad_down),
        )

    return local


def solution(mesh):
    both = P(("dp", "tensor"), None)
    columns, rows = P(None, "tensor"), P("tensor", None)
    return jax.shard_map(
        build(mesh.shape["dp"], mesh.shape["tensor"]),
        mesh=mesh,
        in_specs=(both, P(), columns, columns, columns, rows, P(), columns, columns, rows, both),
        out_specs=(both, both, P(), columns, columns, columns, rows, P(), columns, columns, rows),
        check_vma=False,
    )
```
